32 devices in a mesh: tm: 16 (over z, y, x), space: 2 (over core).
Axes of the slice: x: 2, y: 2, z: 4, core: 2. Of those that a mesh axis runs over, the one named last changes fastest.
Arguments:
- source: float32 [64, 64, 512], P('tm', None, 'space'), may hold values from -3 to 3
- initial: float32 [64, 512], P(None, 'space'), may hold values from -6 to 6
- mass: float32 [64, 512], P(None, 'space'), may hold values from 0.8 to 1.25
- inverses: bfloat16 [3, 64, 64, 512], P(None, None, None, 'space'), may hold values from -0.3 to 1, as said below
- couplings: float32 [3, 6, 16, 16], replicated, may hold values from -0.375 to 0.375
- neighbours: int32 [6, 512], P(None, 'space'), may hold values from 0 to 288, as said below
- sends: int32 [2, 32], P(None, 'space'), may hold values from 0 to 255, as said below
Outputs:
- states: float32 [64, 64, 512], P('tm', None, 'space')
The draws below stay inside these ranges and needn't reach their ends.
Inputs may be any that keep to these rules, and one draw needn't show every extreme that they name: `neighbours`: each device's elements form a 16 x 4 x 4 block in its own order; an entry below 256 is a slot of the same device, 256 + j the j-th upper-face element of the device below, 272 + j the j-th lower-face element of the device above, 288 no neighbour. `sends`: row 0 lists the device's lower span-end elements, row 1 its upper ones, both in the same order of position on the face. `inverses`: each block is the identity scaled per node plus off-diagonal entries.
All inputs are finite; a program needn't handle non-finite values.
Results may differ from the reference program's by a relative error of at most 0.0003.
Values sent between devices are 32-bit elements; how exact they have to be, the bound alone decides.
A program may use at most 64 MiB of HBM per device.

```python
import math
import jax
import jax.numpy as jnp
from jax import lax

NODES = 64
TRACE = 16
LEVELS = 3
BX = 16
BY = 4
BZ = 4
E_DEV = 256
FACE = 16
ELEMS = 512
STEPS = 64
GROUPS = 4
N_TM = 16


def block_layout(key):
    blocks = ELEMS // E_DEV
    layout_keys = jax.random.split(jax.random.fold_in(key, 11), blocks)
    orders = jax.vmap(lambda one_key: jax.random.permutation(one_key, E_DEV))(layout_keys).astype(jnp.int32)
    placing = jnp.argsort(orders, axis=1).astype(jnp.int32)

    def one_block(order, place_of):
        cell = order
        along_x = cell % BX
        along_y = cell // BX % BY
        along_z = cell // (BX * BY)
        face_pos = along_y + BY * along_z
        blank = E_DEV + 2 * FACE

        def lookup(target):
            return place_of[jnp.clip(target, 0, E_DEV - 1)]
        face_lo_x = jnp.where(along_x > 0, lookup(cell - 1), E_DEV + face_pos)
        face_hi_x = jnp.where(along_x < BX - 1, lookup(cell + 1), E_DEV + FACE + face_pos)
        face_lo_y = jnp.where(along_y > 0, lookup(cell - BX), blank)
        face_hi_y = jnp.where(along_y < BY - 1, lookup(cell + BX), blank)
        face_lo_z = jnp.where(along_z > 0, lookup(cell - BX * BY), blank)
        face_hi_z = jnp.where(along_z < BZ - 1, lookup(cell + BX * BY), blank)
        linked = jnp.stack([face_lo_x, face_hi_x, face_lo_y, face_hi_y, face_lo_z, face_hi_z])
        face_ids = jnp.arange(FACE, dtype=jnp.int32)
        lower_list = place_of[BX * face_ids]
        upper_list = place_of[BX * face_ids + BX - 1]
        return (linked.astype(jnp.int32), jnp.stack([lower_list, upper_list]).astype(jnp.int32))
    linked_all, lists_all = jax.vmap(one_block)(orders, placing)
    return (linked_all, lists_all)


def draw_neighbours(key, part):
    linked_all, lists_all = block_layout(key)
    return jnp.transpose(linked_all, (1, 0, 2)).reshape(6, ELEMS)


def draw_sends(key, part):
    linked_all, lists_all = block_layout(key)
    return jnp.transpose(lists_all, (1, 0, 2)).reshape(2, FACE * (ELEMS // E_DEV))


def draw_inverses(key, part):
    key_diag, key_off = jax.random.split(jax.random.fold_in(key, 21), 2)
    diagonal = jax.random.uniform(key_diag, (LEVELS, NODES, ELEMS), jnp.float32, 0.5, 1.0)
    spread = jnp.clip(jax.random.normal(key_off, (LEVELS, NODES, NODES, ELEMS), jnp.float32), -6.0, 6.0) * (0.3 / 8.0)
    identity = jnp.eye(NODES, dtype=jnp.float32)[None, :, :, None]
    blocks = spread * (1.0 - identity) + identity * diagonal[:, :, None, :]
    return blocks.astype(jnp.bfloat16)


def level_of(own_key, extent, cuts, low, largest):
    loudness, own = 1.0, jax.random.fold_in(own_key, 6)
    for dim, parts in cuts:
        draws = jnp.exp(jax.random.uniform(jax.random.fold_in(own, dim), (parts,), jnp.float32, low / len(cuts), largest / len(cuts)))
        loudness = loudness * jnp.repeat(draws, extent[dim] // parts).reshape([-1 if axis == dim else 1 for axis in range(len(extent))])
    return loudness


def bell_draw(key, extent, width, bound, cuts=(), held_as=jnp.bfloat16):
    values = width * jax.random.normal(key, extent, jnp.float32)
    if cuts:
        values = values * level_of(key, extent, cuts, -0.22, 0.18)
    return jnp.clip(values, -bound, bound).astype(held_as)


def setup_inputs(seed: int = 0) -> dict:
    key_of = jax.random.split(jax.random.key(seed), 8)
    source = bell_draw(key_of[0], (STEPS, NODES, ELEMS), 0.5, 3.0, ((0, 16), (2, 2)), jnp.float32)
    initial = bell_draw(key_of[1], (NODES, ELEMS), 1.0, 6.0, ((1, 2),), jnp.float32)
    mass = jnp.clip(jnp.exp(math.log(1.25) - 0.4462871 * jax.random.uniform(key_of[2], (NODES, ELEMS), jnp.float32) ** level_of(key_of[2], (NODES, ELEMS), ((1, 2),), -0.2, 0.2)), 0.8, 1.25)
    inverses = draw_inverses(jax.random.fold_in(key_of[7], 71), 0)
    couplings = bell_draw(key_of[4], (LEVELS, 6, TRACE, TRACE), 0.06, 0.375, (), jnp.float32)
    neighbours = draw_neighbours(jax.random.fold_in(key_of[7], 71), 0)
    sends = draw_sends(jax.random.fold_in(key_of[7], 71), 0)
    return dict(source=source, initial=initial, mass=mass, inverses=inverses, couplings=couplings, neighbours=neighbours, sends=sends)


def trace_faces(state):
    elements = state.shape[-1]
    node_cube = state.reshape(state.shape[:-2] + (4, 4, 4, elements))
    face_sides = [node_cube[..., :, :, 0, :], node_cube[..., :, :, 3, :], node_cube[..., :, 0, :, :],
                  node_cube[..., :, 3, :, :], node_cube[..., 0, :, :, :], node_cube[..., 3, :, :, :]]
    return jnp.stack([one_side.reshape(state.shape[:-2] + (16, elements)) for one_side in face_sides], axis=-3)


def coupling_table(coupling):
    lifting = trace_faces(jnp.eye(64, dtype=coupling.dtype))
    return jnp.einsum("fkn,fkm->nfm", lifting, coupling, precision=lax.Precision.HIGHEST).reshape(64, 96)


def propagate(state, inverse, mass, table, neighbours, sends):
    batch = state.shape[0]
    blocks = ELEMS // E_DEV
    traces = trace_faces(state).reshape(batch, 6, 16, blocks, E_DEV)
    send_rows = sends.reshape(2, blocks, FACE)
    lower = jnp.take_along_axis(traces[:, 0], send_rows[0][None, None], axis=-1)
    upper = jnp.take_along_axis(traces[:, 1], send_rows[1][None, None], axis=-1)
    blank_block = jnp.zeros((batch, 16, 1, FACE), state.dtype)
    from_below = jnp.concatenate([blank_block, upper[:, :, :-1]], axis=2)
    from_above = jnp.concatenate([lower[:, :, 1:], blank_block], axis=2)
    blank_slot = jnp.zeros((batch, 16, blocks, 1), state.dtype)
    slots = neighbours.reshape(6, blocks, E_DEV)
    picked = []
    for face in range(6):
        extended = jnp.concatenate([traces[:, face ^ 1], from_below, from_above, blank_slot], axis=-1)
        picked.append(jnp.take_along_axis(extended, slots[face][None, None], axis=-1))
    stacked = jnp.stack(picked, axis=1).reshape(batch, 96, ELEMS)
    coupled = jnp.einsum("nk,bke->bne", table, stacked, precision=lax.Precision.HIGHEST)
    rhs_local = mass[None] * state - coupled
    return jnp.einsum("ije,bje->bie", inverse.astype(jnp.float32), rhs_local, precision=lax.Precision.HIGHEST)


def reference(source, initial, mass, inverses, couplings, neighbours, sends):
    tables = [coupling_table(couplings[level_index]) for level_index in range(3)]

    def advance_level(state, level_index):
        return propagate(state, inverses[level_index], mass, tables[level_index], neighbours, sends)

    sources = source.reshape(N_TM, 4, 64, ELEMS)
    device = jnp.arange(N_TM)[:, None, None]
    fine_state = jnp.zeros((N_TM, 64, ELEMS), jnp.float32)
    for offset in range(1, 4):
        fine_state = advance_level(fine_state, 0) + sources[:, offset]
    carried = advance_level(fine_state, 0)
    arrived = jnp.concatenate([jnp.zeros((1, 64, ELEMS), jnp.float32), carried[:-1]], axis=0)
    residual = jnp.where(device == 0, initial[None], sources[:, 0] + arrived)
    grouped = residual.reshape(GROUPS, 4, 64, ELEMS)
    level_one = grouped[:, 1]
    for offset in range(2, 4):
        level_one = advance_level(level_one, 1) + grouped[:, offset]
    carried_one = advance_level(level_one, 1)
    coarse_rhs = grouped[:, 0] + jnp.concatenate([jnp.zeros((1, 64, ELEMS), jnp.float32), carried_one[:-1]], axis=0)
    coarse_value = coarse_rhs[0:1]
    coarse_list = [coarse_value]
    for group_index in range(1, GROUPS):
        coarse_value = advance_level(coarse_value, 2) + coarse_rhs[group_index:group_index + 1]
        coarse_list.append(coarse_value)
    corrected = jnp.concatenate(coarse_list, axis=0)
    level_values = [corrected]
    for offset in range(1, 4):
        corrected = advance_level(corrected, 1) + grouped[:, offset]
        level_values.append(corrected)
    current = jnp.stack(level_values, axis=1).reshape(N_TM, 64, ELEMS)
    states = [current]
    for offset in range(1, 4):
        current = advance_level(current, 0) + sources[:, offset]
        states.append(current)
    return jnp.stack(states, axis=1).reshape(STEPS, 64, ELEMS)
```

```python
import functools
import jax
import jax.numpy as jnp
from jax import lax
from jax.experimental import pallas as pl
from jax.experimental.pallas import tpu as pltpu
from jax.sharding import PartitionSpec as P

MESH = pl.DeviceIdType.MESH
HI = lax.Precision.HIGHEST


def lane_take(block, index):
    return jnp.take_along_axis(block, index, axis=1, mode="promise_in_bounds")


def kernel(tm_size, space_size, source, initial, mass, inverses, couplings, neighbours, sends,
           out, packed, stage, inv, tables, edges, state, traces, halo, rhs, low, high, slots, picks, where_halo,
           next_source, r_all, w_in, s_all,
           inv_sem, halo_send, halo_recv, slot_send, slot_recv, src_send, src_recv,
           r_send, r_recv, s_send, s_recv):
    f32 = jnp.float32
    d = lax.axis_index("tm")
    k = lax.axis_index("space")
    j = lax.rem(d, 4)
    m = lax.div(d, 4)
    groups = tm_size // 4
    above = lax.rem(k + 1, space_size)
    below = lax.rem(k + space_size - 1, space_size)
    peers = [4 * m + lax.rem(j + step, 4) for step in (1, 2, 3)]

    loads = [pltpu.make_async_copy(inverses.at[l], packed.at[l], inv_sem.at[l]) for l in range(3)]
    loads[0].start()
    loads[1].start()
    loads[2].start()

    barrier = pltpu.get_barrier_semaphore()

    def greet(t, s):
        pl.semaphore_signal(barrier, inc=1, device_id=(t, s), device_id_type=MESH)

    greet(d, above)
    greet(d, below)
    for peer in peers:
        greet(peer, k)

    @pl.when(d > 0)
    def _():
        greet(d - 1, k)

    @pl.when(d < tm_size - 1)
    def _():
        greet(d + 1, k)

    for t in range(groups):
        @pl.when(m != t)
        def _(t=t):
            greet(4 * t + j, k)

    slots[0] = jnp.zeros((8, 128), jnp.int32)
    slots[0, 0:2, 0:16] = sends[...]

    n = lax.broadcasted_iota(jnp.int32, (64, 96), 0)
    col = lax.broadcasted_iota(jnp.int32, (64, 96), 1)
    a, b, c = n & 3, (n >> 2) & 3, n >> 4
    face, point = col >> 4, col & 15
    axis = face >> 1
    fixed = jnp.where(axis == 0, a, jnp.where(axis == 1, b, c))
    place = jnp.where(axis == 0, b + 4 * c, jnp.where(axis == 1, a + 4 * c, a + 4 * b))
    lift = ((fixed == 3 * (face & 1)) & (place == point)).astype(f32)
    spread = (lax.broadcasted_iota(jnp.int32, (16, 96), 0)
              == (lax.broadcasted_iota(jnp.int32, (16, 96), 1) & 15)).astype(f32)
    same = (lax.broadcasted_iota(jnp.int32, (96, 96), 0) >> 4
            == lax.broadcasted_iota(jnp.int32, (96, 96), 1) >> 4)

    def split(x):
        top = x.astype(jnp.bfloat16)
        return top, (x - top.astype(f32)).astype(jnp.bfloat16)

    def stacked(x):
        top, rest = split(x)
        return jnp.concatenate([jnp.concatenate([top, top], axis=1),
                                jnp.concatenate([rest, rest], axis=1)], axis=0)

    def times(table, x):
        both = jnp.dot(table, jnp.concatenate(split(x), axis=0), preferred_element_type=f32)
        half = both.shape[0] // 2
        return both[:half] + both[half:]

    for l in range(3):
        wide = jnp.dot(couplings[l], spread, precision=HI, preferred_element_type=f32)
        tables[l] = stacked(jnp.dot(lift, jnp.where(same, wide, 0.0), precision=HI,
                                    preferred_element_type=f32))
        edges[l] = stacked(jnp.where(same, wide, 0.0)[:32, :32])

    def prepare(level, begin, end):
        def block(part, carry):
            for i in range(8):
                whole = packed[level, 8 * part + i].astype(f32)
                for tile in (0, 1):
                    stage[tile, 72 * i:72 * i + 64, :] = whole[:, 128 * tile:128 * tile + 128]
            rows = pl.ds(pl.multiple_of(8 * part, 8), 8)
            for at in range(64):
                for tile in (0, 1):
                    inv[level, at, tile, rows, :] = stage[tile, pl.ds(at, 8, 72), :]
            return carry

        lax.fori_loop(begin, end, block, 0)

    nb = neighbours[...]
    picks[...] = jnp.where(nb < 256, nb, 512)

    loads[0].wait()
    prepare(0, 0, 3)

    pl.semaphore_wait(
        barrier,
        4 + groups + (d > 0).astype(jnp.int32) + (d < tm_size - 1).astype(jnp.int32))

    lists = [
        pltpu.make_async_remote_copy(slots.at[0], slots.at[1], slot_send.at[0], slot_recv.at[0],
                                     device_id=(d, above), device_id_type=MESH),
        pltpu.make_async_remote_copy(slots.at[0], slots.at[2], slot_send.at[1], slot_recv.at[1],
                                     device_id=(d, below), device_id_type=MESH)]
    for copy in lists:
        copy.start()

    back = jnp.maximum(d - 1, 0)
    forth = jnp.where(d > 0, d - 1, 1)
    ahead = pltpu.make_async_remote_copy(source.at[0], next_source, src_send, src_recv,
                                         device_id=(forth, k), device_id_type=MESH)

    @pl.when(d > 0)
    def _():
        ahead.start()

    @pl.when(d == tm_size - 1)
    def _():
        next_source[...] = jnp.zeros_like(next_source)

    prepare(0, 3, 8)
    loads[1].wait()
    loads[2].wait()
    for copy in lists:
        copy.wait()
    for row, (held, line, begin, exists) in enumerate(
            [(1, 1, 256, k > 0), (2, 0, 272, k < space_size - 1)]):
        for tile in (0, 1):
            lanes = pl.ds(128 * tile, 128)
            entry = jnp.broadcast_to(neighbours[row:row + 1, lanes], (8, 128)) - begin
            listed = jnp.broadcast_to(slots[held, line:line + 1, :], (8, 128))
            taken = lane_take(listed, jnp.clip(entry, 0, 15))
            limit = jnp.where(exists, 16, 0)
            valid = (entry >= 0) & (entry < limit)
            where_halo[row, :, lanes] = jnp.where(valid, taken, 512)

    def take_from(block, index_of):
        halves = []
        for tile in (0, 1):
            index = index_of(tile)
            spot = index & 127
            part = index >> 7
            halves.append(jnp.where(part == 0, lane_take(block[:, :128], spot),
                                    jnp.where(part == 1, lane_take(block[:, 128:], spot), 0.0)))
        return jnp.concatenate(halves, axis=1)

    def across(ref, begin, size, stride=None):
        return jnp.concatenate([ref[tile, pl.ds(begin, size, stride), :] for tile in (0, 1)], axis=1)

    def phi(level, slot, value, meanwhile=None):
        for tile in (0, 1):
            state[tile] = value[:, 128 * tile:128 * tile + 128]
        traces[slot, 0] = across(state, 0, 16, 4)
        traces[slot, 1] = across(state, 3, 16, 4)
        moves = [
            pltpu.make_async_remote_copy(traces.at[slot, 1], halo.at[slot, 0], halo_send.at[slot, 0],
                                         halo_recv.at[slot, 0], device_id=(d, above),
                                         device_id_type=MESH),
            pltpu.make_async_remote_copy(traces.at[slot, 0], halo.at[slot, 1], halo_send.at[slot, 1],
                                         halo_recv.at[slot, 1], device_id=(d, below),
                                         device_id_type=MESH)]
        for move in moves:
            move.start()
        faces = [
            traces[slot, 0], traces[slot, 1],
            jnp.concatenate([value[16 * q:16 * q + 4, :] for q in range(4)], axis=0),
            jnp.concatenate([value[16 * q + 12:16 * q + 16, :] for q in range(4)], axis=0),
            value[0:16, :], value[48:64, :]]
        picked = jnp.concatenate(
            [take_from(faces[f ^ 1], lambda tile, f=f: jnp.broadcast_to(
                picks[f:f + 1, 128 * tile:128 * tile + 128], (16, 128))) for f in range(6)], axis=0)
        coupled = times(tables[level], picked)
        known = mass[...] * value - coupled
        for tile in (0, 1):
            rhs[tile] = known[:, 128 * tile:128 * tile + 128]

        def early(q, total):
            for step in (1, 2):
                at = 4 * q + step
                total = total + inv[level, at] * rhs[:, pl.ds(at, 1), :]
            return total

        total = lax.fori_loop(0, 16, early, jnp.zeros((2, 64, 128), f32), unroll=True)
        if meanwhile is not None:
            prepare(*meanwhile)
        for move in moves:
            move.wait()
        got = jnp.concatenate(
            [take_from(halo[slot, row], lambda tile, row=row: jnp.concatenate(
                [where_halo[row, :, 128 * tile:128 * tile + 128]] * 2, axis=0))
             for row in (0, 1)], axis=0)
        change = times(edges[level], got)
        for row, kept, first in ((0, low, 0), (1, high, 3)):
            for tile in (0, 1):
                kept[tile] = (rhs[tile, pl.ds(first, 16, 4), :]
                              - change[16 * row:16 * row + 16, 128 * tile:128 * tile + 128])

        def late(q, total):
            total = total + inv[level, 4 * q] * low[:, pl.ds(q, 1), :]
            return total + inv[level, 4 * q + 3] * high[:, pl.ds(q, 1), :]

        total = lax.fori_loop(0, 16, late, total, unroll=True)
        return jnp.concatenate([total[0], total[1]], axis=1)

    value = source[1]
    value = phi(0, 0, value, (1, 0, 3)) + source[2]
    value = phi(0, 1, value, (1, 3, 6)) + source[3]
    value = phi(0, 0, value, (1, 6, 8))

    @pl.when(d < tm_size - 1)
    def _():
        ahead.wait_recv()

    @pl.when(d > 0)
    def _():
        ahead.wait_send()

    r_all[j] = value + next_source[...]
    shares = [pltpu.make_async_remote_copy(r_all.at[j], r_all.at[j], r_send.at[i], r_recv.at[j],
                                           device_id=(peer, k), device_id_type=MESH)
              for i, peer in enumerate(peers)]
    for share in shares:
        share.start()

    def share_arrived(i):
        @pl.when(j != i)
        def _():
            pltpu.make_async_remote_copy(r_all.at[i], r_all.at[i], r_send.at[0], r_recv.at[i],
                                         device_id=(peers[0], k), device_id_type=MESH).wait_recv()

    prepare(2, 0, 8)
    first = phi(2, 1, initial[...])
    share_arrived(0)
    value = phi(1, 0, r_all[0])
    share_arrived(1)
    value = phi(1, 1, value + r_all[1])
    share_arrived(2)
    value = phi(1, 0, value + r_all[2])
    share_arrived(3)
    s_all[m] = value + r_all[3] + jnp.where(m == 0, first, 0.0)

    onward = {t: pltpu.make_async_remote_copy(
        s_all.at[m], s_all.at[m], s_send.at[t], s_recv.at[m],
        device_id=(jnp.where(m < t, 4 * t + j, lax.rem(d + 4, tm_size)), k), device_id_type=MESH)
        for t in range(groups - 1, 0, -1)}
    for t, copy in onward.items():
        @pl.when(m < t)
        def _(copy=copy):
            copy.start()

    for share in shares:
        share.wait_send()

    def s_arrived(i):
        pltpu.make_async_remote_copy(s_all.at[i], s_all.at[i], s_send.at[0], s_recv.at[i],
                                     device_id=(lax.rem(d + 4, tm_size), k),
                                     device_id_type=MESH).wait_recv()

    @pl.when(m == 0)
    def _():
        w_in[...] = initial[...]

    @pl.when(m > 0)
    def _():
        s_arrived(0)
        w_in[...] = s_all[0]

    def coarse(i, carry):
        moved = phi(2, 2 + lax.rem(i, 2), w_in[...])
        s_arrived(i)
        w_in[...] = moved + s_all[i]
        return carry

    lax.fori_loop(1, m, coarse, 0)

    value = w_in[...]
    for i in (1, 2, 3):
        moved = phi(1, i % 2, value) + r_all[i - 1]
        value = jnp.where(j >= i, moved, value)
    out[0] = value
    for i in (1, 2, 3):
        value = phi(0, (i + 1) % 2, value) + source[i]
        out[i] = value

    for t, copy in onward.items():
        @pl.when(m < t)
        def _(copy=copy):
            copy.wait_send()


def pair_kernel(tm_size, source_in, initial_in, mass_in, inverses, couplings_in, neighbours_in, sends_in,
                out, source, initial, mass, couplings, neighbours, sends, in_sem, packed, inv, gout, ginv, tables, state, rhs, grhs, picks, listed, rows,
                start_out, start_in, gmass, next_source, r_all, rg_out, rg_all, first, w_in, wg_in,
                s_all, sg_out, sg_all, fresh_out, fresh_in,
                inv_sem, gi_send, gi_recv, st_send, st_recv, src_send, src_recv,
                r_send, r_recv, rg_send, rg_recv, s_send, s_recv, sg_send, sg_recv, fr_send, fr_recv):
    f32, bf16, i32 = jnp.float32, jnp.bfloat16, jnp.int32
    d = lax.axis_index("tm")
    k = lax.axis_index("space")
    j = lax.rem(d, 4)
    m = lax.div(d, 4)
    groups = tm_size // 4
    other = 1 - k
    upper = k == 0
    peers = [4 * m + lax.rem(j + step, 4) for step in (1, 2, 3)]

    loads = [pltpu.make_async_copy(inverses.at[l], packed.at[l], inv_sem.at[l]) for l in range(3)]
    fetches = [pltpu.make_async_copy(src, dst, in_sem.at[x]) for x, (src, dst) in enumerate([
        (neighbours_in, neighbours), (sends_in, sends), (source_in, source), (initial_in, initial),
        (mass_in, mass), (couplings_in, couplings)])]
    for copy in [*fetches[:2], loads[0], *fetches[2:], *loads[1:]]:
        copy.start()

    barrier = pltpu.get_barrier_semaphore()

    def greet(t, s):
        pl.semaphore_signal(barrier, inc=1, device_id=(t, s), device_id_type=MESH)

    greet(d, other)
    for peer in peers:
        greet(peer, k)
        greet(peer, other)

    @pl.when(d > 0)
    def _():
        greet(d - 1, k)

    @pl.when(d < tm_size - 1)
    def _():
        greet(d + 1, k)

    for t in range(groups):
        @pl.when(m != t)
        def _(t=t):
            greet(4 * t + j, k)
            greet(4 * t + j, other)

    r256 = lax.broadcasted_iota(i32, (256, 256), 0)
    c256 = lax.broadcasted_iota(i32, (256, 256), 1)
    swap = jnp.where((r256 >> 4 == (c256 & 15)) & ((r256 & 15) == c256 >> 4), 1.0, 0.0).astype(bf16)
    rows[...] = jnp.zeros((8, 128), i32)

    for fetch in fetches[:2]:
        fetch.wait()

    lane = lax.broadcasted_iota(i32, (8, 128), 1)
    place, layer = lane & 15, lane >> 4
    nb = neighbours[...]
    begin = jnp.where(upper, 272, 256)
    spot = nb - begin
    picks[:, 0:256] = jnp.where(nb < 256, nb, jnp.where((spot >= 0) & (spot < 16), 256 + spot, 512))
    rows[0:2, 0:16] = sends[...]

    def both(row):
        return [jnp.broadcast_to(nb[row:row + 1, 128 * t:128 * t + 128], (8, 128)) for t in (0, 1)]

    def chosen(a, b):
        return [jnp.where(upper, x, y) for x, y in zip(a, b)]

    def among(pair, index):
        at = index & 127
        return jnp.where(index < 128, lane_take(pair[0], at), lane_take(pair[1], at))

    facing = chosen(both(1), both(0))
    inward = chosen(both(0), both(1))
    ends = jnp.where(upper, jnp.broadcast_to(rows[1:2, :], (8, 128)), jnp.broadcast_to(rows[0:1, :], (8, 128)))
    edge = lane_take(ends, place)
    deeper = among(inward, edge)
    deepest = among(inward, jnp.minimum(deeper, 255))
    listed[...] = jnp.where(layer == 0, edge, jnp.where(layer == 1, deeper, jnp.where(layer == 2, deepest, 512)))
    twice = jnp.where((lane & 31) < 16, edge, deeper)

    def low_half(shape):
        return lax.broadcasted_iota(i32, shape, 1) < 64

    def boundary(x):
        index = jnp.concatenate([listed[...]] * 8, axis=0)
        at, part = index & 127, index >> 7
        g = jnp.where(part == 0, lane_take(x[:, :128], at), jnp.where(part == 1, lane_take(x[:, 128:], at), 0.0))
        return jnp.where(low_half((32, 128)), g[:32], pltpu.roll(g[32:], 64, 1))

    def opened(p):
        return jnp.concatenate([p, pltpu.roll(p, 64, 1)], axis=0)

    def split(x):
        top = x.astype(bf16)
        return top, (x - top.astype(f32)).astype(bf16)

    def times(table, x):
        pair = jnp.dot(table, jnp.concatenate(split(x), axis=0), preferred_element_type=f32)
        half = pair.shape[0] // 2
        return pair[:half] + pair[half:]

    def tile16(level, bi, bj):
        return jnp.concatenate(
            [packed[level, 16 * bi + i, 16 * bj:16 * bj + 16, :] for i in range(16)], axis=0)

    def prepare(level):
        for bi in range(4):
            for bj in range(4):
                turned = jnp.dot(swap, tile16(level, bi, bj), preferred_element_type=f32)
                for jj in range(16):
                    for tile in (0, 1):
                        inv[level, 16 * bj + jj, tile, 16 * bi:16 * bi + 16, :] = turned[
                            16 * jj:16 * jj + 16, 128 * tile:128 * tile + 128]

    element = lax.broadcasted_iota(i32, (256, 128), 0)
    quarter = lax.broadcasted_iota(i32, (256, 128), 1) >> 5
    hit = element == jnp.concatenate([twice] * 32, axis=0)
    spots = jnp.concatenate([jnp.where(hit & (quarter == q), 1.0, 0.0).astype(bf16) for q in range(4)], axis=0)

    def prepare_ghost(level):
        for bi in range(4):
            taken = jnp.dot(jnp.concatenate([tile16(level, bi, q) for q in range(4)], axis=1), spots,
                            preferred_element_type=f32)
            turned = jnp.dot(swap, taken.astype(bf16), preferred_element_type=f32)
            for jj in range(16):
                gout[level, bi, jj] = turned[16 * jj:16 * jj + 16, :]
            ghosts[level][bi].start()

    for fetch in fetches[2:5]:
        fetch.wait()
    for i in range(3):
        start_out[i] = boundary(source[i + 1])
    start_out[3] = boundary(initial[...])
    start_out[4] = boundary(mass[...])

    pl.semaphore_wait(
        barrier,
        7 + 2 * (groups - 1) + (d > 0).astype(i32) + (d < tm_size - 1).astype(i32))

    def beside_copy(src, dst, send, recv):
        return pltpu.make_async_remote_copy(src, dst, send, recv, device_id=(d, other), device_id_type=MESH)

    began = beside_copy(start_out, start_in, st_send, st_recv)
    began.start()
    ghosts = [[beside_copy(gout.at[l, x], ginv.at[l, x], gi_send.at[l, x], gi_recv.at[l, x])
               for x in range(4)] for l in range(3)]

    forth = jnp.where(d > 0, d - 1, 1)
    ahead = pltpu.make_async_remote_copy(source.at[0], next_source, src_send, src_recv,
                                         device_id=(forth, k), device_id_type=MESH)

    @pl.when(d > 0)
    def _():
        ahead.start()

    @pl.when(d == tm_size - 1)
    def _():
        next_source[...] = jnp.zeros_like(next_source)

    loads[0].wait()
    prepare_ghost(0)
    prepare(0)
    meets = among(facing, edge) - begin
    beside = jnp.zeros((8, 128), i32)
    for p in range(16):
        at = jnp.full((8, 128), p, i32)
        beside = jnp.where(place == lane_take(meets, at), lane_take(edge, at), beside)
    for f in range(2, 6):
        step = among(both(f), beside)
        onto = among(facing, jnp.minimum(step, 255)) - begin
        picks[f:f + 1, 256:384] = jnp.where((step < 256) & (layer < 3), 256 + 16 * layer + (onto & 15), 512)[0:1]
    toward = jnp.where(layer == 0, beside, jnp.where(layer < 3, 240 + lane, 512))
    away = jnp.where(layer < 2, 272 + lane, 512)
    picks[0:1, 256:384] = jnp.where(upper, toward, away)[0:1]
    picks[1:2, 256:384] = jnp.where(upper, away, toward)[0:1]

    fetches[5].wait()
    n = lax.broadcasted_iota(i32, (64, 96), 0)
    col = lax.broadcasted_iota(i32, (64, 96), 1)
    a, b, c = n & 3, (n >> 2) & 3, n >> 4
    face, point = col >> 4, col & 15
    axis = face >> 1
    fixed = jnp.where(axis == 0, a, jnp.where(axis == 1, b, c))
    where = jnp.where(axis == 0, b + 4 * c, jnp.where(axis == 1, a + 4 * c, a + 4 * b))
    lift = ((fixed == 3 * (face & 1)) & (where == point)).astype(f32).astype(bf16)
    spread = (lax.broadcasted_iota(i32, (16, 96), 0)
              == (lax.broadcasted_iota(i32, (16, 96), 1) & 15)).astype(f32).astype(bf16)
    same = (lax.broadcasted_iota(i32, (96, 96), 0) >> 4
            == lax.broadcasted_iota(i32, (96, 96), 1) >> 4)

    blocks = [x for l in range(3) for x in split(couplings[l])]
    wide = jnp.dot(jnp.concatenate(blocks, axis=0), spread, preferred_element_type=f32)
    wide = jnp.concatenate([jnp.where(same, wide[96 * x:96 * x + 96], 0.0) for x in range(6)], axis=1)
    lifted = jnp.dot(lift, wide.astype(bf16), preferred_element_type=f32).astype(bf16)
    for l in range(3):
        for x in (0, 1):
            half = lifted[:, 96 * (2 * l + x):96 * (2 * l + x) + 96]
            tables[l, 64 * x:64 * x + 64, :] = jnp.concatenate([half, half], axis=1)

    began.wait_recv()
    gmass[...] = opened(start_in[4])

    def across(begin, tiles):
        return jnp.concatenate([state[tile, pl.ds(begin, 16, 4), :] for tile in range(tiles)], axis=1)

    once = jnp.minimum(d + 1, 1)

    def phi(level, value, ghost, more, awaited=()):
        tiles = 3 if more else 2
        for tile in (0, 1):
            state[tile] = value[:, 128 * tile:128 * tile + 128]
        state[2] = ghost
        whole = jnp.concatenate([value, ghost], axis=1) if more else value
        faces = [
            across(0, 3), across(3, 3),
            jnp.concatenate([whole[16 * q:16 * q + 4, :] for q in range(4)], axis=0),
            jnp.concatenate([whole[16 * q + 12:16 * q + 16, :] for q in range(4)], axis=0),
            whole[0:16, :], whole[48:64, :]]

        def take_from(f):
            block = faces[f ^ 1]
            parts = []
            for tile in range(tiles):
                index = jnp.broadcast_to(picks[f:f + 1, 128 * tile:128 * tile + 128], (8, 128))
                at, part = index & 127, index >> 7
                at = jnp.concatenate([at, at], axis=0)
                part = jnp.concatenate([part, part], axis=0)
                found = jnp.zeros((16, 128), f32)
                for origin in ((0, 1, 2) if f < 2 else (0, 1) if tile < 2 else (2,)):
                    found = jnp.where(part == origin,
                                      lane_take(block[:, 128 * origin:128 * origin + 128], at), found)
                parts.append(found)
            return jnp.concatenate(parts, axis=1)

        picked = jnp.concatenate([take_from(f) for f in range(6)], axis=0)
        coupled = times(tables[level], picked)
        known = mass[...] * value - coupled[:, :256]
        for tile in (0, 1):
            rhs[tile] = known[:, 128 * tile:128 * tile + 128]
        if more:
            known = gmass[...] * ghost - coupled[:, 256:]
            which = lax.broadcasted_iota(i32, (16, 128), 1) >> 5
            dense = known[0:16]
            for q in (1, 2, 3):
                dense = jnp.where(which == q, pltpu.roll(known[16 * q:16 * q + 16], 32 * q, 1), dense)
            grhs[...] = dense

        def product(_, total):
            for at in range(64):
                total = total + inv[level, at] * rhs[:, pl.ds(at, 1), :]
            return total

        total = lax.fori_loop(0, once, product, jnp.zeros((2, 64, 128), f32))
        result = jnp.concatenate([total[0], total[1]], axis=1)
        if not more:
            return result, ghost
        for copy in awaited:
            copy.wait_recv()

        def ghost_product(_, total):
            for at in range(16):
                row = grhs[pl.ds(at, 1), :]
                total = total + ginv[level, :, at] * row[None]
            return total

        gsum = lax.fori_loop(0, once, ghost_product, jnp.zeros((4, 16, 128), f32)).reshape(64, 128)
        gsum = gsum + pltpu.roll(gsum, 64, 1)
        gsum = gsum + pltpu.roll(gsum, 32, 1)
        return result, gsum

    value, ghost = source[1], opened(start_in[0])
    for i in (2, 3):
        value, ghost = phi(0, value, ghost, True, ghosts[0] if i == 2 else ())
        value, ghost = value + source[i], ghost + opened(start_in[i - 1])
    value, _ = phi(0, value, ghost, False)

    @pl.when(d < tm_size - 1)
    def _():
        ahead.wait_recv()

    @pl.when(d > 0)
    def _():
        ahead.wait_send()

    value = value + next_source[...]
    r_all[j] = value
    rg_out[...] = boundary(value)
    shares = [pltpu.make_async_remote_copy(rg_out, rg_all.at[j], rg_send.at[i], rg_recv.at[j],
                                           device_id=(peer, other), device_id_type=MESH)
              for i, peer in enumerate([*peers, d])]
    shares += [pltpu.make_async_remote_copy(r_all.at[j], r_all.at[j], r_send.at[i], r_recv.at[j],
                                            device_id=(peer, k), device_id_type=MESH)
               for i, peer in enumerate(peers)]
    for share in shares:
        share.start()

    for l in (1, 2):
        loads[l].wait()
        prepare_ghost(l)
        prepare(l)
    first[...] = phi(2, initial[...], opened(start_in[3]), False)[0]

    def share_arrived(i):
        pltpu.make_async_remote_copy(rg_out, rg_all.at[i], rg_send.at[0], rg_recv.at[i],
                                     device_id=(d, other), device_id_type=MESH).wait_recv()

        @pl.when(j != i)
        def _():
            pltpu.make_async_remote_copy(r_all.at[i], r_all.at[i], r_send.at[0], r_recv.at[i],
                                         device_id=(peers[0], k), device_id_type=MESH).wait_recv()

    share_arrived(0)
    value, ghost = r_all[0], opened(rg_all[0])
    for i in (1, 2):
        value, ghost = phi(1, value, ghost, True, ghosts[1] if i == 1 else ())
        share_arrived(i)
        value, ghost = value + r_all[i], ghost + opened(rg_all[i])
    value, _ = phi(1, value, ghost, False)
    share_arrived(3)
    value = value + r_all[3] + jnp.where(m == 0, first[...], 0.0)
    s_all[m] = value
    sg_out[...] = boundary(value)

    onward = []
    for t in range(groups - 1, 0, -1):
        target = jnp.where(m < t, 4 * t + j, lax.rem(d + 4, tm_size))
        onward.append((t, pltpu.make_async_remote_copy(
            s_all.at[m], s_all.at[m], s_send.at[t], s_recv.at[m],
            device_id=(target, k), device_id_type=MESH)))
        onward.append((t, pltpu.make_async_remote_copy(
            sg_out, sg_all.at[m], sg_send.at[t], sg_recv.at[m],
            device_id=(target, other), device_id_type=MESH)))
    for t, copy in onward:
        @pl.when(m < t)
        def _(copy=copy):
            copy.start()

    for share in shares:
        share.wait_send()

    def s_arrived(i):
        pltpu.make_async_remote_copy(s_all.at[i], s_all.at[i], s_send.at[0], s_recv.at[i],
                                     device_id=(lax.rem(d + 4, tm_size), k),
                                     device_id_type=MESH).wait_recv()
        pltpu.make_async_remote_copy(sg_out, sg_all.at[i], sg_send.at[0], sg_recv.at[i],
                                     device_id=(lax.rem(d + 4, tm_size), other),
                                     device_id_type=MESH).wait_recv()

    for copy in ghosts[2]:
        copy.wait_recv()

    @pl.when(m == 0)
    def _():
        w_in[...] = initial[...]

    @pl.when(m > 0)
    def _():
        s_arrived(0)
        w_in[...] = s_all[0]
        wg_in[...] = opened(sg_all[0])

    def refresh(slot, value):
        fresh_out[slot] = boundary(value)
        copy = beside_copy(fresh_out.at[slot], fresh_in.at[slot], fr_send.at[slot], fr_recv.at[slot])
        copy.start()
        copy.wait()
        return opened(fresh_in[slot])

    for i in range(1, groups - 1):
        @pl.when(i < m)
        def _(i=i):
            value = w_in[...]
            ghost = refresh(1 + i, value) if i > 1 and i % 3 == 1 else wg_in[...]
            value, ghost = phi(2, value, ghost, True)
            s_arrived(i)
            w_in[...] = value + s_all[i]
            wg_in[...] = ghost + opened(sg_all[i])

    value = w_in[...]
    ghost = refresh(0, value)
    for i in (1, 2, 3):
        moved, gmoved = phi(1, value, ghost, i < 3)
        value = jnp.where(j >= i, moved + r_all[i - 1], value)
        if i < 3:
            ghost = jnp.where(j >= i, gmoved + opened(rg_all[i - 1]), ghost)
    out[0] = value
    ghost = refresh(1, value)
    for i in (1, 2, 3):
        value, ghost = phi(0, value, ghost, i < 3)
        value = value + source[i]
        if i < 3:
            ghost = ghost + opened(start_in[i - 1])
        out[i] = value

    for t, copy in onward:
        @pl.when(m < t)
        def _(copy=copy):
            copy.wait_send()
    began.wait_send()
    for level in ghosts:
        for copy in level:
            copy.wait_send()


def pair_local(tm_size, source, initial, mass, inverses, couplings, neighbours, sends):
    f32, bf16, i32 = jnp.float32, jnp.bfloat16, jnp.int32
    vmem = pl.BlockSpec(memory_space=pltpu.VMEM)
    dma = pltpu.SemaphoreType.DMA
    groups = tm_size // 4
    return pl.pallas_call(
        functools.partial(pair_kernel, tm_size),
        out_shape=jax.ShapeDtypeStruct(source.shape, f32),
        in_specs=[pl.BlockSpec(memory_space=pltpu.MemorySpace.HBM)] * 7,
        out_specs=vmem,
        scratch_shapes=[
            pltpu.VMEM(source.shape, f32),
            pltpu.VMEM(initial.shape, f32),
            pltpu.VMEM(mass.shape, f32),
            pltpu.VMEM((3, 96, 16), f32),
            pltpu.VMEM(neighbours.shape, i32),
            pltpu.VMEM(sends.shape, i32),
            dma((6,)),
            pltpu.VMEM(inverses.shape, bf16),
            pltpu.VMEM((3, 64, 2, 64, 128), f32),
            pltpu.VMEM((3, 4, 16, 16, 128), f32),
            pltpu.VMEM((3, 4, 16, 16, 128), f32),
            pltpu.VMEM((3, 128, 192), bf16),
            pltpu.VMEM((3, 64, 128), f32),
            pltpu.VMEM((2, 64, 128), f32),
            pltpu.VMEM((16, 128), f32),
            pltpu.VMEM((6, 384), i32),
            pltpu.VMEM((8, 128), i32),
            pltpu.VMEM((8, 128), i32),
            pltpu.VMEM((5, 32, 128), f32),
            pltpu.VMEM((5, 32, 128), f32),
            pltpu.VMEM((64, 128), f32),
            pltpu.VMEM((64, 256), f32),
            pltpu.VMEM((4, 64, 256), f32),
            pltpu.VMEM((32, 128), f32),
            pltpu.VMEM((4, 32, 128), f32),
            pltpu.VMEM((64, 256), f32),
            pltpu.VMEM((64, 256), f32),
            pltpu.VMEM((64, 128), f32),
            pltpu.VMEM((groups, 64, 256), f32),
            pltpu.VMEM((32, 128), f32),
            pltpu.VMEM((groups, 32, 128), f32),
            pltpu.VMEM((max(2, groups), 32, 128), f32),
            pltpu.VMEM((max(2, groups), 32, 128), f32),
            dma((3,)), dma((3, 4)), dma((3, 4)), dma, dma, dma, dma,
            dma((3,)), dma((4,)), dma((4,)), dma((4,)),
            dma((groups,)), dma((groups,)), dma((groups,)), dma((groups,)),
            dma((max(2, groups),)), dma((max(2, groups),)),
        ],
        compiler_params=pltpu.CompilerParams(collective_id=0, has_side_effects=True,
                                             vmem_limit_bytes=48 << 20),
        name="cycle",
    )(*[pltpu.with_memory_space_constraint(x, pltpu.MemorySpace.HBM) for x in (source, initial, mass, inverses, couplings.reshape(3, 96, 16), neighbours, sends)])


def local(tm_size, space_size, source, initial, mass, inverses, couplings, neighbours, sends):
    f32 = jnp.float32
    vmem = pl.BlockSpec(memory_space=pltpu.VMEM)
    dma = pltpu.SemaphoreType.DMA
    return pl.pallas_call(
        functools.partial(kernel, tm_size, space_size),
        out_shape=jax.ShapeDtypeStruct(source.shape, f32),
        in_specs=[vmem, vmem, vmem, pl.BlockSpec(memory_space=pl.ANY), vmem, vmem, vmem],
        out_specs=vmem,
        scratch_shapes=[
            pltpu.VMEM(inverses.shape, jnp.bfloat16),
            pltpu.VMEM((2, 576, 128), f32),
            pltpu.VMEM((3, 64, 2, 64, 128), f32),
            pltpu.VMEM((3, 128, 192), jnp.bfloat16),
            pltpu.VMEM((3, 64, 64), jnp.bfloat16),
            pltpu.VMEM((2, 64, 128), f32),
            pltpu.VMEM((4, 2, 16, 256), f32),
            pltpu.VMEM((4, 2, 16, 256), f32),
            pltpu.VMEM((2, 64, 128), f32),
            pltpu.VMEM((2, 16, 128), f32),
            pltpu.VMEM((2, 16, 128), f32),
            pltpu.VMEM((3, 8, 128), jnp.int32),
            pltpu.VMEM((6, 256), jnp.int32),
            pltpu.VMEM((2, 8, 256), jnp.int32),
            pltpu.VMEM((64, 256), f32),
            pltpu.VMEM((4, 64, 256), f32),
            pltpu.VMEM((64, 256), f32),
            pltpu.VMEM((tm_size // 4, 64, 256), f32),
            dma((3,)), dma((4, 2)), dma((4, 2)), dma((2,)), dma((2,)), dma, dma,
            dma((3,)), dma((4,)), dma((tm_size // 4,)), dma((tm_size // 4,)),
        ],
        compiler_params=pltpu.CompilerParams(collective_id=0, has_side_effects=True),
        name="cycle",
    )(source, initial, mass, inverses, couplings.reshape(3, 96, 16), neighbours, sends)


def solution(mesh):
    placed = (
        P("tm", None, "space"),
        P(None, "space"),
        P(None, "space"),
        P(None, None, None, "space"),
        P(),
        P(None, "space"),
        P(None, "space"),
    )
    body = (functools.partial(pair_local, mesh.shape["tm"]) if mesh.shape["space"] == 2
            else functools.partial(local, mesh.shape["tm"], mesh.shape["space"]))
    return jax.shard_map(
        body,
        mesh=mesh, in_specs=placed, out_specs=P("tm", None, "space"), check_vma=False)
```

```python
import functools
import jax
import jax.numpy as jnp
from jax import lax
from jax.experimental import pallas as pl
from jax.experimental.pallas import tpu as pltpu
from jax.sharding import PartitionSpec as P

MESH = pl.DeviceIdType.MESH
HI = lax.Precision.HIGHEST


def lane_take(block, index):
    return jnp.take_along_axis(block, index, axis=1, mode="promise_in_bounds")


def kernel(tm_size, space_size, source, initial, mass, inverses, couplings, neighbours, sends,
           out, packed, stage, inv, tables, edges, state, traces, halo, rhs, low, high, slots, picks, where_halo,
           next_source, r_all, w_in, s_all,
           inv_sem, halo_send, halo_recv, slot_send, slot_recv, src_send, src_recv,
           r_send, r_recv, s_send, s_recv):
    f32 = jnp.float32
    d = lax.axis_index("tm")
    k = lax.axis_index("space")
    j = lax.rem(d, 4)
    m = lax.div(d, 4)
    groups = tm_size // 4
    above = lax.rem(k + 1, space_size)
    below = lax.rem(k + space_size - 1, space_size)
    peers = [4 * m + lax.rem(j + step, 4) for step in (1, 2, 3)]

    loads = [pltpu.make_async_copy(inverses.at[l], packed.at[l], inv_sem.at[l]) for l in range(3)]
    loads[0].start()
    loads[1].start()
    loads[2].start()

    barrier = pltpu.get_barrier_semaphore()

    def greet(t, s):
        pl.semaphore_signal(barrier, inc=1, device_id=(t, s), device_id_type=MESH)

    greet(d, above)
    greet(d, below)
    for peer in peers:
        greet(peer, k)

    @pl.when(d > 0)
    def _():
        greet(d - 1, k)

    @pl.when(d < tm_size - 1)
    def _():
        greet(d + 1, k)

    for t in range(groups):
        @pl.when(m != t)
        def _(t=t):
            greet(4 * t + j, k)

    slots[0] = jnp.zeros((8, 128), jnp.int32)
    slots[0, 0:2, 0:16] = sends[...]

    n = lax.broadcasted_iota(jnp.int32, (64, 96), 0)
    col = lax.broadcasted_iota(jnp.int32, (64, 96), 1)
    a, b, c = n & 3, (n >> 2) & 3, n >> 4
    face, point = col >> 4, col & 15
    axis = face >> 1
    fixed = jnp.where(axis == 0, a, jnp.where(axis == 1, b, c))
    place = jnp.where(axis == 0, b + 4 * c, jnp.where(axis == 1, a + 4 * c, a + 4 * b))
    lift = ((fixed == 3 * (face & 1)) & (place == point)).astype(f32)
    spread = (lax.broadcasted_iota(jnp.int32, (16, 96), 0)
              == (lax.broadcasted_iota(jnp.int32, (16, 96), 1) & 15)).astype(f32)
    same = (lax.broadcasted_iota(jnp.int32, (96, 96), 0) >> 4
            == lax.broadcasted_iota(jnp.int32, (96, 96), 1) >> 4)

    def split(x):
        top = x.astype(jnp.bfloat16)
        return top, (x - top.astype(f32)).astype(jnp.bfloat16)

    def stacked(x):
        top, rest = split(x)
        return jnp.concatenate([jnp.concatenate([top, top], axis=1),
                                jnp.concatenate([rest, rest], axis=1)], axis=0)

    def times(table, x):
        both = jnp.dot(table, jnp.concatenate(split(x), axis=0), preferred_element_type=f32)
        half = both.shape[0] // 2
        return both[:half] + both[half:]

    for l in range(3):
        wide = jnp.dot(couplings[l], spread, precision=HI, preferred_element_type=f32)
        tables[l] = stacked(jnp.dot(lift, jnp.where(same, wide, 0.0), precision=HI,
                                    preferred_element_type=f32))
        edges[l] = stacked(jnp.where(same, wide, 0.0)[:32, :32])

    def prepare(level, begin, end):
        def block(part, carry):
            for i in range(8):
                whole = packed[level, 8 * part + i].astype(f32)
                for tile in (0, 1):
                    stage[tile, 72 * i:72 * i + 64, :] = whole[:, 128 * tile:128 * tile + 128]
            rows = pl.ds(pl.multiple_of(8 * part, 8), 8)
            for at in range(64):
                for tile in (0, 1):
                    inv[level, at, tile, rows, :] = stage[tile, pl.ds(at, 8, 72), :]
            return carry

        lax.fori_loop(begin, end, block, 0)

    nb = neighbours[...]
    picks[...] = jnp.where(nb < 256, nb, 512)

    loads[0].wait()
    prepare(0, 0, 3)

    pl.semaphore_wait(
        barrier,
        4 + groups + (d > 0).astype(jnp.int32) + (d < tm_size - 1).astype(jnp.int32))

    lists = [
        pltpu.make_async_remote_copy(slots.at[0], slots.at[1], slot_send.at[0], slot_recv.at[0],
                                     device_id=(d, above), device_id_type=MESH),
        pltpu.make_async_remote_copy(slots.at[0], slots.at[2], slot_send.at[1], slot_recv.at[1],
                                     device_id=(d, below), device_id_type=MESH)]
    for copy in lists:
        copy.start()

    back = jnp.maximum(d - 1, 0)
    forth = jnp.where(d > 0, d - 1, 1)
    ahead = pltpu.make_async_remote_copy(source.at[0], next_source, src_send, src_recv,
                                         device_id=(forth, k), device_id_type=MESH)

    @pl.when(d > 0)
    def _():
        ahead.start()

    @pl.when(d == tm_size - 1)
    def _():
        next_source[...] = jnp.zeros_like(next_source)

    prepare(0, 3, 8)
    loads[1].wait()
    loads[2].wait()
    for copy in lists:
        copy.wait()
    for row, (held, line, begin, exists) in enumerate(
            [(1, 1, 256, k > 0), (2, 0, 272, k < space_size - 1)]):
        for tile in (0, 1):
            lanes = pl.ds(128 * tile, 128)
            entry = jnp.broadcast_to(neighbours[row:row + 1, lanes], (8, 128)) - begin
            listed = jnp.broadcast_to(slots[held, line:line + 1, :], (8, 128))
            taken = lane_take(listed, jnp.clip(entry, 0, 15))
            limit = jnp.where(exists, 16, 0)
            valid = (entry >= 0) & (entry < limit)
            where_halo[row, :, lanes] = jnp.where(valid, taken, 512)

    def take_from(block, index_of):
        halves = []
        for tile in (0, 1):
            index = index_of(tile)
            spot = index & 127
            part = index >> 7
            halves.append(jnp.where(part == 0, lane_take(block[:, :128], spot),
                                    jnp.where(part == 1, lane_take(block[:, 128:], spot), 0.0)))
        return jnp.concatenate(halves, axis=1)

    def across(ref, begin, size, stride=None):
        return jnp.concatenate([ref[tile, pl.ds(begin, size, stride), :] for tile in (0, 1)], axis=1)

    def phi(level, slot, value, meanwhile=None):
        for tile in (0, 1):
            state[tile] = value[:, 128 * tile:128 * tile + 128]
        traces[slot, 0] = across(state, 0, 16, 4)
        traces[slot, 1] = across(state, 3, 16, 4)
        moves = [
            pltpu.make_async_remote_copy(traces.at[slot, 1], halo.at[slot, 0], halo_send.at[slot, 0],
                                         halo_recv.at[slot, 0], device_id=(d, above),
                                         device_id_type=MESH),
            pltpu.make_async_remote_copy(traces.at[slot, 0], halo.at[slot, 1], halo_send.at[slot, 1],
                                         halo_recv.at[slot, 1], device_id=(d, below),
                                         device_id_type=MESH)]
        for move in moves:
            move.start()
        faces = [
            traces[slot, 0], traces[slot, 1],
            jnp.concatenate([value[16 * q:16 * q + 4, :] for q in range(4)], axis=0),
            jnp.concatenate([value[16 * q + 12:16 * q + 16, :] for q in range(4)], axis=0),
            value[0:16, :], value[48:64, :]]
        picked = jnp.concatenate(
            [take_from(faces[f ^ 1], lambda tile, f=f: jnp.broadcast_to(
                picks[f:f + 1, 128 * tile:128 * tile + 128], (16, 128))) for f in range(6)], axis=0)
        coupled = times(tables[level], picked)
        known = mass[...] * value - coupled
        for tile in (0, 1):
            rhs[tile] = known[:, 128 * tile:128 * tile + 128]

        def early(q, total):
            for step in (1, 2):
                at = 4 * q + step
                total = total + inv[level, at] * rhs[:, pl.ds(at, 1), :]
            return total

        total = lax.fori_loop(0, 16, early, jnp.zeros((2, 64, 128), f32), unroll=True)
        if meanwhile is not None:
            prepare(*meanwhile)
        for move in moves:
            move.wait()
        got = jnp.concatenate(
            [take_from(halo[slot, row], lambda tile, row=row: jnp.concatenate(
                [where_halo[row, :, 128 * tile:128 * tile + 128]] * 2, axis=0))
             for row in (0, 1)], axis=0)
        change = times(edges[level], got)
        for row, kept, first in ((0, low, 0), (1, high, 3)):
            for tile in (0, 1):
                kept[tile] = (rhs[tile, pl.ds(first, 16, 4), :]
                              - change[16 * row:16 * row + 16, 128 * tile:128 * tile + 128])

        def late(q, total):
            total = total + inv[level, 4 * q] * low[:, pl.ds(q, 1), :]
            return total + inv[level, 4 * q + 3] * high[:, pl.ds(q, 1), :]

        total = lax.fori_loop(0, 16, late, total, unroll=True)
        return jnp.concatenate([total[0], total[1]], axis=1)

    value = source[1]
    value = phi(0, 0, value, (1, 0, 3)) + source[2]
    value = phi(0, 1, value, (1, 3, 6)) + source[3]
    value = phi(0, 0, value, (1, 6, 8))

    @pl.when(d < tm_size - 1)
    def _():
        ahead.wait_recv()

    @pl.when(d > 0)
    def _():
        ahead.wait_send()

    r_all[j] = value + next_source[...]
    shares = [pltpu.make_async_remote_copy(r_all.at[j], r_all.at[j], r_send.at[i], r_recv.at[j],
                                           device_id=(peer, k), device_id_type=MESH)
              for i, peer in enumerate(peers)]
    for share in shares:
        share.start()

    def share_arrived(i):
        @pl.when(j != i)
        def _():
            pltpu.make_async_remote_copy(r_all.at[i], r_all.at[i], r_send.at[0], r_recv.at[i],
                                         device_id=(peers[0], k), device_id_type=MESH).wait_recv()

    prepare(2, 0, 8)
    first = phi(2, 1, initial[...])
    share_arrived(0)
    value = phi(1, 0, r_all[0])
    share_arrived(1)
    value = phi(1, 1, value + r_all[1])
    share_arrived(2)
    value = phi(1, 0, value + r_all[2])
    share_arrived(3)
    s_all[m] = value + r_all[3] + jnp.where(m == 0, first, 0.0)

    onward = {t: pltpu.make_async_remote_copy(
        s_all.at[m], s_all.at[m], s_send.at[t], s_recv.at[m],
        device_id=(jnp.where(m < t, 4 * t + j, lax.rem(d + 4, tm_size)), k), device_id_type=MESH)
        for t in range(groups - 1, 0, -1)}
    for t, copy in onward.items():
        @pl.when(m < t)
        def _(copy=copy):
            copy.start()

    for share in shares:
        share.wait_send()

    def s_arrived(i):
        pltpu.make_async_remote_copy(s_all.at[i], s_all.at[i], s_send.at[0], s_recv.at[i],
                                     device_id=(lax.rem(d + 4, tm_size), k),
                                     device_id_type=MESH).wait_recv()

    @pl.when(m == 0)
    def _():
        w_in[...] = initial[...]

    @pl.when(m > 0)
    def _():
        s_arrived(0)
        w_in[...] = s_all[0]

    def coarse(i, carry):
        moved = phi(2, 2 + lax.rem(i, 2), w_in[...])
        s_arrived(i)
        w_in[...] = moved + s_all[i]
        return carry

    lax.fori_loop(1, m, coarse, 0)

    value = w_in[...]
    for i in (1, 2, 3):
        moved = phi(1, i % 2, value) + r_all[i - 1]
        value = jnp.where(j >= i, moved, value)
    out[0] = value
    for i in (1, 2, 3):
        value = phi(0, (i + 1) % 2, value) + source[i]
        out[i] = value

    for t, copy in onward.items():
        @pl.when(m < t)
        def _(copy=copy):
            copy.wait_send()


def pair_kernel(tm_size, source_in, initial_in, mass_in, inverses, couplings_in, neighbours_in, sends_in,
                out, source, initial, mass, couplings, neighbours, sends, in_sem, packed, inv, gout, ginv, tables, state, rhs, change, grhs, picks, listed, rows,
                start_out, start_in, gmass, next_source, r_all, rg_out, rg_all, first, w_in, wg_in,
                s_all, sg_out, sg_all, fresh_out, fresh_in,
                inv_sem, gi_send, gi_recv, st_send, st_recv, src_send, src_recv,
                r_send, r_recv, rg_send, rg_recv, s_send, s_recv, sg_send, sg_recv, fr_send, fr_recv):
    f32, bf16, i32 = jnp.float32, jnp.bfloat16, jnp.int32
    d = lax.axis_index("tm")
    k = lax.axis_index("space")
    j = lax.rem(d, 4)
    m = lax.div(d, 4)
    groups = tm_size // 4
    other = 1 - k
    upper = k == 0
    peers = [4 * m + j + 1 - 2 * lax.rem(j, 2), 4 * m + lax.rem(j + 2, 4), 4 * m + 3 - j]

    loads = [pltpu.make_async_copy(inverses.at[l], packed.at[l], inv_sem.at[l]) for l in range(3)]
    fetches = [pltpu.make_async_copy(src, dst, in_sem.at[x]) for x, (src, dst) in enumerate([
        (neighbours_in, neighbours), (sends_in, sends), (source_in, source), (initial_in, initial),
        (mass_in, mass), (couplings_in, couplings)])]
    for copy in [*fetches[:2], loads[0], *fetches[2:], *loads[1:]]:
        copy.start()

    barrier = pltpu.get_barrier_semaphore()

    def greet(t, s):
        pl.semaphore_signal(barrier, inc=1, device_id=(t, s), device_id_type=MESH)

    greet(d, other)
    for peer in peers:
        greet(peer, k)
        greet(peer, other)

    @pl.when(d > 0)
    def _():
        greet(d - 1, k)

    @pl.when(d < tm_size - 1)
    def _():
        greet(d + 1, k)

    for t in range(groups):
        @pl.when(m != t)
        def _(t=t):
            greet(4 * t + j, k)
            greet(4 * t + j, other)

    r256 = lax.broadcasted_iota(i32, (256, 256), 0)
    c256 = lax.broadcasted_iota(i32, (256, 256), 1)
    swap = jnp.where((r256 >> 4 == (c256 & 15)) & ((r256 & 15) == c256 >> 4), 1.0, 0.0).astype(bf16)
    rows[...] = jnp.zeros((8, 128), i32)

    for fetch in fetches[:2]:
        fetch.wait()

    lane = lax.broadcasted_iota(i32, (8, 128), 1)
    place, layer = lane & 15, lane >> 4
    nb = neighbours[...]
    begin = jnp.where(upper, 272, 256)
    spot = nb - begin
    picks[:, 0:256] = jnp.where(nb < 256, nb, jnp.where((spot >= 0) & (spot < 16), 256 + spot, 512))
    rows[0:2, 0:16] = sends[...]

    def both(row):
        return [jnp.broadcast_to(nb[row:row + 1, 128 * t:128 * t + 128], (8, 128)) for t in (0, 1)]

    def chosen(a, b):
        return [jnp.where(upper, x, y) for x, y in zip(a, b)]

    def among(pair, index):
        at = index & 127
        return jnp.where(index < 128, lane_take(pair[0], at), lane_take(pair[1], at))

    facing = chosen(both(1), both(0))
    inward = chosen(both(0), both(1))
    ends = jnp.where(upper, jnp.broadcast_to(rows[1:2, :], (8, 128)), jnp.broadcast_to(rows[0:1, :], (8, 128)))
    edge = lane_take(ends, place)
    deeper = among(inward, edge)
    deepest = among(inward, jnp.minimum(deeper, 255))
    listed[...] = jnp.where(layer == 0, edge, jnp.where(layer == 1, deeper, jnp.where(layer == 2, deepest, 512)))
    twice = jnp.where((lane & 31) < 16, edge, deeper)

    def low_half(shape):
        return lax.broadcasted_iota(i32, shape, 1) < 64

    def boundary(x):
        index = jnp.concatenate([listed[...]] * 8, axis=0)
        at, part = index & 127, index >> 7
        g = jnp.where(part == 0, lane_take(x[:, :128], at), jnp.where(part == 1, lane_take(x[:, 128:], at), 0.0))
        return jnp.where(low_half((32, 128)), g[:32], pltpu.roll(g[32:], 64, 1))

    def opened(p):
        return jnp.concatenate([p, pltpu.roll(p, 64, 1)], axis=0)

    def split(x):
        top = x.astype(bf16)
        return top, (x - top.astype(f32)).astype(bf16)

    def times(table, x):
        pair = jnp.dot(table, jnp.concatenate(split(x), axis=0), preferred_element_type=f32)
        half = pair.shape[0] // 2
        return pair[:half] + pair[half:]

    def tile16(level, bi, bj):
        return jnp.concatenate(
            [packed[level, 16 * bi + i, 16 * bj:16 * bj + 16, :] for i in range(16)], axis=0)

    element = lax.broadcasted_iota(i32, (256, 128), 0)
    quarter = lax.broadcasted_iota(i32, (256, 128), 1) >> 5
    hit = element == jnp.concatenate([twice] * 32, axis=0)
    spots = jnp.concatenate([jnp.where(hit & (quarter == q), 1.0, 0.0).astype(bf16) for q in range(4)], axis=0)

    def prepare(level):
        for pair in (0, 2):
            taken = jnp.concatenate([
                jnp.dot(jnp.concatenate([tile16(level, bi, bj) for bj in range(4)], axis=1), spots,
                        preferred_element_type=f32).astype(bf16) for bi in (pair, pair + 1)], axis=1)
            turned = jnp.dot(swap, taken, preferred_element_type=f32)
            for jj in range(16):
                for x in (0, 1):
                    gout[level, pair + x, jj] = turned[16 * jj:16 * jj + 16, 128 * x:128 * x + 128]
        for x in range(4):
            ghosts[level][x].start()
        for bi in range(4):
            for bj in range(4):
                turned = jnp.dot(swap, tile16(level, bi, bj), preferred_element_type=f32)
                for jj in range(16):
                    for tile in (0, 1):
                        inv[level, 16 * bj + jj, tile, 16 * bi:16 * bi + 16, :] = turned[
                            16 * jj:16 * jj + 16, 128 * tile:128 * tile + 128]

    for fetch in fetches[2:]:
        fetch.wait()
    for i in range(3):
        start_out[i] = boundary(source[i + 1])
    start_out[3] = boundary(initial[...])
    start_out[4] = boundary(mass[...])

    pl.semaphore_wait(
        barrier,
        7 + 2 * (groups - 1) + (d > 0).astype(i32) + (d < tm_size - 1).astype(i32))

    def beside_copy(src, dst, send, recv):
        return pltpu.make_async_remote_copy(src, dst, send, recv, device_id=(d, other), device_id_type=MESH)

    began = beside_copy(start_out, start_in, st_send, st_recv)
    began.start()
    ghosts = [[beside_copy(gout.at[l, x], ginv.at[l, x], gi_send.at[l, x], gi_recv.at[l, x])
               for x in range(4)] for l in range(3)]

    forth = jnp.where(d > 0, d - 1, 1)
    ahead = pltpu.make_async_remote_copy(source.at[0], next_source, src_send, src_recv,
                                         device_id=(forth, k), device_id_type=MESH)

    @pl.when(d > 0)
    def _():
        ahead.start()

    @pl.when(d == tm_size - 1)
    def _():
        next_source[...] = jnp.zeros_like(next_source)

    loads[0].wait()
    prepare(0)
    meets = among(facing, edge) - begin
    beside = jnp.zeros((8, 128), i32)
    for p in range(16):
        at = jnp.full((8, 128), p, i32)
        beside = jnp.where(place == lane_take(meets, at), lane_take(edge, at), beside)
    for f in range(2, 6):
        step = among(both(f), beside)
        onto = among(facing, jnp.minimum(step, 255)) - begin
        picks[f:f + 1, 256:384] = jnp.where((step < 256) & (layer < 3), 256 + 16 * layer + (onto & 15), 512)[0:1]
    toward = jnp.where(layer == 0, beside, jnp.where(layer < 3, 240 + lane, 512))
    away = jnp.where(layer < 2, 272 + lane, 512)
    picks[0:1, 256:384] = jnp.where(upper, toward, away)[0:1]
    picks[1:2, 256:384] = jnp.where(upper, away, toward)[0:1]

    n = lax.broadcasted_iota(i32, (64, 96), 0)
    col = lax.broadcasted_iota(i32, (64, 96), 1)
    a, b, c = n & 3, (n >> 2) & 3, n >> 4
    face, point = col >> 4, col & 15
    axis = face >> 1
    fixed = jnp.where(axis == 0, a, jnp.where(axis == 1, b, c))
    where = jnp.where(axis == 0, b + 4 * c, jnp.where(axis == 1, a + 4 * c, a + 4 * b))
    lift = ((fixed == 3 * (face & 1)) & (where == point)).astype(f32).astype(bf16)
    spread = (lax.broadcasted_iota(i32, (16, 96), 0)
              == (lax.broadcasted_iota(i32, (16, 96), 1) & 15)).astype(f32).astype(bf16)
    same = (lax.broadcasted_iota(i32, (96, 96), 0) >> 4
            == lax.broadcasted_iota(i32, (96, 96), 1) >> 4)

    blocks = [x for l in range(3) for x in split(couplings[l])]
    wide = jnp.dot(jnp.concatenate(blocks, axis=0), spread, preferred_element_type=f32)
    wide = jnp.concatenate([jnp.where(same, wide[96 * x:96 * x + 96], 0.0) for x in range(6)], axis=1)
    lifted = jnp.dot(lift, wide.astype(bf16), preferred_element_type=f32).astype(bf16)
    for l in range(3):
        for x in (0, 1):
            half = lifted[:, 96 * (2 * l + x):96 * (2 * l + x) + 96]
            tables[l, 64 * x:64 * x + 64, :] = jnp.concatenate([half, half], axis=1)

    began.wait_recv()
    gmass[...] = opened(start_in[4])

    def across(begin, tiles):
        return jnp.concatenate([state[tile, pl.ds(begin, 16, 4), :] for tile in range(tiles)], axis=1)

    once = jnp.minimum(d + 1, 1)

    def sides(x):
        return [jnp.concatenate([x[16 * q:16 * q + 4, :] for q in range(4)], axis=0),
                jnp.concatenate([x[16 * q + 12:16 * q + 16, :] for q in range(4)], axis=0),
                x[0:16, :], x[48:64, :]]

    def gather(block, f, tile, origins):
        index = jnp.broadcast_to(picks[f:f + 1, 128 * tile:128 * tile + 128], (8, 128))
        at, part = index & 127, index >> 7
        at = jnp.concatenate([at, at], axis=0)
        part = jnp.concatenate([part, part], axis=0)
        found = jnp.zeros((16, 128), f32)
        for origin in origins:
            found = jnp.where(part == origin, lane_take(block(origin), at), found)
        return found

    def columns(block):
        return lambda origin: block[:, 128 * origin:128 * origin + 128]

    def product_of(level, total):
        def product(_, total):
            for at in range(64):
                total = total + inv[level, at] * rhs[:, pl.ds(at, 1), :]
            return total
        return lax.fori_loop(0, once, product, total)

    def ghost_rhs(ghost, coupled):
        known = gmass[...] * ghost - coupled
        which = lax.broadcasted_iota(i32, (16, 128), 1) >> 5
        dense = known[0:16]
        for q in (1, 2, 3):
            dense = jnp.where(which == q, pltpu.roll(known[16 * q:16 * q + 16], 32 * q, 1), dense)
        grhs[...] = dense

    def ghost_step(level):
        def ghost_product(_, total):
            for at in range(16):
                total = total + ginv[level, :, at] * grhs[pl.ds(at, 1), :][None]
            return total

        gsum = lax.fori_loop(0, once, ghost_product, jnp.zeros((4, 16, 128), f32)).reshape(64, 128)
        gsum = gsum + pltpu.roll(gsum, 64, 1)
        return gsum + pltpu.roll(gsum, 32, 1)

    def keep(x, tiles):
        for tile in tiles:
            state[tile] = x[:, 128 * (tile - tiles[0]):128 * (tile - tiles[0]) + 128]

    def phi(level, value, ghost, more, awaited=()):
        tiles = 3 if more else 2
        keep(value, (0, 1))
        state[2] = ghost
        whole = jnp.concatenate([value, ghost], axis=1) if more else value
        faces = [across(0, 3), across(3, 3), *sides(whole)]
        picked = jnp.concatenate([jnp.concatenate([
            gather(columns(faces[f ^ 1]), f, tile, (0, 1, 2) if f < 2 else (0, 1) if tile < 2 else (2,))
            for tile in range(tiles)], axis=1) for f in range(6)], axis=0)
        coupled = times(tables[level], picked)
        known = mass[...] * value - coupled[:, :256]
        for tile in (0, 1):
            rhs[tile] = known[:, 128 * tile:128 * tile + 128]
        if more:
            ghost_rhs(ghost, coupled[:, 256:])
        total = product_of(level, jnp.zeros((2, 64, 128), f32))
        result = jnp.concatenate([total[0], total[1]], axis=1)
        if not more:
            return result, ghost
        for copy in awaited:
            copy.wait_recv()
        return result, ghost_step(level)

    def phi_fresh(level, value, slot):
        fresh_out[slot] = boundary(value)
        copy = beside_copy(fresh_out.at[slot], fresh_in.at[slot], fr_send.at[slot], fr_recv.at[slot])
        copy.start()
        keep(value, (0, 1))
        faces = [across(0, 2), across(3, 2), *sides(value)]
        picked = jnp.concatenate([jnp.concatenate([
            gather(columns(faces[f ^ 1]), f, tile, (0, 1)) for tile in (0, 1)], axis=1)
            for f in range(6)], axis=0)
        known = mass[...] * value - times(tables[level], picked)
        for tile in (0, 1):
            rhs[tile] = known[:, 128 * tile:128 * tile + 128]
        total = product_of(level, jnp.zeros((2, 64, 128), f32))
        copy.wait()
        ghost = opened(fresh_in[slot])
        state[2] = ghost
        ends = [state[2, pl.ds(0, 16, 4), :], state[2, pl.ds(3, 16, 4), :]]
        near = [across(0, 2), across(3, 2)]
        beyond = sides(ghost)
        nothing = jnp.zeros((16, 256), f32)
        rows_of = []
        for f in range(6):
            if f < 2:
                def source_of(origin, f=f):
                    return ends[f ^ 1] if origin == 2 else columns(near[f ^ 1])(origin)
                rows_of.append(jnp.concatenate(
                    [gather(source_of, f, 0, (2,)), gather(source_of, f, 1, (2,)),
                     gather(source_of, f, 2, (0, 1, 2))], axis=1))
            else:
                rows_of.append(jnp.concatenate(
                    [nothing, gather(lambda _, f=f: beyond[(f ^ 1) - 2], f, 2, (2,))], axis=1))
        coupled = times(tables[level], jnp.concatenate(rows_of, axis=0))
        ghost_rhs(ghost, coupled[:, 256:])
        for tile in (0, 1):
            state[tile] = coupled[:, 128 * tile:128 * tile + 128]
            change[tile] = jnp.where(upper, state[tile, pl.ds(3, 16, 4), :], state[tile, pl.ds(0, 16, 4), :])
        offset = 3 - 3 * k

        def corrected(_, total):
            for q in range(16):
                total = total - inv[level, 4 * q + offset] * change[:, pl.ds(q, 1), :]
            return total

        total = lax.fori_loop(0, once, corrected, total)
        return jnp.concatenate([total[0], total[1]], axis=1), ghost_step(level), ghost

    value, ghost = source[1], opened(start_in[0])
    for i in (2, 3):
        value, ghost = phi(0, value, ghost, True, ghosts[0] if i == 2 else ())
        value, ghost = value + source[i], ghost + opened(start_in[i - 1])
    value, _ = phi(0, value, ghost, False)

    @pl.when(d < tm_size - 1)
    def _():
        ahead.wait_recv()

    @pl.when(d > 0)
    def _():
        ahead.wait_send()

    value = value + next_source[...]
    r_all[j] = value
    rg_out[...] = boundary(value)
    shares = [pltpu.make_async_remote_copy(rg_out, rg_all.at[j], rg_send.at[i], rg_recv.at[j],
                                           device_id=(peer, other), device_id_type=MESH)
              for i, peer in enumerate([*peers, d])]
    shares += [pltpu.make_async_remote_copy(r_all.at[j], r_all.at[j], r_send.at[i], r_recv.at[j],
                                            device_id=(peer, k), device_id_type=MESH)
               for i, peer in enumerate(peers)]
    for share in shares:
        share.start()

    for l in (1, 2):
        loads[l].wait()
        prepare(l)
    first[...] = phi(2, initial[...], opened(start_in[3]), False)[0]

    def share_arrived(i):
        pltpu.make_async_remote_copy(rg_out, rg_all.at[i], rg_send.at[0], rg_recv.at[i],
                                     device_id=(d, other), device_id_type=MESH).wait_recv()

        @pl.when(j != i)
        def _():
            pltpu.make_async_remote_copy(r_all.at[i], r_all.at[i], r_send.at[0], r_recv.at[i],
                                         device_id=(peers[0], k), device_id_type=MESH).wait_recv()

    share_arrived(0)
    value, ghost = r_all[0], opened(rg_all[0])
    for i in (1, 2):
        value, ghost = phi(1, value, ghost, True, ghosts[1] if i == 1 else ())
        share_arrived(i)
        value, ghost = value + r_all[i], ghost + opened(rg_all[i])
    value, _ = phi(1, value, ghost, False)
    share_arrived(3)
    value = value + r_all[3] + jnp.where(m == 0, first[...], 0.0)
    s_all[m] = value
    sg_out[...] = boundary(value)

    onward = []
    for t in range(groups - 1, 0, -1):
        target = jnp.where(m < t, 4 * t + j, lax.rem(d + 4, tm_size))
        onward.append((t, pltpu.make_async_remote_copy(
            s_all.at[m], s_all.at[m], s_send.at[t], s_recv.at[m],
            device_id=(target, k), device_id_type=MESH)))
        onward.append((t, pltpu.make_async_remote_copy(
            sg_out, sg_all.at[m], sg_send.at[t], sg_recv.at[m],
            device_id=(target, other), device_id_type=MESH)))
    for t, copy in onward:
        @pl.when(m < t)
        def _(copy=copy):
            copy.start()

    for share in shares:
        share.wait_send()

    def s_arrived(i):
        pltpu.make_async_remote_copy(s_all.at[i], s_all.at[i], s_send.at[0], s_recv.at[i],
                                     device_id=(lax.rem(d + 4, tm_size), k),
                                     device_id_type=MESH).wait_recv()
        pltpu.make_async_remote_copy(sg_out, sg_all.at[i], sg_send.at[0], sg_recv.at[i],
                                     device_id=(lax.rem(d + 4, tm_size), other),
                                     device_id_type=MESH).wait_recv()

    for copy in ghosts[2]:
        copy.wait_recv()

    @pl.when(m == 0)
    def _():
        w_in[...] = initial[...]

    @pl.when(m > 0)
    def _():
        s_arrived(0)
        w_in[...] = s_all[0]
        wg_in[...] = opened(sg_all[0])

    for i in range(1, groups - 1):
        @pl.when(i < m)
        def _(i=i):
            if i > 1 and i % 3 == 1:
                value, ghost, _ = phi_fresh(2, w_in[...], 1 + i)
            else:
                value, ghost = phi(2, w_in[...], wg_in[...], True)
            s_arrived(i)
            w_in[...] = value + s_all[i]
            wg_in[...] = ghost + opened(sg_all[i])

    value = w_in[...]
    for i in (1, 2, 3):
        if i == 1:
            moved, gmoved, ghost = phi_fresh(1, value, 0)
        else:
            moved, gmoved = phi(1, value, ghost, i < 3)
        value = jnp.where(j >= i, moved + r_all[i - 1], value)
        if i < 3:
            ghost = jnp.where(j >= i, gmoved + opened(rg_all[i - 1]), ghost)
    out[0] = value
    for i in (1, 2, 3):
        if i == 1:
            value, ghost, _ = phi_fresh(0, value, 1)
        else:
            value, ghost = phi(0, value, ghost, i < 3)
        value = value + source[i]
        if i < 3:
            ghost = ghost + opened(start_in[i - 1])
        out[i] = value

    for t, copy in onward:
        @pl.when(m < t)
        def _(copy=copy):
            copy.wait_send()
    began.wait_send()
    for level in ghosts:
        for copy in level:
            copy.wait_send()


def pair_local(tm_size, source, initial, mass, inverses, couplings, neighbours, sends):
    f32, bf16, i32 = jnp.float32, jnp.bfloat16, jnp.int32
    vmem = pl.BlockSpec(memory_space=pltpu.VMEM)
    dma = pltpu.SemaphoreType.DMA
    groups = tm_size // 4
    return pl.pallas_call(
        functools.partial(pair_kernel, tm_size),
        out_shape=jax.ShapeDtypeStruct(source.shape, f32),
        in_specs=[pl.BlockSpec(memory_space=pltpu.MemorySpace.HBM)] * 7,
        out_specs=vmem,
        scratch_shapes=[
            pltpu.VMEM(source.shape, f32),
            pltpu.VMEM(initial.shape, f32),
            pltpu.VMEM(mass.shape, f32),
            pltpu.VMEM((3, 96, 16), f32),
            pltpu.VMEM(neighbours.shape, i32),
            pltpu.VMEM(sends.shape, i32),
            dma((6,)),
            pltpu.VMEM(inverses.shape, bf16),
            pltpu.VMEM((3, 64, 2, 64, 128), f32),
            pltpu.VMEM((3, 4, 16, 16, 128), f32),
            pltpu.VMEM((3, 4, 16, 16, 128), f32),
            pltpu.VMEM((3, 128, 192), bf16),
            pltpu.VMEM((3, 64, 128), f32),
            pltpu.VMEM((2, 64, 128), f32),
            pltpu.VMEM((2, 16, 128), f32),
            pltpu.VMEM((16, 128), f32),
            pltpu.VMEM((6, 384), i32),
            pltpu.VMEM((8, 128), i32),
            pltpu.VMEM((8, 128), i32),
            pltpu.VMEM((5, 32, 128), f32),
            pltpu.VMEM((5, 32, 128), f32),
            pltpu.VMEM((64, 128), f32),
            pltpu.VMEM((64, 256), f32),
            pltpu.VMEM((4, 64, 256), f32),
            pltpu.VMEM((32, 128), f32),
            pltpu.VMEM((4, 32, 128), f32),
            pltpu.VMEM((64, 256), f32),
            pltpu.VMEM((64, 256), f32),
            pltpu.VMEM((64, 128), f32),
            pltpu.VMEM((groups, 64, 256), f32),
            pltpu.VMEM((32, 128), f32),
            pltpu.VMEM((groups, 32, 128), f32),
            pltpu.VMEM((max(2, groups), 32, 128), f32),
            pltpu.VMEM((max(2, groups), 32, 128), f32),
            dma((3,)), dma((3, 4)), dma((3, 4)), dma, dma, dma, dma,
            dma((3,)), dma((4,)), dma((4,)), dma((4,)),
            dma((groups,)), dma((groups,)), dma((groups,)), dma((groups,)),
            dma((max(2, groups),)), dma((max(2, groups),)),
        ],
        compiler_params=pltpu.CompilerParams(collective_id=0, has_side_effects=True,
                                             vmem_limit_bytes=48 << 20),
        name="cycle",
    )(*[pltpu.with_memory_space_constraint(x, pltpu.MemorySpace.HBM) for x in (source, initial, mass, inverses, couplings.reshape(3, 96, 16), neighbours, sends)])


def local(tm_size, space_size, source, initial, mass, inverses, couplings, neighbours, sends):
    f32 = jnp.float32
    vmem = pl.BlockSpec(memory_space=pltpu.VMEM)
    dma = pltpu.SemaphoreType.DMA
    return pl.pallas_call(
        functools.partial(kernel, tm_size, space_size),
        out_shape=jax.ShapeDtypeStruct(source.shape, f32),
        in_specs=[vmem, vmem, vmem, pl.BlockSpec(memory_space=pl.ANY), vmem, vmem, vmem],
        out_specs=vmem,
        scratch_shapes=[
            pltpu.VMEM(inverses.shape, jnp.bfloat16),
            pltpu.VMEM((2, 576, 128), f32),
            pltpu.VMEM((3, 64, 2, 64, 128), f32),
            pltpu.VMEM((3, 128, 192), jnp.bfloat16),
            pltpu.VMEM((3, 64, 64), jnp.bfloat16),
            pltpu.VMEM((2, 64, 128), f32),
            pltpu.VMEM((4, 2, 16, 256), f32),
            pltpu.VMEM((4, 2, 16, 256), f32),
            pltpu.VMEM((2, 64, 128), f32),
            pltpu.VMEM((2, 16, 128), f32),
            pltpu.VMEM((2, 16, 128), f32),
            pltpu.VMEM((3, 8, 128), jnp.int32),
            pltpu.VMEM((6, 256), jnp.int32),
            pltpu.VMEM((2, 8, 256), jnp.int32),
            pltpu.VMEM((64, 256), f32),
            pltpu.VMEM((4, 64, 256), f32),
            pltpu.VMEM((64, 256), f32),
            pltpu.VMEM((tm_size // 4, 64, 256), f32),
            dma((3,)), dma((4, 2)), dma((4, 2)), dma((2,)), dma((2,)), dma, dma,
            dma((3,)), dma((4,)), dma((tm_size // 4,)), dma((tm_size // 4,)),
        ],
        compiler_params=pltpu.CompilerParams(collective_id=0, has_side_effects=True),
        name="cycle",
    )(source, initial, mass, inverses, couplings.reshape(3, 96, 16), neighbours, sends)


def solution(mesh):
    placed = (
        P("tm", None, "space"),
        P(None, "space"),
        P(None, "space"),
        P(None, None, None, "space"),
        P(),
        P(None, "space"),
        P(None, "space"),
    )
    body = (functools.partial(pair_local, mesh.shape["tm"]) if mesh.shape["space"] == 2
            else functools.partial(local, mesh.shape["tm"], mesh.shape["space"]))
    return jax.shard_map(
        body,
        mesh=mesh, in_specs=placed, out_specs=P("tm", None, "space"), check_vma=False)
```

```python
import functools
import jax
import jax.numpy as jnp
from jax import lax
from jax.experimental import pallas as pl
from jax.experimental.pallas import tpu as pltpu
from jax.sharding import PartitionSpec as P

MESH = pl.DeviceIdType.MESH
HI = lax.Precision.HIGHEST


def lane_take(block, index):
    return jnp.take_along_axis(block, index, axis=1, mode="promise_in_bounds")


def kernel(tm_size, space_size, source, initial, mass, inverses, couplings, neighbours, sends,
           out, packed, stage, inv, tables, edges, state, traces, halo, rhs, low, high, slots, picks, where_halo,
           next_source, r_all, w_in, s_all,
           inv_sem, halo_send, halo_recv, slot_send, slot_recv, src_send, src_recv,
           r_send, r_recv, s_send, s_recv):
    f32 = jnp.float32
    d = lax.axis_index("tm")
    k = lax.axis_index("space")
    j = lax.rem(d, 4)
    m = lax.div(d, 4)
    groups = tm_size // 4
    above = lax.rem(k + 1, space_size)
    below = lax.rem(k + space_size - 1, space_size)
    peers = [4 * m + lax.rem(j + step, 4) for step in (1, 2, 3)]

    loads = [pltpu.make_async_copy(inverses.at[l], packed.at[l], inv_sem.at[l]) for l in range(3)]
    loads[0].start()
    loads[1].start()
    loads[2].start()

    barrier = pltpu.get_barrier_semaphore()

    def greet(t, s):
        pl.semaphore_signal(barrier, inc=1, device_id=(t, s), device_id_type=MESH)

    greet(d, above)
    greet(d, below)
    for peer in peers:
        greet(peer, k)

    @pl.when(d > 0)
    def _():
        greet(d - 1, k)

    @pl.when(d < tm_size - 1)
    def _():
        greet(d + 1, k)

    for t in range(groups):
        @pl.when(m != t)
        def _(t=t):
            greet(4 * t + j, k)

    slots[0] = jnp.zeros((8, 128), jnp.int32)
    slots[0, 0:2, 0:16] = sends[...]

    n = lax.broadcasted_iota(jnp.int32, (64, 96), 0)
    col = lax.broadcasted_iota(jnp.int32, (64, 96), 1)
    a, b, c = n & 3, (n >> 2) & 3, n >> 4
    face, point = col >> 4, col & 15
    axis = face >> 1
    fixed = jnp.where(axis == 0, a, jnp.where(axis == 1, b, c))
    place = jnp.where(axis == 0, b + 4 * c, jnp.where(axis == 1, a + 4 * c, a + 4 * b))
    lift = ((fixed == 3 * (face & 1)) & (place == point)).astype(f32)
    spread = (lax.broadcasted_iota(jnp.int32, (16, 96), 0)
              == (lax.broadcasted_iota(jnp.int32, (16, 96), 1) & 15)).astype(f32)
    same = (lax.broadcasted_iota(jnp.int32, (96, 96), 0) >> 4
            == lax.broadcasted_iota(jnp.int32, (96, 96), 1) >> 4)

    def split(x):
        top = x.astype(jnp.bfloat16)
        return top, (x - top.astype(f32)).astype(jnp.bfloat16)

    def stacked(x):
        top, rest = split(x)
        return jnp.concatenate([jnp.concatenate([top, top], axis=1),
                                jnp.concatenate([rest, rest], axis=1)], axis=0)

    def times(table, x):
        both = jnp.dot(table, jnp.concatenate(split(x), axis=0), preferred_element_type=f32)
        half = both.shape[0] // 2
        return both[:half] + both[half:]

    for l in range(3):
        wide = jnp.dot(couplings[l], spread, precision=HI, preferred_element_type=f32)
        tables[l] = stacked(jnp.dot(lift, jnp.where(same, wide, 0.0), precision=HI,
                                    preferred_element_type=f32))
        edges[l] = stacked(jnp.where(same, wide, 0.0)[:32, :32])

    def prepare(level, begin, end):
        def block(part, carry):
            for i in range(8):
                whole = packed[level, 8 * part + i].astype(f32)
                for tile in (0, 1):
                    stage[tile, 72 * i:72 * i + 64, :] = whole[:, 128 * tile:128 * tile + 128]
            rows = pl.ds(pl.multiple_of(8 * part, 8), 8)
            for at in range(64):
                for tile in (0, 1):
                    inv[level, at, tile, rows, :] = stage[tile, pl.ds(at, 8, 72), :]
            return carry

        lax.fori_loop(begin, end, block, 0)

    nb = neighbours[...]
    picks[...] = jnp.where(nb < 256, nb, 512)

    loads[0].wait()
    prepare(0, 0, 3)

    pl.semaphore_wait(
        barrier,
        4 + groups + (d > 0).astype(jnp.int32) + (d < tm_size - 1).astype(jnp.int32))

    lists = [
        pltpu.make_async_remote_copy(slots.at[0], slots.at[1], slot_send.at[0], slot_recv.at[0],
                                     device_id=(d, above), device_id_type=MESH),
        pltpu.make_async_remote_copy(slots.at[0], slots.at[2], slot_send.at[1], slot_recv.at[1],
                                     device_id=(d, below), device_id_type=MESH)]
    for copy in lists:
        copy.start()

    back = jnp.maximum(d - 1, 0)
    forth = jnp.where(d > 0, d - 1, 1)
    ahead = pltpu.make_async_remote_copy(source.at[0], next_source, src_send, src_recv,
                                         device_id=(forth, k), device_id_type=MESH)

    @pl.when(d > 0)
    def _():
        ahead.start()

    @pl.when(d == tm_size - 1)
    def _():
        next_source[...] = jnp.zeros_like(next_source)

    prepare(0, 3, 8)
    loads[1].wait()
    loads[2].wait()
    for copy in lists:
        copy.wait()
    for row, (held, line, begin, exists) in enumerate(
            [(1, 1, 256, k > 0), (2, 0, 272, k < space_size - 1)]):
        for tile in (0, 1):
            lanes = pl.ds(128 * tile, 128)
            entry = jnp.broadcast_to(neighbours[row:row + 1, lanes], (8, 128)) - begin
            listed = jnp.broadcast_to(slots[held, line:line + 1, :], (8, 128))
            taken = lane_take(listed, jnp.clip(entry, 0, 15))
            limit = jnp.where(exists, 16, 0)
            valid = (entry >= 0) & (entry < limit)
            where_halo[row, :, lanes] = jnp.where(valid, taken, 512)

    def take_from(block, index_of):
        halves = []
        for tile in (0, 1):
            index = index_of(tile)
            spot = index & 127
            part = index >> 7
            halves.append(jnp.where(part == 0, lane_take(block[:, :128], spot),
                                    jnp.where(part == 1, lane_take(block[:, 128:], spot), 0.0)))
        return jnp.concatenate(halves, axis=1)

    def across(ref, begin, size, stride=None):
        return jnp.concatenate([ref[tile, pl.ds(begin, size, stride), :] for tile in (0, 1)], axis=1)

    def phi(level, slot, value, meanwhile=None):
        for tile in (0, 1):
            state[tile] = value[:, 128 * tile:128 * tile + 128]
        traces[slot, 0] = across(state, 0, 16, 4)
        traces[slot, 1] = across(state, 3, 16, 4)
        moves = [
            pltpu.make_async_remote_copy(traces.at[slot, 1], halo.at[slot, 0], halo_send.at[slot, 0],
                                         halo_recv.at[slot, 0], device_id=(d, above),
                                         device_id_type=MESH),
            pltpu.make_async_remote_copy(traces.at[slot, 0], halo.at[slot, 1], halo_send.at[slot, 1],
                                         halo_recv.at[slot, 1], device_id=(d, below),
                                         device_id_type=MESH)]
        for move in moves:
            move.start()
        faces = [
            traces[slot, 0], traces[slot, 1],
            jnp.concatenate([value[16 * q:16 * q + 4, :] for q in range(4)], axis=0),
            jnp.concatenate([value[16 * q + 12:16 * q + 16, :] for q in range(4)], axis=0),
            value[0:16, :], value[48:64, :]]
        picked = jnp.concatenate(
            [take_from(faces[f ^ 1], lambda tile, f=f: jnp.broadcast_to(
                picks[f:f + 1, 128 * tile:128 * tile + 128], (16, 128))) for f in range(6)], axis=0)
        coupled = times(tables[level], picked)
        known = mass[...] * value - coupled
        for tile in (0, 1):
            rhs[tile] = known[:, 128 * tile:128 * tile + 128]

        def early(q, total):
            for step in (1, 2):
                at = 4 * q + step
                total = total + inv[level, at] * rhs[:, pl.ds(at, 1), :]
            return total

        total = lax.fori_loop(0, 16, early, jnp.zeros((2, 64, 128), f32), unroll=True)
        if meanwhile is not None:
            prepare(*meanwhile)
        for move in moves:
            move.wait()
        got = jnp.concatenate(
            [take_from(halo[slot, row], lambda tile, row=row: jnp.concatenate(
                [where_halo[row, :, 128 * tile:128 * tile + 128]] * 2, axis=0))
             for row in (0, 1)], axis=0)
        change = times(edges[level], got)
        for row, kept, first in ((0, low, 0), (1, high, 3)):
            for tile in (0, 1):
                kept[tile] = (rhs[tile, pl.ds(first, 16, 4), :]
                              - change[16 * row:16 * row + 16, 128 * tile:128 * tile + 128])

        def late(q, total):
            total = total + inv[level, 4 * q] * low[:, pl.ds(q, 1), :]
            return total + inv[level, 4 * q + 3] * high[:, pl.ds(q, 1), :]

        total = lax.fori_loop(0, 16, late, total, unroll=True)
        return jnp.concatenate([total[0], total[1]], axis=1)

    value = source[1]
    value = phi(0, 0, value, (1, 0, 3)) + source[2]
    value = phi(0, 1, value, (1, 3, 6)) + source[3]
    value = phi(0, 0, value, (1, 6, 8))

    @pl.when(d < tm_size - 1)
    def _():
        ahead.wait_recv()

    @pl.when(d > 0)
    def _():
        ahead.wait_send()

    r_all[j] = value + next_source[...]
    shares = [pltpu.make_async_remote_copy(r_all.at[j], r_all.at[j], r_send.at[i], r_recv.at[j],
                                           device_id=(peer, k), device_id_type=MESH)
              for i, peer in enumerate(peers)]
    for share in shares:
        share.start()

    def share_arrived(i):
        @pl.when(j != i)
        def _():
            pltpu.make_async_remote_copy(r_all.at[i], r_all.at[i], r_send.at[0], r_recv.at[i],
                                         device_id=(peers[0], k), device_id_type=MESH).wait_recv()

    prepare(2, 0, 8)
    first = phi(2, 1, initial[...])
    share_arrived(0)
    value = phi(1, 0, r_all[0])
    share_arrived(1)
    value = phi(1, 1, value + r_all[1])
    share_arrived(2)
    value = phi(1, 0, value + r_all[2])
    share_arrived(3)
    s_all[m] = value + r_all[3] + jnp.where(m == 0, first, 0.0)

    onward = {t: pltpu.make_async_remote_copy(
        s_all.at[m], s_all.at[m], s_send.at[t], s_recv.at[m],
        device_id=(jnp.where(m < t, 4 * t + j, lax.rem(d + 4, tm_size)), k), device_id_type=MESH)
        for t in range(groups - 1, 0, -1)}
    for t, copy in onward.items():
        @pl.when(m < t)
        def _(copy=copy):
            copy.start()

    for share in shares:
        share.wait_send()

    def s_arrived(i):
        pltpu.make_async_remote_copy(s_all.at[i], s_all.at[i], s_send.at[0], s_recv.at[i],
                                     device_id=(lax.rem(d + 4, tm_size), k),
                                     device_id_type=MESH).wait_recv()

    @pl.when(m == 0)
    def _():
        w_in[...] = initial[...]

    @pl.when(m > 0)
    def _():
        s_arrived(0)
        w_in[...] = s_all[0]

    def coarse(i, carry):
        moved = phi(2, 2 + lax.rem(i, 2), w_in[...])
        s_arrived(i)
        w_in[...] = moved + s_all[i]
        return carry

    lax.fori_loop(1, m, coarse, 0)

    value = w_in[...]
    for i in (1, 2, 3):
        moved = phi(1, i % 2, value) + r_all[i - 1]
        value = jnp.where(j >= i, moved, value)
    out[0] = value
    for i in (1, 2, 3):
        value = phi(0, (i + 1) % 2, value) + source[i]
        out[i] = value

    for t, copy in onward.items():
        @pl.when(m < t)
        def _(copy=copy):
            copy.wait_send()


def pair_kernel(tm_size, source_in, initial_in, mass_in, inverses, couplings_in, neighbours_in, sends_in,
                out, source, initial, mass, couplings, neighbours, sends, in_sem, packed, inv, gout, ginv, tables, state, rhs, change, grhs, picks, listed, rows,
                start_out, start_in, gmass, next_source, r_all, rg_out, rg_all, first, w_in, wg_in,
                s_all, sg_out, sg_all, fresh_out, fresh_in,
                inv_sem, gi_send, gi_recv, st_send, st_recv, src_send, src_recv,
                r_send, r_recv, rg_send, rg_recv, s_send, s_recv, sg_send, sg_recv, fr_send, fr_recv):
    f32, bf16, i32 = jnp.float32, jnp.bfloat16, jnp.int32
    d = lax.axis_index("tm")
    k = lax.axis_index("space")
    j = lax.rem(d, 4)
    m = lax.div(d, 4)
    groups = tm_size // 4
    other = 1 - k
    upper = k == 0
    peers = [4 * m + j + 1 - 2 * lax.rem(j, 2), 4 * m + lax.rem(j + 2, 4), 4 * m + 3 - j]

    loads = [pltpu.make_async_copy(inverses.at[l], packed.at[l], inv_sem.at[l]) for l in range(3)]
    fetches = [pltpu.make_async_copy(src, dst, in_sem.at[x]) for x, (src, dst) in enumerate([
        (neighbours_in, neighbours), (sends_in, sends), (source_in, source), (initial_in, initial),
        (mass_in, mass), (couplings_in, couplings)])]
    for copy in [*fetches[:2], loads[0], *fetches[2:]]:
        copy.start()

    barrier = pltpu.get_barrier_semaphore()

    def greet(t, s):
        pl.semaphore_signal(barrier, inc=1, device_id=(t, s), device_id_type=MESH)

    greet(d, other)
    for peer in peers:
        greet(peer, k)
        greet(peer, other)

    @pl.when(d > 0)
    def _():
        greet(d - 1, k)

    @pl.when(d < tm_size - 1)
    def _():
        greet(d + 1, k)

    for t in range(groups):
        @pl.when(m != t)
        def _(t=t):
            greet(4 * t + j, k)
            greet(4 * t + j, other)

    r256 = lax.broadcasted_iota(i32, (256, 256), 0)
    c256 = lax.broadcasted_iota(i32, (256, 256), 1)
    swap = jnp.where((r256 >> 4 == (c256 & 15)) & ((r256 & 15) == c256 >> 4), 1.0, 0.0).astype(bf16)
    rows[...] = jnp.zeros((8, 128), i32)

    for fetch in fetches[:2]:
        fetch.wait()

    lane = lax.broadcasted_iota(i32, (8, 128), 1)
    place, layer = lane & 15, lane >> 4
    nb = neighbours[...]
    begin = jnp.where(upper, 272, 256)
    spot = nb - begin
    picks[:, 0:256] = jnp.where(nb < 256, nb, jnp.where((spot >= 0) & (spot < 16), 256 + spot, 512))
    rows[0:2, 0:16] = sends[...]

    def both(row):
        return [jnp.broadcast_to(nb[row:row + 1, 128 * t:128 * t + 128], (8, 128)) for t in (0, 1)]

    def chosen(a, b):
        return [jnp.where(upper, x, y) for x, y in zip(a, b)]

    def among(pair, index):
        at = index & 127
        return jnp.where(index < 128, lane_take(pair[0], at), lane_take(pair[1], at))

    facing = chosen(both(1), both(0))
    inward = chosen(both(0), both(1))
    ends = jnp.where(upper, jnp.broadcast_to(rows[1:2, :], (8, 128)), jnp.broadcast_to(rows[0:1, :], (8, 128)))
    edge = lane_take(ends, place)
    deeper = among(inward, edge)
    deepest = among(inward, jnp.minimum(deeper, 255))
    listed[...] = jnp.where(layer == 0, edge, jnp.where(layer == 1, deeper, jnp.where(layer == 2, deepest, 512)))
    twice = jnp.where((lane & 31) < 16, edge, deeper)

    def low_half(shape):
        return lax.broadcasted_iota(i32, shape, 1) < 64

    def boundary(x):
        index = jnp.concatenate([listed[...]] * 8, axis=0)
        at, part = index & 127, index >> 7
        g = jnp.where(part == 0, lane_take(x[:, :128], at), jnp.where(part == 1, lane_take(x[:, 128:], at), 0.0))
        return jnp.where(low_half((32, 128)), g[:32], pltpu.roll(g[32:], 64, 1))

    def opened(p):
        return jnp.concatenate([p, pltpu.roll(p, 64, 1)], axis=0)

    def split(x):
        top = x.astype(bf16)
        return top, (x - top.astype(f32)).astype(bf16)

    def times(table, x):
        pair = jnp.dot(table, jnp.concatenate(split(x), axis=0), preferred_element_type=f32)
        half = pair.shape[0] // 2
        return pair[:half] + pair[half:]

    def tile16(level, bi, bj):
        return jnp.concatenate(
            [packed[level, 16 * bi + i, 16 * bj:16 * bj + 16, :] for i in range(16)], axis=0)

    element = lax.broadcasted_iota(i32, (256, 128), 0)
    quarter = lax.broadcasted_iota(i32, (256, 128), 1) >> 5
    hit = element == jnp.concatenate([twice] * 32, axis=0)
    spots = jnp.concatenate([jnp.where(hit & (quarter == q), 1.0, 0.0).astype(bf16) for q in range(4)], axis=0)

    def prepare_ghost(level):
        for pair in (0, 2):
            taken = jnp.concatenate([
                jnp.dot(jnp.concatenate([tile16(level, bi, bj) for bj in range(4)], axis=1), spots,
                        preferred_element_type=f32).astype(bf16) for bi in (pair, pair + 1)], axis=1)
            turned = jnp.dot(swap, taken, preferred_element_type=f32)
            for jj in range(16):
                for x in (0, 1):
                    gout[level, pair + x, jj] = turned[16 * jj:16 * jj + 16, 128 * x:128 * x + 128]

    def prepare(level):
        for bi in range(4):
            for bj in range(4):
                turned = jnp.dot(swap, tile16(level, bi, bj), preferred_element_type=f32)
                for jj in range(16):
                    for tile in (0, 1):
                        inv[level, 16 * bj + jj, tile, 16 * bi:16 * bi + 16, :] = turned[
                            16 * jj:16 * jj + 16, 128 * tile:128 * tile + 128]

    for fetch in fetches[2:]:
        fetch.wait()
    for i in range(3):
        start_out[i] = boundary(source[i + 1])
    start_out[3] = boundary(initial[...])
    start_out[4] = boundary(mass[...])

    loads[0].wait()
    for load in loads[1:]:
        load.start()
    prepare_ghost(0)
    pl.semaphore_wait(
        barrier,
        7 + 2 * (groups - 1) + (d > 0).astype(i32) + (d < tm_size - 1).astype(i32))

    def beside_copy(src, dst, send, recv):
        return pltpu.make_async_remote_copy(src, dst, send, recv, device_id=(d, other), device_id_type=MESH)

    began = beside_copy(start_out, start_in, st_send, st_recv)
    began.start()
    ghosts = [[beside_copy(gout.at[l, x], ginv.at[l, x], gi_send.at[l, x], gi_recv.at[l, x])
               for x in range(4)] for l in range(3)]
    for copy in ghosts[0]:
        copy.start()

    forth = jnp.where(d > 0, d - 1, 1)
    ahead = pltpu.make_async_remote_copy(source.at[0], next_source, src_send, src_recv,
                                         device_id=(forth, k), device_id_type=MESH)

    @pl.when(d > 0)
    def _():
        ahead.start()

    @pl.when(d == tm_size - 1)
    def _():
        next_source[...] = jnp.zeros_like(next_source)

    prepare(0)
    meets = among(facing, edge) - begin
    beside = jnp.zeros((8, 128), i32)
    for p in range(16):
        at = jnp.full((8, 128), p, i32)
        beside = jnp.where(place == lane_take(meets, at), lane_take(edge, at), beside)
    for f in range(2, 6):
        step = among(both(f), beside)
        onto = among(facing, jnp.minimum(step, 255)) - begin
        picks[f:f + 1, 256:384] = jnp.where((step < 256) & (layer < 3), 256 + 16 * layer + (onto & 15), 512)[0:1]
    toward = jnp.where(layer == 0, beside, jnp.where(layer < 3, 240 + lane, 512))
    away = jnp.where(layer < 2, 272 + lane, 512)
    picks[0:1, 256:384] = jnp.where(upper, toward, away)[0:1]
    picks[1:2, 256:384] = jnp.where(upper, away, toward)[0:1]

    n = lax.broadcasted_iota(i32, (64, 96), 0)
    col = lax.broadcasted_iota(i32, (64, 96), 1)
    a, b, c = n & 3, (n >> 2) & 3, n >> 4
    face, point = col >> 4, col & 15
    axis = face >> 1
    fixed = jnp.where(axis == 0, a, jnp.where(axis == 1, b, c))
    where = jnp.where(axis == 0, b + 4 * c, jnp.where(axis == 1, a + 4 * c, a + 4 * b))
    lift = ((fixed == 3 * (face & 1)) & (where == point)).astype(f32).astype(bf16)
    spread = (lax.broadcasted_iota(i32, (16, 96), 0)
              == (lax.broadcasted_iota(i32, (16, 96), 1) & 15)).astype(f32).astype(bf16)
    same = (lax.broadcasted_iota(i32, (96, 96), 0) >> 4
            == lax.broadcasted_iota(i32, (96, 96), 1) >> 4)

    blocks = [x for l in range(3) for x in split(couplings[l])]
    wide = jnp.dot(jnp.concatenate(blocks, axis=0), spread, preferred_element_type=f32)
    wide = jnp.concatenate([jnp.where(same, wide[96 * x:96 * x + 96], 0.0) for x in range(6)], axis=1)
    lifted = jnp.dot(lift, wide.astype(bf16), preferred_element_type=f32).astype(bf16)
    for l in range(3):
        for x in (0, 1):
            half = lifted[:, 96 * (2 * l + x):96 * (2 * l + x) + 96]
            tables[l, 64 * x:64 * x + 64, :] = jnp.concatenate([half, half], axis=1)

    began.wait_recv()
    gmass[...] = opened(start_in[4])

    def across(begin, tiles):
        return jnp.concatenate([state[tile, pl.ds(begin, 16, 4), :] for tile in range(tiles)], axis=1)

    once = jnp.minimum(d + 1, 1)

    def sides(x):
        return [jnp.concatenate([x[16 * q:16 * q + 4, :] for q in range(4)], axis=0),
                jnp.concatenate([x[16 * q + 12:16 * q + 16, :] for q in range(4)], axis=0),
                x[0:16, :], x[48:64, :]]

    def gather(block, f, tile, origins):
        index = jnp.broadcast_to(picks[f:f + 1, 128 * tile:128 * tile + 128], (8, 128))
        at, part = index & 127, index >> 7
        at = jnp.concatenate([at, at], axis=0)
        part = jnp.concatenate([part, part], axis=0)
        found = jnp.zeros((16, 128), f32)
        for origin in origins:
            found = jnp.where(part == origin, lane_take(block(origin), at), found)
        return found

    def columns(block):
        return lambda origin: block[:, 128 * origin:128 * origin + 128]

    def product_of(level, total):
        def product(_, total):
            for at in range(64):
                total = total + inv[level, at] * rhs[:, pl.ds(at, 1), :]
            return total
        return lax.fori_loop(0, once, product, total)

    def ghost_rhs(ghost, coupled):
        known = gmass[...] * ghost - coupled
        which = lax.broadcasted_iota(i32, (16, 128), 1) >> 5
        dense = known[0:16]
        for q in (1, 2, 3):
            dense = jnp.where(which == q, pltpu.roll(known[16 * q:16 * q + 16], 32 * q, 1), dense)
        grhs[...] = dense

    def ghost_step(level):
        def ghost_product(_, total):
            for at in range(16):
                total = total + ginv[level, :, at] * grhs[pl.ds(at, 1), :][None]
            return total

        gsum = lax.fori_loop(0, once, ghost_product, jnp.zeros((4, 16, 128), f32)).reshape(64, 128)
        gsum = gsum + pltpu.roll(gsum, 64, 1)
        return gsum + pltpu.roll(gsum, 32, 1)

    def keep(x, tiles):
        for tile in tiles:
            state[tile] = x[:, 128 * (tile - tiles[0]):128 * (tile - tiles[0]) + 128]

    def phi(level, value, ghost, more, awaited=()):
        tiles = 3 if more else 2
        keep(value, (0, 1))
        state[2] = ghost
        whole = jnp.concatenate([value, ghost], axis=1) if more else value
        faces = [across(0, 3), across(3, 3), *sides(whole)]
        picked = jnp.concatenate([jnp.concatenate([
            gather(columns(faces[f ^ 1]), f, tile, (0, 1, 2) if f < 2 else (0, 1) if tile < 2 else (2,))
            for tile in range(tiles)], axis=1) for f in range(6)], axis=0)
        coupled = times(tables[level], picked)
        known = mass[...] * value - coupled[:, :256]
        for tile in (0, 1):
            rhs[tile] = known[:, 128 * tile:128 * tile + 128]
        if more:
            ghost_rhs(ghost, coupled[:, 256:])
        total = product_of(level, jnp.zeros((2, 64, 128), f32))
        result = jnp.concatenate([total[0], total[1]], axis=1)
        if not more:
            return result, ghost
        for copy in awaited:
            copy.wait_recv()
        return result, ghost_step(level)

    def phi_fresh(level, value, slot):
        fresh_out[slot] = boundary(value)
        copy = beside_copy(fresh_out.at[slot], fresh_in.at[slot], fr_send.at[slot], fr_recv.at[slot])
        copy.start()
        keep(value, (0, 1))
        faces = [across(0, 2), across(3, 2), *sides(value)]
        picked = jnp.concatenate([jnp.concatenate([
            gather(columns(faces[f ^ 1]), f, tile, (0, 1)) for tile in (0, 1)], axis=1)
            for f in range(6)], axis=0)
        known = mass[...] * value - times(tables[level], picked)
        for tile in (0, 1):
            rhs[tile] = known[:, 128 * tile:128 * tile + 128]
        total = product_of(level, jnp.zeros((2, 64, 128), f32))
        copy.wait()
        ghost = opened(fresh_in[slot])
        state[2] = ghost
        ends = [state[2, pl.ds(0, 16, 4), :], state[2, pl.ds(3, 16, 4), :]]
        near = [across(0, 2), across(3, 2)]
        beyond = sides(ghost)
        nothing = jnp.zeros((16, 256), f32)
        rows_of = []
        for f in range(6):
            if f < 2:
                def source_of(origin, f=f):
                    return ends[f ^ 1] if origin == 2 else columns(near[f ^ 1])(origin)
                rows_of.append(jnp.concatenate(
                    [gather(source_of, f, 0, (2,)), gather(source_of, f, 1, (2,)),
                     gather(source_of, f, 2, (0, 1, 2))], axis=1))
            else:
                rows_of.append(jnp.concatenate(
                    [nothing, gather(lambda _, f=f: beyond[(f ^ 1) - 2], f, 2, (2,))], axis=1))
        coupled = times(tables[level], jnp.concatenate(rows_of, axis=0))
        ghost_rhs(ghost, coupled[:, 256:])
        for tile in (0, 1):
            state[tile] = coupled[:, 128 * tile:128 * tile + 128]
            change[tile] = jnp.where(upper, state[tile, pl.ds(3, 16, 4), :], state[tile, pl.ds(0, 16, 4), :])
        offset = 3 - 3 * k

        def corrected(_, total):
            for q in range(16):
                total = total - inv[level, 4 * q + offset] * change[:, pl.ds(q, 1), :]
            return total

        total = lax.fori_loop(0, once, corrected, total)
        return jnp.concatenate([total[0], total[1]], axis=1), ghost_step(level), ghost

    value, ghost = source[1], opened(start_in[0])
    for i in (2, 3):
        value, ghost = phi(0, value, ghost, True, ghosts[0] if i == 2 else ())
        value, ghost = value + source[i], ghost + opened(start_in[i - 1])
    value, _ = phi(0, value, ghost, False)

    @pl.when(d < tm_size - 1)
    def _():
        ahead.wait_recv()

    @pl.when(d > 0)
    def _():
        ahead.wait_send()

    value = value + next_source[...]
    r_all[j] = value
    rg_out[...] = boundary(value)
    edges_out = [pltpu.make_async_remote_copy(rg_out, rg_all.at[j], rg_send.at[i], rg_recv.at[j],
                                              device_id=(peer, other), device_id_type=MESH)
                 for i, peer in enumerate([*peers, d])]
    shares = [pltpu.make_async_remote_copy(r_all.at[j], r_all.at[j], r_send.at[i], r_recv.at[j],
                                           device_id=(peer, k), device_id_type=MESH)
              for i, peer in enumerate(peers)]

    @pl.when(j < 3)
    def _():
        for copy in edges_out:
            copy.start()

    for share in shares:
        share.start()

    loads[1].wait()
    prepare_ghost(1)
    for copy in ghosts[1]:
        copy.start()
    prepare(1)
    loads[2].wait()
    prepare(2)
    first[...] = phi(2, initial[...], opened(start_in[3]), False)[0]

    def share_arrived(i):
        if i < 3:
            pltpu.make_async_remote_copy(rg_out, rg_all.at[i], rg_send.at[0], rg_recv.at[i],
                                         device_id=(d, other), device_id_type=MESH).wait_recv()

        @pl.when(j != i)
        def _():
            pltpu.make_async_remote_copy(r_all.at[i], r_all.at[i], r_send.at[0], r_recv.at[i],
                                         device_id=(peers[0], k), device_id_type=MESH).wait_recv()

    share_arrived(0)
    value, ghost = r_all[0], opened(rg_all[0])
    for i in (1, 2):
        value, ghost = phi(1, value, ghost, True, ghosts[1] if i == 1 else ())
        share_arrived(i)
        value, ghost = value + r_all[i], ghost + opened(rg_all[i])
    value, _ = phi(1, value, ghost, False)
    share_arrived(3)
    value = value + r_all[3] + jnp.where(m == 0, first[...], 0.0)
    s_all[m] = value
    sg_out[...] = boundary(value)

    onward = []
    for t in range(groups - 1, 0, -1):
        target = jnp.where(m < t, 4 * t + j, lax.rem(d + 4, tm_size))
        own = pltpu.make_async_remote_copy(
            s_all.at[m], s_all.at[m], s_send.at[t], s_recv.at[m],
            device_id=(target, k), device_id_type=MESH)
        edge_out = pltpu.make_async_remote_copy(
            sg_out, sg_all.at[m], sg_send.at[t], sg_recv.at[m],
            device_id=(target, other), device_id_type=MESH)
        onward += [(m < t - 1, edge_out), (m < t, own)]

        @pl.when(m < t - 1)
        def _(edge_out=edge_out):
            edge_out.start()

        @pl.when(m < t)
        def _(own=own):
            own.start()

    @pl.when(j < 3)
    def _():
        for copy in edges_out:
            copy.wait_send()

    for share in shares:
        share.wait_send()

    def s_arrived(i):
        pltpu.make_async_remote_copy(s_all.at[i], s_all.at[i], s_send.at[0], s_recv.at[i],
                                     device_id=(lax.rem(d + 4, tm_size), k),
                                     device_id_type=MESH).wait_recv()

    prepare_ghost(2)
    for copy in ghosts[2]:
        copy.start()

    def s_edge_arrived(i):
        pltpu.make_async_remote_copy(sg_out, sg_all.at[i], sg_send.at[0], sg_recv.at[i],
                                     device_id=(lax.rem(d + 4, tm_size), other),
                                     device_id_type=MESH).wait_recv()

    for copy in ghosts[2]:
        copy.wait_recv()

    @pl.when(m == 0)
    def _():
        w_in[...] = initial[...]

    @pl.when(m > 0)
    def _():
        s_arrived(0)
        w_in[...] = s_all[0]

    @pl.when(m > 1)
    def _():
        s_edge_arrived(0)
        wg_in[...] = opened(sg_all[0])

    for i in range(1, groups - 1):
        @pl.when(i < m)
        def _(i=i):
            if i > 1 and i % 3 == 1:
                value, ghost, _ = phi_fresh(2, w_in[...], 1 + i)
            else:
                value, ghost = phi(2, w_in[...], wg_in[...], True)
            s_arrived(i)
            w_in[...] = value + s_all[i]

            @pl.when(i < m - 1)
            def _():
                s_edge_arrived(i)
                wg_in[...] = ghost + opened(sg_all[i])

    value = w_in[...]
    for i in (1, 2, 3):
        if i == 1:
            moved, gmoved, ghost = phi_fresh(1, value, 0)
        else:
            moved, gmoved = phi(1, value, ghost, i < 3)
        value = jnp.where(j >= i, moved + r_all[i - 1], value)
        if i < 3:
            ghost = jnp.where(j >= i, gmoved + opened(rg_all[i - 1]), ghost)
    out[0] = value
    for i in (1, 2, 3):
        if i == 1:
            value, ghost, _ = phi_fresh(0, value, 1)
        else:
            value, ghost = phi(0, value, ghost, i < 3)
        value = value + source[i]
        if i < 3:
            ghost = ghost + opened(start_in[i - 1])
        out[i] = value

    for sent, copy in onward:
        @pl.when(sent)
        def _(copy=copy):
            copy.wait_send()
    began.wait_send()
    for level in ghosts:
        for copy in level:
            copy.wait_send()


def pair_local(tm_size, source, initial, mass, inverses, couplings, neighbours, sends):
    f32, bf16, i32 = jnp.float32, jnp.bfloat16, jnp.int32
    vmem = pl.BlockSpec(memory_space=pltpu.VMEM)
    dma = pltpu.SemaphoreType.DMA
    groups = tm_size // 4
    return pl.pallas_call(
        functools.partial(pair_kernel, tm_size),
        out_shape=jax.ShapeDtypeStruct(source.shape, f32),
        in_specs=[pl.BlockSpec(memory_space=pltpu.MemorySpace.HBM)] * 7,
        out_specs=vmem,
        scratch_shapes=[
            pltpu.VMEM(source.shape, f32),
            pltpu.VMEM(initial.shape, f32),
            pltpu.VMEM(mass.shape, f32),
            pltpu.VMEM((3, 96, 16), f32),
            pltpu.VMEM(neighbours.shape, i32),
            pltpu.VMEM(sends.shape, i32),
            dma((6,)),
            pltpu.VMEM(inverses.shape, bf16),
            pltpu.VMEM((3, 64, 2, 64, 128), f32),
            pltpu.VMEM((3, 4, 16, 16, 128), f32),
            pltpu.VMEM((3, 4, 16, 16, 128), f32),
            pltpu.VMEM((3, 128, 192), bf16),
            pltpu.VMEM((3, 64, 128), f32),
            pltpu.VMEM((2, 64, 128), f32),
            pltpu.VMEM((2, 16, 128), f32),
            pltpu.VMEM((16, 128), f32),
            pltpu.VMEM((6, 384), i32),
            pltpu.VMEM((8, 128), i32),
            pltpu.VMEM((8, 128), i32),
            pltpu.VMEM((5, 32, 128), f32),
            pltpu.VMEM((5, 32, 128), f32),
            pltpu.VMEM((64, 128), f32),
            pltpu.VMEM((64, 256), f32),
            pltpu.VMEM((4, 64, 256), f32),
            pltpu.VMEM((32, 128), f32),
            pltpu.VMEM((4, 32, 128), f32),
            pltpu.VMEM((64, 256), f32),
            pltpu.VMEM((64, 256), f32),
            pltpu.VMEM((64, 128), f32),
            pltpu.VMEM((groups, 64, 256), f32),
            pltpu.VMEM((32, 128), f32),
            pltpu.VMEM((groups, 32, 128), f32),
            pltpu.VMEM((max(2, groups), 32, 128), f32),
            pltpu.VMEM((max(2, groups), 32, 128), f32),
            dma((3,)), dma((3, 4)), dma((3, 4)), dma, dma, dma, dma,
            dma((3,)), dma((4,)), dma((4,)), dma((4,)),
            dma((groups,)), dma((groups,)), dma((groups,)), dma((groups,)),
            dma((max(2, groups),)), dma((max(2, groups),)),
        ],
        compiler_params=pltpu.CompilerParams(collective_id=0, has_side_effects=True,
                                             vmem_limit_bytes=48 << 20),
        name="cycle",
    )(*[pltpu.with_memory_space_constraint(x, pltpu.MemorySpace.HBM) for x in (source, initial, mass, inverses, couplings.reshape(3, 96, 16), neighbours, sends)])


def local(tm_size, space_size, source, initial, mass, inverses, couplings, neighbours, sends):
    f32 = jnp.float32
    vmem = pl.BlockSpec(memory_space=pltpu.VMEM)
    dma = pltpu.SemaphoreType.DMA
    return pl.pallas_call(
        functools.partial(kernel, tm_size, space_size),
        out_shape=jax.ShapeDtypeStruct(source.shape, f32),
        in_specs=[vmem, vmem, vmem, pl.BlockSpec(memory_space=pl.ANY), vmem, vmem, vmem],
        out_specs=vmem,
        scratch_shapes=[
            pltpu.VMEM(inverses.shape, jnp.bfloat16),
            pltpu.VMEM((2, 576, 128), f32),
            pltpu.VMEM((3, 64, 2, 64, 128), f32),
            pltpu.VMEM((3, 128, 192), jnp.bfloat16),
            pltpu.VMEM((3, 64, 64), jnp.bfloat16),
            pltpu.VMEM((2, 64, 128), f32),
            pltpu.VMEM((4, 2, 16, 256), f32),
            pltpu.VMEM((4, 2, 16, 256), f32),
            pltpu.VMEM((2, 64, 128), f32),
            pltpu.VMEM((2, 16, 128), f32),
            pltpu.VMEM((2, 16, 128), f32),
            pltpu.VMEM((3, 8, 128), jnp.int32),
            pltpu.VMEM((6, 256), jnp.int32),
            pltpu.VMEM((2, 8, 256), jnp.int32),
            pltpu.VMEM((64, 256), f32),
            pltpu.VMEM((4, 64, 256), f32),
            pltpu.VMEM((64, 256), f32),
            pltpu.VMEM((tm_size // 4, 64, 256), f32),
            dma((3,)), dma((4, 2)), dma((4, 2)), dma((2,)), dma((2,)), dma, dma,
            dma((3,)), dma((4,)), dma((tm_size // 4,)), dma((tm_size // 4,)),
        ],
        compiler_params=pltpu.CompilerParams(collective_id=0, has_side_effects=True),
        name="cycle",
    )(source, initial, mass, inverses, couplings.reshape(3, 96, 16), neighbours, sends)


def solution(mesh):
    placed = (
        P("tm", None, "space"),
        P(None, "space"),
        P(None, "space"),
        P(None, None, None, "space"),
        P(),
        P(None, "space"),
        P(None, "space"),
    )
    body = (functools.partial(pair_local, mesh.shape["tm"]) if mesh.shape["space"] == 2
            else functools.partial(local, mesh.shape["tm"], mesh.shape["space"]))
    return jax.shard_map(
        body,
        mesh=mesh, in_specs=placed, out_specs=P("tm", None, "space"), check_vma=False)
```

```python
import functools
import jax
import jax.numpy as jnp
from jax import lax
from jax.experimental import pallas as pl
from jax.experimental.pallas import tpu as pltpu
from jax.sharding import PartitionSpec as P

MESH = pl.DeviceIdType.MESH
HI = lax.Precision.HIGHEST


def lane_take(block, index):
    return jnp.take_along_axis(block, index, axis=1, mode="promise_in_bounds")


def kernel(tm_size, space_size, source, initial, mass, inverses, couplings, neighbours, sends,
           out, packed, stage, inv, tables, edges, state, traces, halo, rhs, low, high, slots, picks, where_halo,
           next_source, r_all, w_in, s_all,
           inv_sem, halo_send, halo_recv, slot_send, slot_recv, src_send, src_recv,
           r_send, r_recv, s_send, s_recv):
    f32 = jnp.float32
    d = lax.axis_index("tm")
    k = lax.axis_index("space")
    j = lax.rem(d, 4)
    m = lax.div(d, 4)
    groups = tm_size // 4
    above = lax.rem(k + 1, space_size)
    below = lax.rem(k + space_size - 1, space_size)
    peers = [4 * m + lax.rem(j + step, 4) for step in (1, 2, 3)]

    loads = [pltpu.make_async_copy(inverses.at[l], packed.at[l], inv_sem.at[l]) for l in range(3)]
    loads[0].start()
    loads[1].start()
    loads[2].start()

    barrier = pltpu.get_barrier_semaphore()

    def greet(t, s):
        pl.semaphore_signal(barrier, inc=1, device_id=(t, s), device_id_type=MESH)

    greet(d, above)
    greet(d, below)
    for peer in peers:
        greet(peer, k)

    @pl.when(d > 0)
    def _():
        greet(d - 1, k)

    @pl.when(d < tm_size - 1)
    def _():
        greet(d + 1, k)

    for t in range(groups):
        @pl.when(m != t)
        def _(t=t):
            greet(4 * t + j, k)

    slots[0] = jnp.zeros((8, 128), jnp.int32)
    slots[0, 0:2, 0:16] = sends[...]

    n = lax.broadcasted_iota(jnp.int32, (64, 96), 0)
    col = lax.broadcasted_iota(jnp.int32, (64, 96), 1)
    a, b, c = n & 3, (n >> 2) & 3, n >> 4
    face, point = col >> 4, col & 15
    axis = face >> 1
    fixed = jnp.where(axis == 0, a, jnp.where(axis == 1, b, c))
    place = jnp.where(axis == 0, b + 4 * c, jnp.where(axis == 1, a + 4 * c, a + 4 * b))
    lift = ((fixed == 3 * (face & 1)) & (place == point)).astype(f32)
    spread = (lax.broadcasted_iota(jnp.int32, (16, 96), 0)
              == (lax.broadcasted_iota(jnp.int32, (16, 96), 1) & 15)).astype(f32)
    same = (lax.broadcasted_iota(jnp.int32, (96, 96), 0) >> 4
            == lax.broadcasted_iota(jnp.int32, (96, 96), 1) >> 4)

    def split(x):
        top = x.astype(jnp.bfloat16)
        return top, (x - top.astype(f32)).astype(jnp.bfloat16)

    def stacked(x):
        top, rest = split(x)
        return jnp.concatenate([jnp.concatenate([top, top], axis=1),
                                jnp.concatenate([rest, rest], axis=1)], axis=0)

    def times(table, x):
        both = jnp.dot(table, jnp.concatenate(split(x), axis=0), preferred_element_type=f32)
        half = both.shape[0] // 2
        return both[:half] + both[half:]

    for l in range(3):
        wide = jnp.dot(couplings[l], spread, precision=HI, preferred_element_type=f32)
        tables[l] = stacked(jnp.dot(lift, jnp.where(same, wide, 0.0), precision=HI,
                                    preferred_element_type=f32))
        edges[l] = stacked(jnp.where(same, wide, 0.0)[:32, :32])

    def prepare(level, begin, end):
        def block(part, carry):
            for i in range(8):
                whole = packed[level, 8 * part + i].astype(f32)
                for tile in (0, 1):
                    stage[tile, 72 * i:72 * i + 64, :] = whole[:, 128 * tile:128 * tile + 128]
            rows = pl.ds(pl.multiple_of(8 * part, 8), 8)
            for at in range(64):
                for tile in (0, 1):
                    inv[level, at, tile, rows, :] = stage[tile, pl.ds(at, 8, 72), :]
            return carry

        lax.fori_loop(begin, end, block, 0)

    nb = neighbours[...]
    picks[...] = jnp.where(nb < 256, nb, 512)

    loads[0].wait()
    prepare(0, 0, 3)

    pl.semaphore_wait(
        barrier,
        4 + groups + (d > 0).astype(jnp.int32) + (d < tm_size - 1).astype(jnp.int32))

    lists = [
        pltpu.make_async_remote_copy(slots.at[0], slots.at[1], slot_send.at[0], slot_recv.at[0],
                                     device_id=(d, above), device_id_type=MESH),
        pltpu.make_async_remote_copy(slots.at[0], slots.at[2], slot_send.at[1], slot_recv.at[1],
                                     device_id=(d, below), device_id_type=MESH)]
    for copy in lists:
        copy.start()

    back = jnp.maximum(d - 1, 0)
    forth = jnp.where(d > 0, d - 1, 1)
    ahead = pltpu.make_async_remote_copy(source.at[0], next_source, src_send, src_recv,
                                         device_id=(forth, k), device_id_type=MESH)

    @pl.when(d > 0)
    def _():
        ahead.start()

    @pl.when(d == tm_size - 1)
    def _():
        next_source[...] = jnp.zeros_like(next_source)

    prepare(0, 3, 8)
    loads[1].wait()
    loads[2].wait()
    for copy in lists:
        copy.wait()
    for row, (held, line, begin, exists) in enumerate(
            [(1, 1, 256, k > 0), (2, 0, 272, k < space_size - 1)]):
        for tile in (0, 1):
            lanes = pl.ds(128 * tile, 128)
            entry = jnp.broadcast_to(neighbours[row:row + 1, lanes], (8, 128)) - begin
            listed = jnp.broadcast_to(slots[held, line:line + 1, :], (8, 128))
            taken = lane_take(listed, jnp.clip(entry, 0, 15))
            limit = jnp.where(exists, 16, 0)
            valid = (entry >= 0) & (entry < limit)
            where_halo[row, :, lanes] = jnp.where(valid, taken, 512)

    def take_from(block, index_of):
        halves = []
        for tile in (0, 1):
            index = index_of(tile)
            spot = index & 127
            part = index >> 7
            halves.append(jnp.where(part == 0, lane_take(block[:, :128], spot),
                                    jnp.where(part == 1, lane_take(block[:, 128:], spot), 0.0)))
        return jnp.concatenate(halves, axis=1)

    def across(ref, begin, size, stride=None):
        return jnp.concatenate([ref[tile, pl.ds(begin, size, stride), :] for tile in (0, 1)], axis=1)

    def phi(level, slot, value, meanwhile=None):
        for tile in (0, 1):
            state[tile] = value[:, 128 * tile:128 * tile + 128]
        traces[slot, 0] = across(state, 0, 16, 4)
        traces[slot, 1] = across(state, 3, 16, 4)
        moves = [
            pltpu.make_async_remote_copy(traces.at[slot, 1], halo.at[slot, 0], halo_send.at[slot, 0],
                                         halo_recv.at[slot, 0], device_id=(d, above),
                                         device_id_type=MESH),
            pltpu.make_async_remote_copy(traces.at[slot, 0], halo.at[slot, 1], halo_send.at[slot, 1],
                                         halo_recv.at[slot, 1], device_id=(d, below),
                                         device_id_type=MESH)]
        for move in moves:
            move.start()
        faces = [
            traces[slot, 0], traces[slot, 1],
            jnp.concatenate([value[16 * q:16 * q + 4, :] for q in range(4)], axis=0),
            jnp.concatenate([value[16 * q + 12:16 * q + 16, :] for q in range(4)], axis=0),
            value[0:16, :], value[48:64, :]]
        picked = jnp.concatenate(
            [take_from(faces[f ^ 1], lambda tile, f=f: jnp.broadcast_to(
                picks[f:f + 1, 128 * tile:128 * tile + 128], (16, 128))) for f in range(6)], axis=0)
        coupled = times(tables[level], picked)
        known = mass[...] * value - coupled
        for tile in (0, 1):
            rhs[tile] = known[:, 128 * tile:128 * tile + 128]

        def early(q, total):
            for step in (1, 2):
                at = 4 * q + step
                total = total + inv[level, at] * rhs[:, pl.ds(at, 1), :]
            return total

        total = lax.fori_loop(0, 16, early, jnp.zeros((2, 64, 128), f32), unroll=True)
        if meanwhile is not None:
            prepare(*meanwhile)
        for move in moves:
            move.wait()
        got = jnp.concatenate(
            [take_from(halo[slot, row], lambda tile, row=row: jnp.concatenate(
                [where_halo[row, :, 128 * tile:128 * tile + 128]] * 2, axis=0))
             for row in (0, 1)], axis=0)
        change = times(edges[level], got)
        for row, kept, first in ((0, low, 0), (1, high, 3)):
            for tile in (0, 1):
                kept[tile] = (rhs[tile, pl.ds(first, 16, 4), :]
                              - change[16 * row:16 * row + 16, 128 * tile:128 * tile + 128])

        def late(q, total):
            total = total + inv[level, 4 * q] * low[:, pl.ds(q, 1), :]
            return total + inv[level, 4 * q + 3] * high[:, pl.ds(q, 1), :]

        total = lax.fori_loop(0, 16, late, total, unroll=True)
        return jnp.concatenate([total[0], total[1]], axis=1)

    value = source[1]
    value = phi(0, 0, value, (1, 0, 3)) + source[2]
    value = phi(0, 1, value, (1, 3, 6)) + source[3]
    value = phi(0, 0, value, (1, 6, 8))

    @pl.when(d < tm_size - 1)
    def _():
        ahead.wait_recv()

    @pl.when(d > 0)
    def _():
        ahead.wait_send()

    r_all[j] = value + next_source[...]
    shares = [pltpu.make_async_remote_copy(r_all.at[j], r_all.at[j], r_send.at[i], r_recv.at[j],
                                           device_id=(peer, k), device_id_type=MESH)
              for i, peer in enumerate(peers)]
    for share in shares:
        share.start()

    def share_arrived(i):
        @pl.when(j != i)
        def _():
            pltpu.make_async_remote_copy(r_all.at[i], r_all.at[i], r_send.at[0], r_recv.at[i],
                                         device_id=(peers[0], k), device_id_type=MESH).wait_recv()

    prepare(2, 0, 8)
    first = phi(2, 1, initial[...])
    share_arrived(0)
    value = phi(1, 0, r_all[0])
    share_arrived(1)
    value = phi(1, 1, value + r_all[1])
    share_arrived(2)
    value = phi(1, 0, value + r_all[2])
    share_arrived(3)
    s_all[m] = value + r_all[3] + jnp.where(m == 0, first, 0.0)

    onward = {t: pltpu.make_async_remote_copy(
        s_all.at[m], s_all.at[m], s_send.at[t], s_recv.at[m],
        device_id=(jnp.where(m < t, 4 * t + j, lax.rem(d + 4, tm_size)), k), device_id_type=MESH)
        for t in range(groups - 1, 0, -1)}
    for t, copy in onward.items():
        @pl.when(m < t)
        def _(copy=copy):
            copy.start()

    for share in shares:
        share.wait_send()

    def s_arrived(i):
        pltpu.make_async_remote_copy(s_all.at[i], s_all.at[i], s_send.at[0], s_recv.at[i],
                                     device_id=(lax.rem(d + 4, tm_size), k),
                                     device_id_type=MESH).wait_recv()

    @pl.when(m == 0)
    def _():
        w_in[...] = initial[...]

    @pl.when(m > 0)
    def _():
        s_arrived(0)
        w_in[...] = s_all[0]

    def coarse(i, carry):
        moved = phi(2, 2 + lax.rem(i, 2), w_in[...])
        s_arrived(i)
        w_in[...] = moved + s_all[i]
        return carry

    lax.fori_loop(1, m, coarse, 0)

    value = w_in[...]
    for i in (1, 2, 3):
        moved = phi(1, i % 2, value) + r_all[i - 1]
        value = jnp.where(j >= i, moved, value)
    out[0] = value
    for i in (1, 2, 3):
        value = phi(0, (i + 1) % 2, value) + source[i]
        out[i] = value

    for t, copy in onward.items():
        @pl.when(m < t)
        def _(copy=copy):
            copy.wait_send()


def pair_kernel(tm_size, source_in, initial_in, mass_in, inverses, couplings_in, neighbours_in, sends_in,
                out, source, initial, mass, couplings, neighbours, sends, in_sem, packed, inv, gout, ginv, tables, state, rhs, change, grhs, picks, listed, rows,
                start_out, start_in, gmass, next_source, r_all, rg_out, rg_all, first, w_in, wg_in,
                s_all, sg_out, sg_all, fresh_out, fresh_in,
                inv_sem, gi_send, gi_recv, st_send, st_recv, src_send, src_recv,
                r_send, r_recv, rg_send, rg_recv, s_send, s_recv, sg_send, sg_recv, fr_send, fr_recv):
    f32, bf16, i32 = jnp.float32, jnp.bfloat16, jnp.int32
    d = lax.axis_index("tm")
    k = lax.axis_index("space")
    j = lax.rem(d, 4)
    m = lax.div(d, 4)
    groups = tm_size // 4
    other = 1 - k
    upper = k == 0
    peers = [4 * m + j + 1 - 2 * lax.rem(j, 2), 4 * m + lax.rem(j + 2, 4), 4 * m + 3 - j]

    loads = [pltpu.make_async_copy(inverses.at[l], packed.at[l], inv_sem.at[l]) for l in range(3)]
    fetches = [pltpu.make_async_copy(src, dst, in_sem.at[x]) for x, (src, dst) in enumerate([
        (neighbours_in, neighbours), (sends_in, sends), (source_in, source), (initial_in, initial),
        (mass_in, mass), (couplings_in, couplings)])]
    for copy in [*fetches[:2], fetches[5], loads[0], *fetches[2:5]]:
        copy.start()

    barrier = pltpu.get_barrier_semaphore()

    def greet(t, s):
        pl.semaphore_signal(barrier, inc=1, device_id=(t, s), device_id_type=MESH)

    greet(d, other)
    for peer in peers:
        greet(peer, k)
        greet(peer, other)

    @pl.when(d > 0)
    def _():
        greet(d - 1, k)

    @pl.when(d < tm_size - 1)
    def _():
        greet(d + 1, k)

    for t in range(groups):
        @pl.when(m != t)
        def _(t=t):
            greet(4 * t + j, k)
            greet(4 * t + j, other)

    r256 = lax.broadcasted_iota(i32, (256, 256), 0)
    c256 = lax.broadcasted_iota(i32, (256, 256), 1)
    swap = jnp.where((r256 >> 4 == (c256 & 15)) & ((r256 & 15) == c256 >> 4), 1.0, 0.0).astype(bf16)
    rows[...] = jnp.zeros((8, 128), i32)

    def split(x):
        top = x.astype(bf16)
        return top, (x - top.astype(f32)).astype(bf16)

    for fetch in [*fetches[:2], fetches[5]]:
        fetch.wait()

    lane = lax.broadcasted_iota(i32, (8, 128), 1)
    place, layer = lane & 15, lane >> 4
    nb = neighbours[...]
    begin = jnp.where(upper, 272, 256)
    spot = nb - begin
    picks[:, 0:256] = jnp.where(nb < 256, nb, jnp.where((spot >= 0) & (spot < 16), 256 + spot, 512))
    rows[0:2, 0:16] = sends[...]

    def both(row):
        return [jnp.broadcast_to(nb[row:row + 1, 128 * t:128 * t + 128], (8, 128)) for t in (0, 1)]

    def chosen(a, b):
        return [jnp.where(upper, x, y) for x, y in zip(a, b)]

    def among(pair, index):
        at = index & 127
        return jnp.where(index < 128, lane_take(pair[0], at), lane_take(pair[1], at))

    facing = chosen(both(1), both(0))
    inward = chosen(both(0), both(1))
    ends = jnp.where(upper, jnp.broadcast_to(rows[1:2, :], (8, 128)), jnp.broadcast_to(rows[0:1, :], (8, 128)))
    edge = lane_take(ends, place)
    deeper = among(inward, edge)
    deepest = among(inward, jnp.minimum(deeper, 255))
    listed[...] = jnp.where(layer == 0, edge, jnp.where(layer == 1, deeper, jnp.where(layer == 2, deepest, 512)))
    twice = jnp.where((lane & 31) < 16, edge, deeper)

    n = lax.broadcasted_iota(i32, (64, 96), 0)
    col = lax.broadcasted_iota(i32, (64, 96), 1)
    a, b, c = n & 3, (n >> 2) & 3, n >> 4
    face, point = col >> 4, col & 15
    axis = face >> 1
    fixed = jnp.where(axis == 0, a, jnp.where(axis == 1, b, c))
    where = jnp.where(axis == 0, b + 4 * c, jnp.where(axis == 1, a + 4 * c, a + 4 * b))
    lift = ((fixed == 3 * (face & 1)) & (where == point)).astype(f32).astype(bf16)
    spread = (lax.broadcasted_iota(i32, (16, 96), 0)
              == (lax.broadcasted_iota(i32, (16, 96), 1) & 15)).astype(f32).astype(bf16)
    same = (lax.broadcasted_iota(i32, (96, 96), 0) >> 4
            == lax.broadcasted_iota(i32, (96, 96), 1) >> 4)

    blocks = [x for l in range(3) for x in split(couplings[l])]
    wide = jnp.dot(jnp.concatenate(blocks, axis=0), spread, preferred_element_type=f32)
    wide = jnp.concatenate([jnp.where(same, wide[96 * x:96 * x + 96], 0.0) for x in range(6)], axis=1)
    lifted = jnp.dot(lift, wide.astype(bf16), preferred_element_type=f32).astype(bf16)
    for l in range(3):
        for x in (0, 1):
            half = lifted[:, 96 * (2 * l + x):96 * (2 * l + x) + 96]
            tables[l, 64 * x:64 * x + 64, :] = jnp.concatenate([half, half], axis=1)

    def low_half(shape):
        return lax.broadcasted_iota(i32, shape, 1) < 64

    def boundary(x):
        index = jnp.concatenate([listed[...]] * 8, axis=0)
        at, part = index & 127, index >> 7
        g = jnp.where(part == 0, lane_take(x[:, :128], at), jnp.where(part == 1, lane_take(x[:, 128:], at), 0.0))
        return jnp.where(low_half((32, 128)), g[:32], pltpu.roll(g[32:], 64, 1))

    def opened(p):
        return jnp.concatenate([p, pltpu.roll(p, 64, 1)], axis=0)

    def times(table, x):
        pair = jnp.dot(table, jnp.concatenate(split(x), axis=0), preferred_element_type=f32)
        half = pair.shape[0] // 2
        return pair[:half] + pair[half:]

    def tile16(level, bi, bj):
        return jnp.concatenate(
            [packed[level, 16 * bi + i, 16 * bj:16 * bj + 16, :] for i in range(16)], axis=0)

    element = lax.broadcasted_iota(i32, (256, 128), 0)
    quarter = lax.broadcasted_iota(i32, (256, 128), 1) >> 5
    hit = element == jnp.concatenate([twice] * 32, axis=0)
    spots = jnp.concatenate([jnp.where(hit & (quarter == q), 1.0, 0.0).astype(bf16) for q in range(4)], axis=0)

    def prepare_ghost(level):
        for pair in (0, 2):
            taken = jnp.concatenate([
                jnp.dot(jnp.concatenate([tile16(level, bi, bj) for bj in range(4)], axis=1), spots,
                        preferred_element_type=f32).astype(bf16) for bi in (pair, pair + 1)], axis=1)
            turned = jnp.dot(swap, taken, preferred_element_type=f32)
            for jj in range(16):
                for x in (0, 1):
                    gout[level, pair + x, jj] = turned[16 * jj:16 * jj + 16, 128 * x:128 * x + 128]

    def prepare(level):
        for bi in range(4):
            for bj in range(4):
                turned = jnp.dot(swap, tile16(level, bi, bj), preferred_element_type=f32)
                for jj in range(16):
                    for tile in (0, 1):
                        inv[level, 16 * bj + jj, tile, 16 * bi:16 * bi + 16, :] = turned[
                            16 * jj:16 * jj + 16, 128 * tile:128 * tile + 128]

    for fetch in fetches[2:5]:
        fetch.wait()
    for i in range(3):
        start_out[i] = boundary(source[i + 1])
    start_out[3] = boundary(initial[...])
    start_out[4] = boundary(mass[...])

    loads[0].wait()
    for load in loads[1:]:
        load.start()
    prepare_ghost(0)
    pl.semaphore_wait(
        barrier,
        7 + 2 * (groups - 1) + (d > 0).astype(i32) + (d < tm_size - 1).astype(i32))

    def beside_copy(src, dst, send, recv):
        return pltpu.make_async_remote_copy(src, dst, send, recv, device_id=(d, other), device_id_type=MESH)

    began = beside_copy(start_out, start_in, st_send, st_recv)
    began.start()
    ghosts = [[beside_copy(gout.at[l, x], ginv.at[l, x], gi_send.at[l, x], gi_recv.at[l, x])
               for x in range(4)] for l in range(3)]
    for copy in ghosts[0]:
        copy.start()

    forth = jnp.where(d > 0, d - 1, 1)
    ahead = pltpu.make_async_remote_copy(source.at[0], next_source, src_send, src_recv,
                                         device_id=(forth, k), device_id_type=MESH)

    @pl.when(d > 0)
    def _():
        ahead.start()

    @pl.when(d == tm_size - 1)
    def _():
        next_source[...] = jnp.zeros_like(next_source)

    prepare(0)
    meets = among(facing, edge) - begin
    beside = jnp.zeros((8, 128), i32)
    for p in range(16):
        at = jnp.full((8, 128), p, i32)
        beside = jnp.where(place == lane_take(meets, at), lane_take(edge, at), beside)
    for f in range(2, 6):
        step = among(both(f), beside)
        onto = among(facing, jnp.minimum(step, 255)) - begin
        picks[f:f + 1, 256:384] = jnp.where((step < 256) & (layer < 3), 256 + 16 * layer + (onto & 15), 512)[0:1]
    toward = jnp.where(layer == 0, beside, jnp.where(layer < 3, 240 + lane, 512))
    away = jnp.where(layer < 2, 272 + lane, 512)
    picks[0:1, 256:384] = jnp.where(upper, toward, away)[0:1]
    picks[1:2, 256:384] = jnp.where(upper, away, toward)[0:1]

    began.wait_recv()
    gmass[...] = opened(start_in[4])

    def across(begin, tiles):
        return jnp.concatenate([state[tile, pl.ds(begin, 16, 4), :] for tile in range(tiles)], axis=1)

    once = jnp.minimum(d + 1, 1)

    def sides(x):
        return [jnp.concatenate([x[16 * q:16 * q + 4, :] for q in range(4)], axis=0),
                jnp.concatenate([x[16 * q + 12:16 * q + 16, :] for q in range(4)], axis=0),
                x[0:16, :], x[48:64, :]]

    def gather(block, f, tile, origins):
        index = jnp.broadcast_to(picks[f:f + 1, 128 * tile:128 * tile + 128], (8, 128))
        at, part = index & 127, index >> 7
        at = jnp.concatenate([at, at], axis=0)
        part = jnp.concatenate([part, part], axis=0)
        found = jnp.zeros((16, 128), f32)
        for origin in origins:
            found = jnp.where(part == origin, lane_take(block(origin), at), found)
        return found

    def columns(block):
        return lambda origin: block[:, 128 * origin:128 * origin + 128]

    def ghost_sum(level, total):
        for at in range(16):
            total = total + ginv[level, :, at] * grhs[pl.ds(at, 1), :][None]
        total = total.reshape(64, 128)
        total = total + pltpu.roll(total, 64, 1)
        return (total + pltpu.roll(total, 32, 1)).reshape(4, 16, 128)

    def own_sum(level, total):
        for at in range(64):
            total = total + inv[level, at] * rhs[:, pl.ds(at, 1), :]
        return total

    def alone(step, total):
        return lax.fori_loop(0, once, lambda _, x: step(x), total)

    def together(first_step, second_step, total):
        total, gsum = lax.fori_loop(
            0, once, lambda _, x: (first_step(x[0]), second_step(x[1])), (total, jnp.zeros((4, 16, 128), f32)))
        return total, gsum.reshape(64, 128)

    def ghost_rhs(ghost, coupled):
        known = gmass[...] * ghost - coupled
        which = lax.broadcasted_iota(i32, (16, 128), 1) >> 5
        dense = known[0:16]
        for q in (1, 2, 3):
            dense = jnp.where(which == q, pltpu.roll(known[16 * q:16 * q + 16], 32 * q, 1), dense)
        grhs[...] = dense

    def ghost_step(level):
        return alone(functools.partial(ghost_sum, level), jnp.zeros((4, 16, 128), f32)).reshape(64, 128)

    def keep(x, tiles):
        for tile in tiles:
            state[tile] = x[:, 128 * (tile - tiles[0]):128 * (tile - tiles[0]) + 128]

    def phi(level, value, ghost, more, awaited=()):
        tiles = 3 if more else 2
        keep(value, (0, 1))
        state[2] = ghost
        whole = jnp.concatenate([value, ghost], axis=1) if more else value
        faces = [across(0, 3), across(3, 3), *sides(whole)]
        picked = jnp.concatenate([jnp.concatenate([
            gather(columns(faces[f ^ 1]), f, tile, (0, 1, 2) if f < 2 else (0, 1) if tile < 2 else (2,))
            for tile in range(tiles)], axis=1) for f in range(6)], axis=0)
        coupled = times(tables[level], picked)
        known = mass[...] * value - coupled[:, :256]
        for tile in (0, 1):
            rhs[tile] = known[:, 128 * tile:128 * tile + 128]
        if more:
            ghost_rhs(ghost, coupled[:, 256:])
        own = functools.partial(own_sum, level)
        if more and not awaited:
            total, gsum = together(own, functools.partial(ghost_sum, level), jnp.zeros((2, 64, 128), f32))
            return jnp.concatenate([total[0], total[1]], axis=1), gsum
        total = alone(own, jnp.zeros((2, 64, 128), f32))
        result = jnp.concatenate([total[0], total[1]], axis=1)
        if not more:
            return result, ghost
        for copy in awaited:
            copy.wait_recv()
        return result, ghost_step(level)

    def phi_fresh(level, value, slot):
        fresh_out[slot] = boundary(value)
        copy = beside_copy(fresh_out.at[slot], fresh_in.at[slot], fr_send.at[slot], fr_recv.at[slot])
        copy.start()
        keep(value, (0, 1))
        faces = [across(0, 2), across(3, 2), *sides(value)]
        picked = jnp.concatenate([jnp.concatenate([
            gather(columns(faces[f ^ 1]), f, tile, (0, 1)) for tile in (0, 1)], axis=1)
            for f in range(6)], axis=0)
        known = mass[...] * value - times(tables[level], picked)
        for tile in (0, 1):
            rhs[tile] = known[:, 128 * tile:128 * tile + 128]
        total = alone(functools.partial(own_sum, level), jnp.zeros((2, 64, 128), f32))
        copy.wait()
        ghost = opened(fresh_in[slot])
        state[2] = ghost
        ends = [state[2, pl.ds(0, 16, 4), :], state[2, pl.ds(3, 16, 4), :]]
        near = [across(0, 2), across(3, 2)]
        beyond = sides(ghost)
        nothing = jnp.zeros((16, 256), f32)
        rows_of = []
        for f in range(6):
            if f < 2:
                def source_of(origin, f=f):
                    return ends[f ^ 1] if origin == 2 else columns(near[f ^ 1])(origin)
                rows_of.append(jnp.concatenate(
                    [gather(source_of, f, 0, (2,)), gather(source_of, f, 1, (2,)),
                     gather(source_of, f, 2, (0, 1, 2))], axis=1))
            else:
                rows_of.append(jnp.concatenate(
                    [nothing, gather(lambda _, f=f: beyond[(f ^ 1) - 2], f, 2, (2,))], axis=1))
        coupled = times(tables[level], jnp.concatenate(rows_of, axis=0))
        ghost_rhs(ghost, coupled[:, 256:])
        for tile in (0, 1):
            state[tile] = coupled[:, 128 * tile:128 * tile + 128]
            change[tile] = jnp.where(upper, state[tile, pl.ds(3, 16, 4), :], state[tile, pl.ds(0, 16, 4), :])
        offset = 3 - 3 * k

        def corrected(total):
            for q in range(16):
                total = total - inv[level, 4 * q + offset] * change[:, pl.ds(q, 1), :]
            return total

        total, gsum = together(corrected, functools.partial(ghost_sum, level), total)
        return jnp.concatenate([total[0], total[1]], axis=1), gsum, ghost

    value, ghost = source[1], opened(start_in[0])
    for i in (2, 3):
        value, ghost = phi(0, value, ghost, True, ghosts[0] if i == 2 else ())
        value, ghost = value + source[i], ghost + opened(start_in[i - 1])
    value, _ = phi(0, value, ghost, False)

    @pl.when(d < tm_size - 1)
    def _():
        ahead.wait_recv()

    @pl.when(d > 0)
    def _():
        ahead.wait_send()

    value = value + next_source[...]
    r_all[j] = value
    rg_out[...] = boundary(value)
    edges_out = [pltpu.make_async_remote_copy(rg_out, rg_all.at[j], rg_send.at[i], rg_recv.at[j],
                                              device_id=(peer, other), device_id_type=MESH)
                 for i, peer in enumerate([*peers, d])]
    shares = [pltpu.make_async_remote_copy(r_all.at[j], r_all.at[j], r_send.at[i], r_recv.at[j],
                                           device_id=(peer, k), device_id_type=MESH)
              for i, peer in enumerate(peers)]

    @pl.when(j < 3)
    def _():
        for copy in edges_out:
            copy.start()

    for share in shares:
        share.start()

    loads[1].wait()
    prepare_ghost(1)
    for copy in ghosts[1]:
        copy.start()
    prepare(1)
    loads[2].wait()
    prepare(2)
    first[...] = phi(2, initial[...], opened(start_in[3]), False)[0]

    def share_arrived(i):
        if i < 3:
            pltpu.make_async_remote_copy(rg_out, rg_all.at[i], rg_send.at[0], rg_recv.at[i],
                                         device_id=(d, other), device_id_type=MESH).wait_recv()

        @pl.when(j != i)
        def _():
            pltpu.make_async_remote_copy(r_all.at[i], r_all.at[i], r_send.at[0], r_recv.at[i],
                                         device_id=(peers[0], k), device_id_type=MESH).wait_recv()

    share_arrived(0)
    value, ghost = r_all[0], opened(rg_all[0])
    for i in (1, 2):
        value, ghost = phi(1, value, ghost, True, ghosts[1] if i == 1 else ())
        share_arrived(i)
        value, ghost = value + r_all[i], ghost + opened(rg_all[i])
    value, _ = phi(1, value, ghost, False)
    share_arrived(3)
    value = value + r_all[3] + jnp.where(m == 0, first[...], 0.0)
    s_all[m] = value
    sg_out[...] = boundary(value)

    onward = []
    for t in range(groups - 1, 0, -1):
        target = jnp.where(m < t, 4 * t + j, lax.rem(d + 4, tm_size))
        own = pltpu.make_async_remote_copy(
            s_all.at[m], s_all.at[m], s_send.at[t], s_recv.at[m],
            device_id=(target, k), device_id_type=MESH)
        edge_out = pltpu.make_async_remote_copy(
            sg_out, sg_all.at[m], sg_send.at[t], sg_recv.at[m],
            device_id=(target, other), device_id_type=MESH)
        onward += [(m < t - 1, edge_out), (m < t, own)]

        @pl.when(m < t - 1)
        def _(edge_out=edge_out):
            edge_out.start()

        @pl.when(m < t)
        def _(own=own):
            own.start()

    @pl.when(j < 3)
    def _():
        for copy in edges_out:
            copy.wait_send()

    for share in shares:
        share.wait_send()

    def s_arrived(i):
        pltpu.make_async_remote_copy(s_all.at[i], s_all.at[i], s_send.at[0], s_recv.at[i],
                                     device_id=(lax.rem(d + 4, tm_size), k),
                                     device_id_type=MESH).wait_recv()

    prepare_ghost(2)
    for copy in ghosts[2]:
        copy.start()

    def s_edge_arrived(i):
        pltpu.make_async_remote_copy(sg_out, sg_all.at[i], sg_send.at[0], sg_recv.at[i],
                                     device_id=(lax.rem(d + 4, tm_size), other),
                                     device_id_type=MESH).wait_recv()

    for copy in ghosts[2]:
        copy.wait_recv()

    @pl.when(m == 0)
    def _():
        w_in[...] = initial[...]

    @pl.when(m > 0)
    def _():
        s_arrived(0)
        w_in[...] = s_all[0]

    @pl.when(m > 1)
    def _():
        s_edge_arrived(0)
        wg_in[...] = opened(sg_all[0])

    for i in range(1, groups - 1):
        @pl.when(i < m)
        def _(i=i):
            if i > 1 and i % 3 == 1:
                value, ghost, _ = phi_fresh(2, w_in[...], 1 + i)
            else:
                value, ghost = phi(2, w_in[...], wg_in[...], True)
            s_arrived(i)
            w_in[...] = value + s_all[i]

            @pl.when(i < m - 1)
            def _():
                s_edge_arrived(i)
                wg_in[...] = ghost + opened(sg_all[i])

    value = w_in[...]
    for i in (1, 2, 3):
        if i == 1:
            moved, gmoved, ghost = phi_fresh(1, value, 0)
        else:
            moved, gmoved = phi(1, value, ghost, i < 3)
        value = jnp.where(j >= i, moved + r_all[i - 1], value)
        if i < 3:
            ghost = jnp.where(j >= i, gmoved + opened(rg_all[i - 1]), ghost)
    out[0] = value
    for i in (1, 2, 3):
        if i == 1:
            value, ghost, _ = phi_fresh(0, value, 1)
        else:
            value, ghost = phi(0, value, ghost, i < 3)
        value = value + source[i]
        if i < 3:
            ghost = ghost + opened(start_in[i - 1])
        out[i] = value

    for sent, copy in onward:
        @pl.when(sent)
        def _(copy=copy):
            copy.wait_send()
    began.wait_send()
    for level in ghosts:
        for copy in level:
            copy.wait_send()


def pair_local(tm_size, source, initial, mass, inverses, couplings, neighbours, sends):
    f32, bf16, i32 = jnp.float32, jnp.bfloat16, jnp.int32
    vmem = pl.BlockSpec(memory_space=pltpu.VMEM)
    dma = pltpu.SemaphoreType.DMA
    groups = tm_size // 4
    return pl.pallas_call(
        functools.partial(pair_kernel, tm_size),
        out_shape=jax.ShapeDtypeStruct(source.shape, f32),
        in_specs=[pl.BlockSpec(memory_space=pltpu.MemorySpace.HBM)] * 7,
        out_specs=vmem,
        scratch_shapes=[
            pltpu.VMEM(source.shape, f32),
            pltpu.VMEM(initial.shape, f32),
            pltpu.VMEM(mass.shape, f32),
            pltpu.VMEM((3, 96, 16), f32),
            pltpu.VMEM(neighbours.shape, i32),
            pltpu.VMEM(sends.shape, i32),
            dma((6,)),
            pltpu.VMEM(inverses.shape, bf16),
            pltpu.VMEM((3, 64, 2, 64, 128), f32),
            pltpu.VMEM((3, 4, 16, 16, 128), f32),
            pltpu.VMEM((3, 4, 16, 16, 128), f32),
            pltpu.VMEM((3, 128, 192), bf16),
            pltpu.VMEM((3, 64, 128), f32),
            pltpu.VMEM((2, 64, 128), f32),
            pltpu.VMEM((2, 16, 128), f32),
            pltpu.VMEM((16, 128), f32),
            pltpu.VMEM((6, 384), i32),
            pltpu.VMEM((8, 128), i32),
            pltpu.VMEM((8, 128), i32),
            pltpu.VMEM((5, 32, 128), f32),
            pltpu.VMEM((5, 32, 128), f32),
            pltpu.VMEM((64, 128), f32),
            pltpu.VMEM((64, 256), f32),
            pltpu.VMEM((4, 64, 256), f32),
            pltpu.VMEM((32, 128), f32),
            pltpu.VMEM((4, 32, 128), f32),
            pltpu.VMEM((64, 256), f32),
            pltpu.VMEM((64, 256), f32),
            pltpu.VMEM((64, 128), f32),
            pltpu.VMEM((groups, 64, 256), f32),
            pltpu.VMEM((32, 128), f32),
            pltpu.VMEM((groups, 32, 128), f32),
            pltpu.VMEM((max(2, groups), 32, 128), f32),
            pltpu.VMEM((max(2, groups), 32, 128), f32),
            dma((3,)), dma((3, 4)), dma((3, 4)), dma, dma, dma, dma,
            dma((3,)), dma((4,)), dma((4,)), dma((4,)),
            dma((groups,)), dma((groups,)), dma((groups,)), dma((groups,)),
            dma((max(2, groups),)), dma((max(2, groups),)),
        ],
        compiler_params=pltpu.CompilerParams(collective_id=0, has_side_effects=True,
                                             vmem_limit_bytes=48 << 20),
        name="cycle",
    )(*[pltpu.with_memory_space_constraint(x, pltpu.MemorySpace.HBM) for x in (source, initial, mass, inverses, couplings.reshape(3, 96, 16), neighbours, sends)])


def local(tm_size, space_size, source, initial, mass, inverses, couplings, neighbours, sends):
    f32 = jnp.float32
    vmem = pl.BlockSpec(memory_space=pltpu.VMEM)
    dma = pltpu.SemaphoreType.DMA
    return pl.pallas_call(
        functools.partial(kernel, tm_size, space_size),
        out_shape=jax.ShapeDtypeStruct(source.shape, f32),
        in_specs=[vmem, vmem, vmem, pl.BlockSpec(memory_space=pl.ANY), vmem, vmem, vmem],
        out_specs=vmem,
        scratch_shapes=[
            pltpu.VMEM(inverses.shape, jnp.bfloat16),
            pltpu.VMEM((2, 576, 128), f32),
            pltpu.VMEM((3, 64, 2, 64, 128), f32),
            pltpu.VMEM((3, 128, 192), jnp.bfloat16),
            pltpu.VMEM((3, 64, 64), jnp.bfloat16),
            pltpu.VMEM((2, 64, 128), f32),
            pltpu.VMEM((4, 2, 16, 256), f32),
            pltpu.VMEM((4, 2, 16, 256), f32),
            pltpu.VMEM((2, 64, 128), f32),
            pltpu.VMEM((2, 16, 128), f32),
            pltpu.VMEM((2, 16, 128), f32),
            pltpu.VMEM((3, 8, 128), jnp.int32),
            pltpu.VMEM((6, 256), jnp.int32),
            pltpu.VMEM((2, 8, 256), jnp.int32),
            pltpu.VMEM((64, 256), f32),
            pltpu.VMEM((4, 64, 256), f32),
            pltpu.VMEM((64, 256), f32),
            pltpu.VMEM((tm_size // 4, 64, 256), f32),
            dma((3,)), dma((4, 2)), dma((4, 2)), dma((2,)), dma((2,)), dma, dma,
            dma((3,)), dma((4,)), dma((tm_size // 4,)), dma((tm_size // 4,)),
        ],
        compiler_params=pltpu.CompilerParams(collective_id=0, has_side_effects=True),
        name="cycle",
    )(source, initial, mass, inverses, couplings.reshape(3, 96, 16), neighbours, sends)


def solution(mesh):
    placed = (
        P("tm", None, "space"),
        P(None, "space"),
        P(None, "space"),
        P(None, None, None, "space"),
        P(),
        P(None, "space"),
        P(None, "space"),
    )
    body = (functools.partial(pair_local, mesh.shape["tm"]) if mesh.shape["space"] == 2
            else functools.partial(local, mesh.shape["tm"], mesh.shape["space"]))
    return jax.shard_map(
        body,
        mesh=mesh, in_specs=placed, out_specs=P("tm", None, "space"), check_vma=False)
```

```python
import functools
import jax
import jax.numpy as jnp
from jax import lax
from jax.experimental import pallas as pl
from jax.experimental.pallas import tpu as pltpu
from jax.sharding import PartitionSpec as P

MESH = pl.DeviceIdType.MESH
HI = lax.Precision.HIGHEST


def lane_take(block, index):
    return jnp.take_along_axis(block, index, axis=1, mode="promise_in_bounds")


def kernel(tm_size, space_size, source, initial, mass, inverses, couplings, neighbours, sends,
           out, packed, stage, inv, tables, edges, state, traces, halo, rhs, low, high, slots, picks, where_halo,
           next_source, r_all, w_in, s_all,
           inv_sem, halo_send, halo_recv, slot_send, slot_recv, src_send, src_recv,
           r_send, r_recv, s_send, s_recv):
    f32 = jnp.float32
    d = lax.axis_index("tm")
    k = lax.axis_index("space")
    j = lax.rem(d, 4)
    m = lax.div(d, 4)
    groups = tm_size // 4
    above = lax.rem(k + 1, space_size)
    below = lax.rem(k + space_size - 1, space_size)
    peers = [4 * m + lax.rem(j + step, 4) for step in (1, 2, 3)]

    loads = [pltpu.make_async_copy(inverses.at[l], packed.at[l], inv_sem.at[l]) for l in range(3)]
    loads[0].start()
    loads[1].start()
    loads[2].start()

    barrier = pltpu.get_barrier_semaphore()

    def greet(t, s):
        pl.semaphore_signal(barrier, inc=1, device_id=(t, s), device_id_type=MESH)

    greet(d, above)
    greet(d, below)
    for peer in peers:
        greet(peer, k)

    @pl.when(d > 0)
    def _():
        greet(d - 1, k)

    @pl.when(d < tm_size - 1)
    def _():
        greet(d + 1, k)

    for t in range(groups):
        @pl.when(m != t)
        def _(t=t):
            greet(4 * t + j, k)

    slots[0] = jnp.zeros((8, 128), jnp.int32)
    slots[0, 0:2, 0:16] = sends[...]

    n = lax.broadcasted_iota(jnp.int32, (64, 96), 0)
    col = lax.broadcasted_iota(jnp.int32, (64, 96), 1)
    a, b, c = n & 3, (n >> 2) & 3, n >> 4
    face, point = col >> 4, col & 15
    axis = face >> 1
    fixed = jnp.where(axis == 0, a, jnp.where(axis == 1, b, c))
    place = jnp.where(axis == 0, b + 4 * c, jnp.where(axis == 1, a + 4 * c, a + 4 * b))
    lift = ((fixed == 3 * (face & 1)) & (place == point)).astype(f32)
    spread = (lax.broadcasted_iota(jnp.int32, (16, 96), 0)
              == (lax.broadcasted_iota(jnp.int32, (16, 96), 1) & 15)).astype(f32)
    same = (lax.broadcasted_iota(jnp.int32, (96, 96), 0) >> 4
            == lax.broadcasted_iota(jnp.int32, (96, 96), 1) >> 4)

    def split(x):
        top = x.astype(jnp.bfloat16)
        return top, (x - top.astype(f32)).astype(jnp.bfloat16)

    def stacked(x):
        top, rest = split(x)
        return jnp.concatenate([jnp.concatenate([top, top], axis=1),
                                jnp.concatenate([rest, rest], axis=1)], axis=0)

    def times(table, x):
        both = jnp.dot(table, jnp.concatenate(split(x), axis=0), preferred_element_type=f32)
        half = both.shape[0] // 2
        return both[:half] + both[half:]

    for l in range(3):
        wide = jnp.dot(couplings[l], spread, precision=HI, preferred_element_type=f32)
        tables[l] = stacked(jnp.dot(lift, jnp.where(same, wide, 0.0), precision=HI,
                                    preferred_element_type=f32))
        edges[l] = stacked(jnp.where(same, wide, 0.0)[:32, :32])

    def prepare(level, begin, end):
        def block(part, carry):
            for i in range(8):
                whole = packed[level, 8 * part + i].astype(f32)
                for tile in (0, 1):
                    stage[tile, 72 * i:72 * i + 64, :] = whole[:, 128 * tile:128 * tile + 128]
            rows = pl.ds(pl.multiple_of(8 * part, 8), 8)
            for at in range(64):
                for tile in (0, 1):
                    inv[level, at, tile, rows, :] = stage[tile, pl.ds(at, 8, 72), :]
            return carry

        lax.fori_loop(begin, end, block, 0)

    nb = neighbours[...]
    picks[...] = jnp.where(nb < 256, nb, 512)

    loads[0].wait()
    prepare(0, 0, 3)

    pl.semaphore_wait(
        barrier,
        4 + groups + (d > 0).astype(jnp.int32) + (d < tm_size - 1).astype(jnp.int32))

    lists = [
        pltpu.make_async_remote_copy(slots.at[0], slots.at[1], slot_send.at[0], slot_recv.at[0],
                                     device_id=(d, above), device_id_type=MESH),
        pltpu.make_async_remote_copy(slots.at[0], slots.at[2], slot_send.at[1], slot_recv.at[1],
                                     device_id=(d, below), device_id_type=MESH)]
    for copy in lists:
        copy.start()

    back = jnp.maximum(d - 1, 0)
    forth = jnp.where(d > 0, d - 1, 1)
    ahead = pltpu.make_async_remote_copy(source.at[0], next_source, src_send, src_recv,
                                         device_id=(forth, k), device_id_type=MESH)

    @pl.when(d > 0)
    def _():
        ahead.start()

    @pl.when(d == tm_size - 1)
    def _():
        next_source[...] = jnp.zeros_like(next_source)

    prepare(0, 3, 8)
    loads[1].wait()
    loads[2].wait()
    for copy in lists:
        copy.wait()
    for row, (held, line, begin, exists) in enumerate(
            [(1, 1, 256, k > 0), (2, 0, 272, k < space_size - 1)]):
        for tile in (0, 1):
            lanes = pl.ds(128 * tile, 128)
            entry = jnp.broadcast_to(neighbours[row:row + 1, lanes], (8, 128)) - begin
            listed = jnp.broadcast_to(slots[held, line:line + 1, :], (8, 128))
            taken = lane_take(listed, jnp.clip(entry, 0, 15))
            limit = jnp.where(exists, 16, 0)
            valid = (entry >= 0) & (entry < limit)
            where_halo[row, :, lanes] = jnp.where(valid, taken, 512)

    def take_from(block, index_of):
        halves = []
        for tile in (0, 1):
            index = index_of(tile)
            spot = index & 127
            part = index >> 7
            halves.append(jnp.where(part == 0, lane_take(block[:, :128], spot),
                                    jnp.where(part == 1, lane_take(block[:, 128:], spot), 0.0)))
        return jnp.concatenate(halves, axis=1)

    def across(ref, begin, size, stride=None):
        return jnp.concatenate([ref[tile, pl.ds(begin, size, stride), :] for tile in (0, 1)], axis=1)

    def phi(level, slot, value, meanwhile=None):
        for tile in (0, 1):
            state[tile] = value[:, 128 * tile:128 * tile + 128]
        traces[slot, 0] = across(state, 0, 16, 4)
        traces[slot, 1] = across(state, 3, 16, 4)
        moves = [
            pltpu.make_async_remote_copy(traces.at[slot, 1], halo.at[slot, 0], halo_send.at[slot, 0],
                                         halo_recv.at[slot, 0], device_id=(d, above),
                                         device_id_type=MESH),
            pltpu.make_async_remote_copy(traces.at[slot, 0], halo.at[slot, 1], halo_send.at[slot, 1],
                                         halo_recv.at[slot, 1], device_id=(d, below),
                                         device_id_type=MESH)]
        for move in moves:
            move.start()
        faces = [
            traces[slot, 0], traces[slot, 1],
            jnp.concatenate([value[16 * q:16 * q + 4, :] for q in range(4)], axis=0),
            jnp.concatenate([value[16 * q + 12:16 * q + 16, :] for q in range(4)], axis=0),
            value[0:16, :], value[48:64, :]]
        picked = jnp.concatenate(
            [take_from(faces[f ^ 1], lambda tile, f=f: jnp.broadcast_to(
                picks[f:f + 1, 128 * tile:128 * tile + 128], (16, 128))) for f in range(6)], axis=0)
        coupled = times(tables[level], picked)
        known = mass[...] * value - coupled
        for tile in (0, 1):
            rhs[tile] = known[:, 128 * tile:128 * tile + 128]

        def early(q, total):
            for step in (1, 2):
                at = 4 * q + step
                total = total + inv[level, at] * rhs[:, pl.ds(at, 1), :]
            return total

        total = lax.fori_loop(0, 16, early, jnp.zeros((2, 64, 128), f32), unroll=True)
        if meanwhile is not None:
            prepare(*meanwhile)
        for move in moves:
            move.wait()
        got = jnp.concatenate(
            [take_from(halo[slot, row], lambda tile, row=row: jnp.concatenate(
                [where_halo[row, :, 128 * tile:128 * tile + 128]] * 2, axis=0))
             for row in (0, 1)], axis=0)
        change = times(edges[level], got)
        for row, kept, first in ((0, low, 0), (1, high, 3)):
            for tile in (0, 1):
                kept[tile] = (rhs[tile, pl.ds(first, 16, 4), :]
                              - change[16 * row:16 * row + 16, 128 * tile:128 * tile + 128])

        def late(q, total):
            total = total + inv[level, 4 * q] * low[:, pl.ds(q, 1), :]
            return total + inv[level, 4 * q + 3] * high[:, pl.ds(q, 1), :]

        total = lax.fori_loop(0, 16, late, total, unroll=True)
        return jnp.concatenate([total[0], total[1]], axis=1)

    value = source[1]
    value = phi(0, 0, value, (1, 0, 3)) + source[2]
    value = phi(0, 1, value, (1, 3, 6)) + source[3]
    value = phi(0, 0, value, (1, 6, 8))

    @pl.when(d < tm_size - 1)
    def _():
        ahead.wait_recv()

    @pl.when(d > 0)
    def _():
        ahead.wait_send()

    r_all[j] = value + next_source[...]
    shares = [pltpu.make_async_remote_copy(r_all.at[j], r_all.at[j], r_send.at[i], r_recv.at[j],
                                           device_id=(peer, k), device_id_type=MESH)
              for i, peer in enumerate(peers)]
    for share in shares:
        share.start()

    def share_arrived(i):
        @pl.when(j != i)
        def _():
            pltpu.make_async_remote_copy(r_all.at[i], r_all.at[i], r_send.at[0], r_recv.at[i],
                                         device_id=(peers[0], k), device_id_type=MESH).wait_recv()

    prepare(2, 0, 8)
    first = phi(2, 1, initial[...])
    share_arrived(0)
    value = phi(1, 0, r_all[0])
    share_arrived(1)
    value = phi(1, 1, value + r_all[1])
    share_arrived(2)
    value = phi(1, 0, value + r_all[2])
    share_arrived(3)
    s_all[m] = value + r_all[3] + jnp.where(m == 0, first, 0.0)

    onward = {t: pltpu.make_async_remote_copy(
        s_all.at[m], s_all.at[m], s_send.at[t], s_recv.at[m],
        device_id=(jnp.where(m < t, 4 * t + j, lax.rem(d + 4, tm_size)), k), device_id_type=MESH)
        for t in range(groups - 1, 0, -1)}
    for t, copy in onward.items():
        @pl.when(m < t)
        def _(copy=copy):
            copy.start()

    for share in shares:
        share.wait_send()

    def s_arrived(i):
        pltpu.make_async_remote_copy(s_all.at[i], s_all.at[i], s_send.at[0], s_recv.at[i],
                                     device_id=(lax.rem(d + 4, tm_size), k),
                                     device_id_type=MESH).wait_recv()

    @pl.when(m == 0)
    def _():
        w_in[...] = initial[...]

    @pl.when(m > 0)
    def _():
        s_arrived(0)
        w_in[...] = s_all[0]

    def coarse(i, carry):
        moved = phi(2, 2 + lax.rem(i, 2), w_in[...])
        s_arrived(i)
        w_in[...] = moved + s_all[i]
        return carry

    lax.fori_loop(1, m, coarse, 0)

    value = w_in[...]
    for i in (1, 2, 3):
        moved = phi(1, i % 2, value) + r_all[i - 1]
        value = jnp.where(j >= i, moved, value)
    out[0] = value
    for i in (1, 2, 3):
        value = phi(0, (i + 1) % 2, value) + source[i]
        out[i] = value

    for t, copy in onward.items():
        @pl.when(m < t)
        def _(copy=copy):
            copy.wait_send()


def pair_kernel(tm_size, source_in, initial_in, mass_in, inverses, couplings_in, neighbours_in, sends_in,
                out, source, initial, mass, couplings, neighbours, sends, in_sem, packed, inv, gout, ginv, tables, state, rhs, change, grhs, picks, listed, rows,
                start_out, start_in, gmass, next_source, r_all, rg_out, rg_all, first, w_in, wg_in,
                s_all, sg_out, sg_all, fresh_out, fresh_in,
                inv_sem, gi_send, gi_recv, st_send, st_recv, src_send, src_recv,
                r_send, r_recv, rg_send, rg_recv, s_send, s_recv, sg_send, sg_recv, fr_send, fr_recv):
    f32, bf16, i32 = jnp.float32, jnp.bfloat16, jnp.int32
    d = lax.axis_index("tm")
    k = lax.axis_index("space")
    j = lax.rem(d, 4)
    m = lax.div(d, 4)
    groups = tm_size // 4
    other = 1 - k
    upper = k == 0
    peers = [4 * m + j + 1 - 2 * lax.rem(j, 2), 4 * m + lax.rem(j + 2, 4), 4 * m + 3 - j]

    loads = [pltpu.make_async_copy(inverses.at[l], packed.at[l], inv_sem.at[l]) for l in range(3)]
    fetches = [pltpu.make_async_copy(src, dst, in_sem.at[x]) for x, (src, dst) in enumerate([
        (neighbours_in, neighbours), (sends_in, sends), (source_in, source), (initial_in, initial),
        (mass_in, mass), (couplings_in, couplings)])]
    for copy in [*fetches[:2], fetches[5], loads[0], *fetches[2:5]]:
        copy.start()

    barrier = pltpu.get_barrier_semaphore()

    def greet(t, s):
        pl.semaphore_signal(barrier, inc=1, device_id=(t, s), device_id_type=MESH)

    greet(d, other)
    for peer in peers:
        greet(peer, k)
        greet(peer, other)

    @pl.when(d > 0)
    def _():
        greet(d - 1, k)

    @pl.when(d < tm_size - 1)
    def _():
        greet(d + 1, k)

    for t in range(groups):
        @pl.when(m != t)
        def _(t=t):
            greet(4 * t + j, k)
            greet(4 * t + j, other)

    r256 = lax.broadcasted_iota(i32, (256, 256), 0)
    c256 = lax.broadcasted_iota(i32, (256, 256), 1)
    swap = jnp.where((r256 >> 4 == (c256 & 15)) & ((r256 & 15) == c256 >> 4), 1.0, 0.0).astype(bf16)
    rows[...] = jnp.zeros((8, 128), i32)

    def split(x):
        top = x.astype(bf16)
        return top, (x - top.astype(f32)).astype(bf16)

    for fetch in [*fetches[:2], fetches[5]]:
        fetch.wait()

    lane = lax.broadcasted_iota(i32, (8, 128), 1)
    place, layer = lane & 15, lane >> 4
    nb = neighbours[...]
    begin = jnp.where(upper, 272, 256)
    spot = nb - begin
    picks[:, 0:256] = jnp.where(nb < 256, nb, jnp.where((spot >= 0) & (spot < 16), 256 + spot, 512))
    rows[0:2, 0:16] = sends[...]

    def both(row):
        return [jnp.broadcast_to(nb[row:row + 1, 128 * t:128 * t + 128], (8, 128)) for t in (0, 1)]

    def chosen(a, b):
        return [jnp.where(upper, x, y) for x, y in zip(a, b)]

    def among(pair, index):
        at = index & 127
        return jnp.where(index < 128, lane_take(pair[0], at), lane_take(pair[1], at))

    facing = chosen(both(1), both(0))
    inward = chosen(both(0), both(1))
    ends = jnp.where(upper, jnp.broadcast_to(rows[1:2, :], (8, 128)), jnp.broadcast_to(rows[0:1, :], (8, 128)))
    edge = lane_take(ends, place)
    deeper = among(inward, edge)
    deepest = among(inward, jnp.minimum(deeper, 255))
    listed[...] = jnp.where(layer == 0, edge, jnp.where(layer == 1, deeper, jnp.where(layer == 2, deepest, 512)))
    twice = jnp.where((lane & 31) < 16, edge, deeper)

    n = lax.broadcasted_iota(i32, (64, 96), 0)
    col = lax.broadcasted_iota(i32, (64, 96), 1)
    a, b, c = n & 3, (n >> 2) & 3, n >> 4
    face, point = col >> 4, col & 15
    axis = face >> 1
    fixed = jnp.where(axis == 0, a, jnp.where(axis == 1, b, c))
    where = jnp.where(axis == 0, b + 4 * c, jnp.where(axis == 1, a + 4 * c, a + 4 * b))
    lift = ((fixed == 3 * (face & 1)) & (where == point)).astype(f32).astype(bf16)
    spread = (lax.broadcasted_iota(i32, (16, 96), 0)
              == (lax.broadcasted_iota(i32, (16, 96), 1) & 15)).astype(f32).astype(bf16)
    same = (lax.broadcasted_iota(i32, (96, 96), 0) >> 4
            == lax.broadcasted_iota(i32, (96, 96), 1) >> 4)

    blocks = [x for l in range(3) for x in split(couplings[l])]
    wide = jnp.dot(jnp.concatenate(blocks, axis=0), spread, preferred_element_type=f32)
    wide = jnp.concatenate([jnp.where(same, wide[96 * x:96 * x + 96], 0.0) for x in range(6)], axis=1)
    lifted = jnp.dot(lift, wide.astype(bf16), preferred_element_type=f32).astype(bf16)
    for l in range(3):
        for x in (0, 1):
            half = lifted[:, 96 * (2 * l + x):96 * (2 * l + x) + 96]
            tables[l, 64 * x:64 * x + 64, :] = jnp.concatenate([half, half], axis=1)

    def low_half(shape):
        return lax.broadcasted_iota(i32, shape, 1) < 64

    def boundary(x):
        index = jnp.concatenate([listed[...]] * 8, axis=0)
        at, part = index & 127, index >> 7
        g = jnp.where(part == 0, lane_take(x[:, :128], at), jnp.where(part == 1, lane_take(x[:, 128:], at), 0.0))
        return jnp.where(low_half((32, 128)), g[:32], pltpu.roll(g[32:], 64, 1))

    def opened(p):
        return jnp.concatenate([p, pltpu.roll(p, 64, 1)], axis=0)

    def times(table, x):
        pair = jnp.dot(table, jnp.concatenate(split(x), axis=0), preferred_element_type=f32)
        half = pair.shape[0] // 2
        return pair[:half] + pair[half:]

    def tile16(level, bi, bj):
        return jnp.concatenate(
            [packed[level, 16 * bi + i, 16 * bj:16 * bj + 16, :] for i in range(16)], axis=0)

    element = lax.broadcasted_iota(i32, (256, 128), 0)
    quarter = lax.broadcasted_iota(i32, (256, 128), 1) >> 5
    hit = element == jnp.concatenate([twice] * 32, axis=0)
    spots = jnp.concatenate([jnp.where(hit & (quarter == q), 1.0, 0.0).astype(bf16) for q in range(4)], axis=0)

    def prepare_ghost(level):
        for pair in (0, 2):
            taken = jnp.concatenate([
                jnp.dot(jnp.concatenate([tile16(level, bi, bj) for bj in range(4)], axis=1), spots,
                        preferred_element_type=f32).astype(bf16) for bi in (pair, pair + 1)], axis=1)
            turned = jnp.dot(swap, taken, preferred_element_type=f32)
            for jj in range(16):
                for x in (0, 1):
                    gout[level, pair + x, jj] = turned[16 * jj:16 * jj + 16, 128 * x:128 * x + 128]

    def prepare(level):
        for bi in range(4):
            for bj in range(4):
                turned = jnp.dot(swap, tile16(level, bi, bj), preferred_element_type=f32)
                for jj in range(16):
                    for tile in (0, 1):
                        inv[level, 16 * bj + jj, tile, 16 * bi:16 * bi + 16, :] = turned[
                            16 * jj:16 * jj + 16, 128 * tile:128 * tile + 128]

    for fetch in fetches[2:5]:
        fetch.wait()
    for i in range(3):
        start_out[i] = boundary(source[i + 1])
    start_out[3] = boundary(initial[...])
    start_out[4] = boundary(mass[...])

    loads[0].wait()
    for load in loads[1:]:
        load.start()
    prepare_ghost(0)
    pl.semaphore_wait(
        barrier,
        7 + 2 * (groups - 1) + (d > 0).astype(i32) + (d < tm_size - 1).astype(i32))

    def beside_copy(src, dst, send, recv):
        return pltpu.make_async_remote_copy(src, dst, send, recv, device_id=(d, other), device_id_type=MESH)

    began = beside_copy(start_out, start_in, st_send, st_recv)
    began.start()
    ghosts = [[beside_copy(gout.at[l, x], ginv.at[l, x], gi_send.at[l, x], gi_recv.at[l, x])
               for x in range(4)] for l in range(3)]
    for copy in ghosts[0]:
        copy.start()

    forth = jnp.where(d > 0, d - 1, 1)
    ahead = pltpu.make_async_remote_copy(source.at[0], next_source, src_send, src_recv,
                                         device_id=(forth, k), device_id_type=MESH)

    @pl.when(d > 0)
    def _():
        ahead.start()

    @pl.when(d == tm_size - 1)
    def _():
        next_source[...] = jnp.zeros_like(next_source)

    prepare(0)
    meets = among(facing, edge) - begin
    beside = jnp.zeros((8, 128), i32)
    for p in range(16):
        at = jnp.full((8, 128), p, i32)
        beside = jnp.where(place == lane_take(meets, at), lane_take(edge, at), beside)
    for f in range(2, 6):
        step = among(both(f), beside)
        onto = among(facing, jnp.minimum(step, 255)) - begin
        picks[f:f + 1, 256:384] = jnp.where((step < 256) & (layer < 3), 256 + 16 * layer + (onto & 15), 512)[0:1]
    toward = jnp.where(layer == 0, beside, jnp.where(layer < 3, 240 + lane, 512))
    away = jnp.where(layer < 2, 272 + lane, 512)
    picks[0:1, 256:384] = jnp.where(upper, toward, away)[0:1]
    picks[1:2, 256:384] = jnp.where(upper, away, toward)[0:1]

    began.wait_recv()
    gmass[...] = opened(start_in[4])

    def across(begin, tiles):
        return jnp.concatenate([state[tile, pl.ds(begin, 16, 4), :] for tile in range(tiles)], axis=1)

    once = jnp.minimum(d + 1, 1)

    def sides(x):
        return [jnp.concatenate([x[16 * q:16 * q + 4, :] for q in range(4)], axis=0),
                jnp.concatenate([x[16 * q + 12:16 * q + 16, :] for q in range(4)], axis=0),
                x[0:16, :], x[48:64, :]]

    def gather(block, f, tile, origins):
        index = jnp.broadcast_to(picks[f:f + 1, 128 * tile:128 * tile + 128], (8, 128))
        at, part = index & 127, index >> 7
        at = jnp.concatenate([at, at], axis=0)
        part = jnp.concatenate([part, part], axis=0)
        found = jnp.zeros((16, 128), f32)
        for origin in origins:
            found = jnp.where(part == origin, lane_take(block(origin), at), found)
        return found

    def columns(block):
        return lambda origin: block[:, 128 * origin:128 * origin + 128]

    def ghost_sum(level, total):
        for at in range(16):
            total = total + ginv[level, :, at] * grhs[pl.ds(at, 1), :][None]
        total = total.reshape(64, 128)
        total = total + pltpu.roll(total, 64, 1)
        return (total + pltpu.roll(total, 32, 1)).reshape(4, 16, 128)

    def own_sum(level, total):
        for at in range(64):
            total = total + inv[level, at] * rhs[:, pl.ds(at, 1), :]
        return total

    def alone(step, total):
        return lax.fori_loop(0, once, lambda _, x: step(x), total)

    def together(first_step, second_step, total):
        total, gsum = lax.fori_loop(
            0, once, lambda _, x: (first_step(x[0]), second_step(x[1])), (total, jnp.zeros((4, 16, 128), f32)))
        return total, gsum.reshape(64, 128)

    def ghost_rhs(ghost, coupled):
        known = gmass[...] * ghost - coupled
        which = lax.broadcasted_iota(i32, (16, 128), 1) >> 5
        dense = known[0:16]
        for q in (1, 2, 3):
            dense = jnp.where(which == q, pltpu.roll(known[16 * q:16 * q + 16], 32 * q, 1), dense)
        grhs[...] = dense

    def ghost_step(level):
        return alone(functools.partial(ghost_sum, level), jnp.zeros((4, 16, 128), f32)).reshape(64, 128)

    def keep(x, tiles):
        for tile in tiles:
            state[tile] = x[:, 128 * (tile - tiles[0]):128 * (tile - tiles[0]) + 128]

    def phi(level, value, ghost, more, awaited=()):
        tiles = 3 if more else 2
        keep(value, (0, 1))
        state[2] = ghost
        whole = jnp.concatenate([value, ghost], axis=1) if more else value
        faces = [across(0, 3), across(3, 3), *sides(whole)]
        picked = jnp.concatenate([jnp.concatenate([
            gather(columns(faces[f ^ 1]), f, tile, (0, 1, 2) if f < 2 else (0, 1) if tile < 2 else (2,))
            for tile in range(tiles)], axis=1) for f in range(6)], axis=0)
        coupled = times(tables[level], picked)
        known = mass[...] * value - coupled[:, :256]
        for tile in (0, 1):
            rhs[tile] = known[:, 128 * tile:128 * tile + 128]
        if more:
            ghost_rhs(ghost, coupled[:, 256:])
        own = functools.partial(own_sum, level)
        if more and not awaited:
            total, gsum = together(own, functools.partial(ghost_sum, level), jnp.zeros((2, 64, 128), f32))
            return jnp.concatenate([total[0], total[1]], axis=1), gsum
        total = alone(own, jnp.zeros((2, 64, 128), f32))
        result = jnp.concatenate([total[0], total[1]], axis=1)
        if not more:
            return result, ghost
        for copy in awaited:
            copy.wait_recv()
        return result, ghost_step(level)

    def phi_fresh(level, value, slot):
        fresh_out[slot] = boundary(value)
        copy = beside_copy(fresh_out.at[slot], fresh_in.at[slot], fr_send.at[slot], fr_recv.at[slot])
        copy.start()
        keep(value, (0, 1))
        faces = [across(0, 2), across(3, 2), *sides(value)]
        picked = jnp.concatenate([jnp.concatenate([
            gather(columns(faces[f ^ 1]), f, tile, (0, 1)) for tile in (0, 1)], axis=1)
            for f in range(6)], axis=0)
        known = mass[...] * value - times(tables[level], picked)
        for tile in (0, 1):
            rhs[tile] = known[:, 128 * tile:128 * tile + 128]
        total = alone(functools.partial(own_sum, level), jnp.zeros((2, 64, 128), f32))
        copy.wait()
        ghost = opened(fresh_in[slot])
        state[2] = ghost
        ends = [state[2, pl.ds(0, 16, 4), :], state[2, pl.ds(3, 16, 4), :]]
        near = [across(0, 2), across(3, 2)]
        beyond = sides(ghost)
        nothing = jnp.zeros((16, 256), f32)
        rows_of = []
        for f in range(6):
            if f < 2:
                def source_of(origin, f=f):
                    return ends[f ^ 1] if origin == 2 else columns(near[f ^ 1])(origin)
                rows_of.append(jnp.concatenate(
                    [gather(source_of, f, 0, (2,)), gather(source_of, f, 1, (2,)),
                     gather(source_of, f, 2, (0, 1, 2))], axis=1))
            else:
                rows_of.append(jnp.concatenate(
                    [nothing, gather(lambda _, f=f: beyond[(f ^ 1) - 2], f, 2, (2,))], axis=1))
        coupled = times(tables[level], jnp.concatenate(rows_of, axis=0))
        ghost_rhs(ghost, coupled[:, 256:])
        for tile in (0, 1):
            state[tile] = coupled[:, 128 * tile:128 * tile + 128]
            change[tile] = jnp.where(upper, state[tile, pl.ds(3, 16, 4), :], state[tile, pl.ds(0, 16, 4), :])
        offset = 3 - 3 * k

        def corrected(total):
            for q in range(16):
                total = total - inv[level, 4 * q + offset] * change[:, pl.ds(q, 1), :]
            return total

        total, gsum = together(corrected, functools.partial(ghost_sum, level), total)
        return jnp.concatenate([total[0], total[1]], axis=1), gsum, ghost

    value, ghost = source[1], opened(start_in[0])
    for i in (2, 3):
        value, ghost = phi(0, value, ghost, True, ghosts[0] if i == 2 else ())
        value, ghost = value + source[i], ghost + opened(start_in[i - 1])
    value, _ = phi(0, value, ghost, False)

    @pl.when(d < tm_size - 1)
    def _():
        ahead.wait_recv()

    @pl.when(d > 0)
    def _():
        ahead.wait_send()

    value = value + next_source[...]
    r_all[j] = value
    rg_out[...] = boundary(value)
    edges_out = [pltpu.make_async_remote_copy(rg_out, rg_all.at[j], rg_send.at[i], rg_recv.at[j],
                                              device_id=(peer, other), device_id_type=MESH)
                 for i, peer in enumerate([*peers, d])]
    shares = [pltpu.make_async_remote_copy(r_all.at[j], r_all.at[j], r_send.at[i], r_recv.at[j],
                                           device_id=(peer, k), device_id_type=MESH)
              for i, peer in enumerate(peers)]

    @pl.when(j < 3)
    def _():
        for copy in edges_out:
            copy.start()

    for share in shares:
        share.start()

    loads[1].wait()
    prepare_ghost(1)
    for copy in ghosts[1]:
        copy.start()
    prepare(1)
    loads[2].wait()
    prepare(2)
    @pl.when(m == 0)
    def _():
        first[...] = phi(2, initial[...], opened(start_in[3]), False)[0]

    @pl.when(m > 0)
    def _():
        first[...] = jnp.zeros_like(first)


    def share_arrived(i):
        if i < 3:
            pltpu.make_async_remote_copy(rg_out, rg_all.at[i], rg_send.at[0], rg_recv.at[i],
                                         device_id=(d, other), device_id_type=MESH).wait_recv()

        @pl.when(j != i)
        def _():
            pltpu.make_async_remote_copy(r_all.at[i], r_all.at[i], r_send.at[0], r_recv.at[i],
                                         device_id=(peers[0], k), device_id_type=MESH).wait_recv()

    share_arrived(0)
    value, ghost = r_all[0], opened(rg_all[0])
    for i in (1, 2):
        value, ghost = phi(1, value, ghost, True, ghosts[1] if i == 1 else ())
        share_arrived(i)
        value, ghost = value + r_all[i], ghost + opened(rg_all[i])
    value, _ = phi(1, value, ghost, False)
    share_arrived(3)
    value = value + r_all[3] + first[...]
    s_all[m] = value
    sg_out[...] = boundary(value)

    onward = []
    for t in range(groups - 1, 0, -1):
        target = jnp.where(m < t, 4 * t + j, lax.rem(d + 4, tm_size))
        own = pltpu.make_async_remote_copy(
            s_all.at[m], s_all.at[m], s_send.at[t], s_recv.at[m],
            device_id=(target, k), device_id_type=MESH)
        edge_out = pltpu.make_async_remote_copy(
            sg_out, sg_all.at[m], sg_send.at[t], sg_recv.at[m],
            device_id=(target, other), device_id_type=MESH)
        onward += [(m < t - 1, edge_out), (m < t, own)]

        @pl.when(m < t - 1)
        def _(edge_out=edge_out):
            edge_out.start()

        @pl.when(m < t)
        def _(own=own):
            own.start()

    @pl.when(j < 3)
    def _():
        for copy in edges_out:
            copy.wait_send()

    for share in shares:
        share.wait_send()

    def s_arrived(i):
        pltpu.make_async_remote_copy(s_all.at[i], s_all.at[i], s_send.at[0], s_recv.at[i],
                                     device_id=(lax.rem(d + 4, tm_size), k),
                                     device_id_type=MESH).wait_recv()

    prepare_ghost(2)
    for copy in ghosts[2]:
        copy.start()

    def s_edge_arrived(i):
        pltpu.make_async_remote_copy(sg_out, sg_all.at[i], sg_send.at[0], sg_recv.at[i],
                                     device_id=(lax.rem(d + 4, tm_size), other),
                                     device_id_type=MESH).wait_recv()

    for copy in ghosts[2]:
        copy.wait_recv()

    @pl.when(m == 0)
    def _():
        w_in[...] = initial[...]

    @pl.when(m > 0)
    def _():
        s_arrived(0)
        w_in[...] = s_all[0]

    @pl.when(m > 1)
    def _():
        s_edge_arrived(0)
        wg_in[...] = opened(sg_all[0])

    for i in range(1, groups - 1):
        @pl.when(i < m)
        def _(i=i):
            if i > 1 and i % 3 == 1:
                value, ghost, _ = phi_fresh(2, w_in[...], 1 + i)
            else:
                value, ghost = phi(2, w_in[...], wg_in[...], True)
            s_arrived(i)
            w_in[...] = value + s_all[i]

            @pl.when(i < m - 1)
            def _():
                s_edge_arrived(i)
                wg_in[...] = ghost + opened(sg_all[i])

    value = w_in[...]
    for i in (1, 2, 3):
        if i == 1:
            moved, gmoved, ghost = phi_fresh(1, value, 0)
        else:
            moved, gmoved = phi(1, value, ghost, i < 3)
        value = jnp.where(j >= i, moved + r_all[i - 1], value)
        if i < 3:
            ghost = jnp.where(j >= i, gmoved + opened(rg_all[i - 1]), ghost)
    out[0] = value
    for i in (1, 2, 3):
        if i == 1:
            value, ghost, _ = phi_fresh(0, value, 1)
        else:
            value, ghost = phi(0, value, ghost, i < 3)
        value = value + source[i]
        if i < 3:
            ghost = ghost + opened(start_in[i - 1])
        out[i] = value

    for sent, copy in onward:
        @pl.when(sent)
        def _(copy=copy):
            copy.wait_send()
    began.wait_send()
    for level in ghosts:
        for copy in level:
            copy.wait_send()


def pair_local(tm_size, source, initial, mass, inverses, couplings, neighbours, sends):
    f32, bf16, i32 = jnp.float32, jnp.bfloat16, jnp.int32
    vmem = pl.BlockSpec(memory_space=pltpu.VMEM)
    dma = pltpu.SemaphoreType.DMA
    groups = tm_size // 4
    return pl.pallas_call(
        functools.partial(pair_kernel, tm_size),
        out_shape=jax.ShapeDtypeStruct(source.shape, f32),
        in_specs=[pl.BlockSpec(memory_space=pltpu.MemorySpace.HBM)] * 7,
        out_specs=vmem,
        scratch_shapes=[
            pltpu.VMEM(source.shape, f32),
            pltpu.VMEM(initial.shape, f32),
            pltpu.VMEM(mass.shape, f32),
            pltpu.VMEM((3, 96, 16), f32),
            pltpu.VMEM(neighbours.shape, i32),
            pltpu.VMEM(sends.shape, i32),
            dma((6,)),
            pltpu.VMEM(inverses.shape, bf16),
            pltpu.VMEM((3, 64, 2, 64, 128), f32),
            pltpu.VMEM((3, 4, 16, 16, 128), f32),
            pltpu.VMEM((3, 4, 16, 16, 128), f32),
            pltpu.VMEM((3, 128, 192), bf16),
            pltpu.VMEM((3, 64, 128), f32),
            pltpu.VMEM((2, 64, 128), f32),
            pltpu.VMEM((2, 16, 128), f32),
            pltpu.VMEM((16, 128), f32),
            pltpu.VMEM((6, 384), i32),
            pltpu.VMEM((8, 128), i32),
            pltpu.VMEM((8, 128), i32),
            pltpu.VMEM((5, 32, 128), f32),
            pltpu.VMEM((5, 32, 128), f32),
            pltpu.VMEM((64, 128), f32),
            pltpu.VMEM((64, 256), f32),
            pltpu.VMEM((4, 64, 256), f32),
            pltpu.VMEM((32, 128), f32),
            pltpu.VMEM((4, 32, 128), f32),
            pltpu.VMEM((64, 256), f32),
            pltpu.VMEM((64, 256), f32),
            pltpu.VMEM((64, 128), f32),
            pltpu.VMEM((groups, 64, 256), f32),
            pltpu.VMEM((32, 128), f32),
            pltpu.VMEM((groups, 32, 128), f32),
            pltpu.VMEM((max(2, groups), 32, 128), f32),
            pltpu.VMEM((max(2, groups), 32, 128), f32),
            dma((3,)), dma((3, 4)), dma((3, 4)), dma, dma, dma, dma,
            dma((3,)), dma((4,)), dma((4,)), dma((4,)),
            dma((groups,)), dma((groups,)), dma((groups,)), dma((groups,)),
            dma((max(2, groups),)), dma((max(2, groups),)),
        ],
        compiler_params=pltpu.CompilerParams(collective_id=0, has_side_effects=True,
                                             vmem_limit_bytes=48 << 20),
        name="cycle",
    )(*[pltpu.with_memory_space_constraint(x, pltpu.MemorySpace.HBM) for x in (source, initial, mass, inverses, couplings.reshape(3, 96, 16), neighbours, sends)])


def local(tm_size, space_size, source, initial, mass, inverses, couplings, neighbours, sends):
    f32 = jnp.float32
    vmem = pl.BlockSpec(memory_space=pltpu.VMEM)
    dma = pltpu.SemaphoreType.DMA
    return pl.pallas_call(
        functools.partial(kernel, tm_size, space_size),
        out_shape=jax.ShapeDtypeStruct(source.shape, f32),
        in_specs=[vmem, vmem, vmem, pl.BlockSpec(memory_space=pl.ANY), vmem, vmem, vmem],
        out_specs=vmem,
        scratch_shapes=[
            pltpu.VMEM(inverses.shape, jnp.bfloat16),
            pltpu.VMEM((2, 576, 128), f32),
            pltpu.VMEM((3, 64, 2, 64, 128), f32),
            pltpu.VMEM((3, 128, 192), jnp.bfloat16),
            pltpu.VMEM((3, 64, 64), jnp.bfloat16),
            pltpu.VMEM((2, 64, 128), f32),
            pltpu.VMEM((4, 2, 16, 256), f32),
            pltpu.VMEM((4, 2, 16, 256), f32),
            pltpu.VMEM((2, 64, 128), f32),
            pltpu.VMEM((2, 16, 128), f32),
            pltpu.VMEM((2, 16, 128), f32),
            pltpu.VMEM((3, 8, 128), jnp.int32),
            pltpu.VMEM((6, 256), jnp.int32),
            pltpu.VMEM((2, 8, 256), jnp.int32),
            pltpu.VMEM((64, 256), f32),
            pltpu.VMEM((4, 64, 256), f32),
            pltpu.VMEM((64, 256), f32),
            pltpu.VMEM((tm_size // 4, 64, 256), f32),
            dma((3,)), dma((4, 2)), dma((4, 2)), dma((2,)), dma((2,)), dma, dma,
            dma((3,)), dma((4,)), dma((tm_size // 4,)), dma((tm_size // 4,)),
        ],
        compiler_params=pltpu.CompilerParams(collective_id=0, has_side_effects=True),
        name="cycle",
    )(source, initial, mass, inverses, couplings.reshape(3, 96, 16), neighbours, sends)


def solution(mesh):
    placed = (
        P("tm", None, "space"),
        P(None, "space"),
        P(None, "space"),
        P(None, None, None, "space"),
        P(),
        P(None, "space"),
        P(None, "space"),
    )
    body = (functools.partial(pair_local, mesh.shape["tm"]) if mesh.shape["space"] == 2
            else functools.partial(local, mesh.shape["tm"], mesh.shape["space"]))
    return jax.shard_map(
        body,
        mesh=mesh, in_specs=placed, out_specs=P("tm", None, "space"), check_vma=False)
```
